512 devices in a mesh: dp: 16 (over x, y), tm: 32 (over z, core).
Axes of the slice: x: 4, y: 4, z: 16, core: 2. Of those that a mesh axis runs over, the one named last changes fastest.
Arguments:
- records: bfloat16 [16, 4096, 1024], P('dp', 'tm'), may hold values from -6 to 6
- x_weight: bfloat16 [1024, 512], replicated, may hold values from -0.1875 to 0.1875
- bc_weight: bfloat16 [1024, 256], replicated, may hold values from -0.1875 to 0.1875
- decay_codes: int32 [16, 4096, 8], P('dp', 'tm'), may hold values from 0 to 524
- out_grad: bfloat16 [16, 4096, 512], P('dp', 'tm'), may hold values from -6 to 6
Outputs:
- y_out: bfloat16 [16, 4096, 512], P('dp', 'tm')
- x_grad: float32 [1024, 512], P('tm')
- bc_grad: float32 [1024, 256], P('tm')
The draws below stay inside these ranges and needn't reach their ends.
All inputs are finite; a program needn't handle non-finite values.
Results may differ from the reference program's by a relative error of at most 0.0085.
Values sent between devices are 32-bit elements; how exact they have to be, the bound alone decides.
No kernel may reach another device: no remote copies, remote signals or barrier semaphores. Data moves between devices by JAX's collectives and lax.ppermute only.
A program may use at most 64 MiB of HBM per device.

```python
import jax
import jax.numpy as jnp
from jax import lax

D = 1024
HEADS = 8
HEAD = 64
STATE = 128
SPAN = 128
LD = 128
FRAMES = 4096
RECS = 16


def draw_decay_codes(key, part):
    level_key = jax.random.fold_in(key, 11)
    rough_key = jax.random.fold_in(key, 23)
    blocks = FRAMES // LD
    powers = jax.random.randint(level_key, (RECS, blocks, 1, HEADS), 0, 11)
    levels = jnp.minimum(jnp.left_shift(jnp.ones_like(powers), powers) - 1, 524)
    rough = jax.random.randint(rough_key, (RECS, blocks, LD, HEADS), 0, 13)
    codes = jnp.minimum(levels + rough, 524)
    return codes.reshape(RECS, FRAMES, HEADS).astype(jnp.int32)


def block_scale(stream_key, shape, cuts, smallest, largest):
    def one(dim, parts):
        draws = jax.random.uniform(jax.random.fold_in(jax.random.fold_in(stream_key, 6), dim), (parts,), jnp.float32, smallest / len(cuts), largest / len(cuts))
        return jnp.repeat(jnp.exp(draws), shape[dim] // parts).reshape((-1,) + (1,) * (len(shape) - dim - 1))

    level = one(*cuts[0])
    for cut in cuts[1:]:
        level = level * one(*cut)
    return level


def centred(own_key, shape, deviation, most, shards=(), held_as=jnp.bfloat16):
    drawn = deviation * jax.random.normal(own_key, shape, jnp.float32)
    if shards:
        drawn = drawn * block_scale(own_key, shape, shards, -0.22, 0.18)
    return jnp.clip(drawn, -most, most).astype(held_as)


def setup_inputs(seed: int = 0) -> dict:
    keys = jax.random.split(jax.random.key(seed), 6)
    return {
        "records": centred(keys[0], (RECS, FRAMES, D), 1.0, 6.0, ((0, 16), (1, 32))),
        "x_weight": centred(keys[1], (D, HEADS * HEAD), D ** -0.5, 0.1875),
        "bc_weight": centred(keys[2], (D, 2 * STATE), D ** -0.5, 0.1875),
        "decay_codes": draw_decay_codes(jax.random.fold_in(keys[5], 71), 0),
        "out_grad": centred(keys[4], (RECS, FRAMES, HEADS * HEAD), 1.0, 6.0, ((0, 16), (1, 32))),
    }


highest = lax.Precision.HIGHEST


def span_kernel(log_decay):
    running = jnp.cumsum(log_decay, axis=1)
    length = log_decay.shape[1]
    causal = lax.broadcasted_iota(jnp.int32, (length, length), 0) >= lax.broadcasted_iota(jnp.int32, (length, length), 1)
    causal = causal[None, None, :, :]
    heads_first = jnp.transpose(running, (0, 2, 1))
    gaps = heads_first[:, :, :, None] - heads_first[:, :, None, :]
    kernel = jnp.where(causal, jnp.exp(jnp.where(causal, gaps, 0.0)), 0.0)
    return running, kernel


def block_scores(readout, inject):
    return jnp.einsum("rtn,rsn->rts", readout.astype(jnp.bfloat16), inject.astype(jnp.bfloat16), preferred_element_type=jnp.float32)


def forward_span(carry_state, pieces):
    mixer_f, inject, readout, cot_heads, log_decay = pieces
    running, kernel = span_kernel(log_decay)
    scores = block_scores(readout, inject)
    mixing = kernel * scores[:, None, :, :]
    decayed = jnp.exp(running)
    within = jnp.einsum("rhts,rshp->rthp", mixing, mixer_f, precision=highest)
    carried = decayed[..., None] * jnp.einsum("rhpn,rtn->rthp", carry_state, readout, precision=highest)
    pair_dots = jnp.einsum("rthp,rshp->rhts", cot_heads, mixer_f, precision=highest)
    grad_read = jnp.einsum("rhts,rsn->rtn", kernel * pair_dots, inject, precision=highest)
    grad_read = grad_read + jnp.einsum("rthp,rhpn->rtn", decayed[..., None] * cot_heads, carry_state, precision=highest)
    to_end = jnp.exp(running[:, -1:, :] - running)
    new_state = jnp.exp(running[:, -1, :])[:, :, None, None] * carry_state
    new_state = new_state + jnp.einsum("rshp,rsn->rhpn", to_end[..., None] * mixer_f, inject, precision=highest)
    return new_state, (within + carried, grad_read)


def reverse_span(adjoint, pieces):
    mixer_f, inject, readout, cot_heads, log_decay = pieces
    running, kernel = span_kernel(log_decay)
    scores = block_scores(readout, inject)
    mixing = kernel * scores[:, None, :, :]
    pair_dots = jnp.einsum("rthp,rshp->rhts", cot_heads, mixer_f, precision=highest)
    to_end = jnp.exp(running[:, -1:, :] - running)
    grad_mixer = jnp.einsum("rhts,rthp->rshp", mixing, cot_heads, precision=highest)
    grad_mixer = grad_mixer + to_end[..., None] * jnp.einsum("rhpn,rsn->rshp", adjoint, inject, precision=highest)
    grad_inject = jnp.einsum("rhts,rtn->rsn", kernel * pair_dots, readout, precision=highest)
    grad_inject = grad_inject + jnp.einsum("rshp,rhpn->rsn", to_end[..., None] * mixer_f, adjoint, precision=highest)
    new_adjoint = jnp.exp(running[:, -1, :])[:, :, None, None] * adjoint
    new_adjoint = new_adjoint + jnp.einsum("rthp,rtn->rhpn", jnp.exp(running)[..., None] * cot_heads, readout, precision=highest)
    return new_adjoint, (grad_mixer, grad_inject)


def to_blocks(array, frames):
    return array.reshape((frames // SPAN, 1, SPAN) + array.shape[1:])


def reference(records, x_weight, bc_weight, decay_codes, out_grad):
    out_scale = (STATE * FRAMES) ** -0.5
    grad_scale = (RECS * FRAMES) ** -0.5
    decay_unit = 1.0 / (32.0 * FRAMES)

    def record_pass(pieces):
        signal, codes, cot_in = pieces
        mixer_in = jnp.dot(signal, x_weight, preferred_element_type=jnp.float32).astype(jnp.bfloat16)
        state_proj = jnp.dot(signal, bc_weight, preferred_element_type=jnp.float32).astype(jnp.bfloat16)
        log_decay = -decay_unit * codes.astype(jnp.float32)
        cotangent = cot_in.astype(jnp.float32) * out_scale
        mixer_f = mixer_in.astype(jnp.float32).reshape(FRAMES, HEADS, HEAD)
        inject = state_proj[:, :STATE].astype(jnp.float32)
        readout = state_proj[:, STATE:].astype(jnp.float32)
        cot_heads = cotangent.reshape(FRAMES, HEADS, HEAD)
        blocks = (to_blocks(mixer_f, FRAMES), to_blocks(inject, FRAMES), to_blocks(readout, FRAMES),
                  to_blocks(cot_heads, FRAMES), to_blocks(log_decay, FRAMES))
        zero_state = jnp.zeros((1, HEADS, HEAD, STATE), jnp.float32)
        ignored, (local_out, local_read) = lax.scan(forward_span, zero_state, blocks)
        ignored_too, (local_grad, local_inject) = lax.scan(reverse_span, zero_state, blocks, reverse=True)
        output = local_out.reshape(FRAMES, HEADS * HEAD).astype(jnp.bfloat16)
        grad_mix = local_grad.reshape(FRAMES, HEADS * HEAD).astype(jnp.bfloat16)
        grad_proj = jnp.concatenate([local_inject.reshape(FRAMES, STATE), local_read.reshape(FRAMES, STATE)], axis=1).astype(jnp.bfloat16)
        grad_cat = jnp.concatenate([grad_mix, grad_proj], axis=1)
        term = jnp.dot(signal.T, grad_cat, preferred_element_type=jnp.float32)
        return output, term

    outputs, terms = lax.map(record_pass, (records, decay_codes, out_grad))
    summed = jnp.sum(terms, axis=0) * grad_scale
    return outputs, summed[:, :HEADS * HEAD], summed[:, HEADS * HEAD:]
```

```python
import jax
import jax.numpy as jnp
from jax import lax
from jax.experimental import pallas as pl
from jax.experimental.pallas import tpu as pltpu
from jax.sharding import Mesh, PartitionSpec as P

f32 = jnp.float32
bf16 = jnp.bfloat16

LD = 128
CHIP = 2 * LD
HEADS = 8
HEAD = 64
STATE = 128
HALF = HEADS * HEAD // 2
ZN = 16
DP = 16
ROWS = HALF // ZN
PAY = 2 * ROWS + 8


def mm(a, b):
    return jnp.dot(a, b, preferred_element_type=f32)


def mm_tn(a, b):
    return lax.dot_general(a, b, (((0,), (0,)), ((), ())), preferred_element_type=f32)


def mm_nt(a, b):
    return lax.dot_general(a, b, (((1,), (1,)), ((), ())), preferred_element_type=f32)


def causal(shape):
    return lax.broadcasted_iota(jnp.int32, shape, 0) >= lax.broadcasted_iota(jnp.int32, shape, 1)


def local_kernel(unit, c_ref, x_ref, g_ref, codes_ref, pack_ref, wx_ref, wbc_ref,
                 pay_ref, u_ref, ue_ref, v_ref, en_ref, ep_ref, te_ref, proj_ref, xc_ref,
                 gs_ref, cs_ref):
    c = c_ref[0]
    own = pl.multiple_of(c * LD, LD)
    oth = pl.multiple_of((1 - c) * LD, LD)
    d = x_ref.shape[1]
    xc_ref[pl.ds(own, LD), :] = x_ref[...]
    xc_ref[pl.ds(oth, LD), :] = pack_ref[:, :d].astype(bf16)
    gs_ref[pl.ds(own, LD), :] = g_ref[...].astype(f32)
    gs_ref[pl.ds(oth, LD), :] = pack_ref[:, d:d + HALF]
    cs_ref[pl.ds(own, LD), :] = codes_ref[...].astype(f32)
    cs_ref[pl.ds(oth, LD), :] = pack_ref[:, d + HALF:d + HALF + HEADS]
    codes = cs_ref[...]
    hi = jnp.floor(codes * (1.0 / 32.0))
    lo = codes - 32.0 * hi
    row = lax.broadcasted_iota(jnp.int32, (HEADS, HALF), 0)
    col = lax.broadcasted_iota(jnp.int32, (HEADS, HALF), 1)
    spread = jnp.where(row == col // HEAD + c * (HEADS // 2), 1.0, 0.0).astype(bf16)
    hi = mm(hi.astype(bf16), spread).astype(bf16)
    lo = mm(lo.astype(bf16), spread).astype(bf16)
    tri = jnp.where(causal((CHIP, CHIP)), 1.0, 0.0).astype(bf16)
    running = unit * (32.0 * mm(tri, hi) + mm(tri, lo))
    last = running[CHIP - 1:CHIP, :]
    en = jnp.exp(-running)
    ep = jnp.exp(running)
    te = jnp.exp(running - last)
    en_ref[...] = en
    ep_ref[...] = ep
    te_ref[...] = te
    xv = xc_ref[...]
    mixer = mm(xv, wx_ref[...]).astype(bf16).astype(f32)
    proj = mm(xv, wbc_ref[...]).astype(bf16)
    proj_ref[...] = proj
    v = (en * gs_ref[...]).astype(bf16)
    ue = (te * mixer).astype(bf16)
    u_ref[...] = (ep * mixer).astype(bf16)
    ue_ref[...] = ue
    v_ref[...] = v
    state = mm_tn(ue, proj[:, :STATE])
    adjoint = mm_tn(v, proj[:, STATE:])
    pay_ref[:, 0:ROWS, :] = state.reshape(ZN, ROWS, STATE)
    pay_ref[:, ROWS:2 * ROWS, :] = adjoint.reshape(ZN, ROWS, STATE)
    per = ZN // (HEADS // 2)
    for h in range(HEADS // 2):
        total = jnp.broadcast_to(last[:, h * HEAD:h * HEAD + 1], (8, STATE))
        for k in range(per):
            pay_ref[h * per + k, 2 * ROWS:, :] = total


def inner_kernel(u_ref, v_ref, proj_ref, yl_ref, gm_ref, gp_ref):
    mask = causal((CHIP, CHIP))
    inject = proj_ref[:, :STATE]
    readout = proj_ref[:, STATE:]
    u = u_ref[...]
    v = v_ref[...]
    scores = jnp.where(mask, mm_nt(readout, inject), 0.0).astype(bf16)
    pairs = jnp.where(mask, mm_nt(v, u), 0.0).astype(bf16)
    yl_ref[...] = mm(scores, u)
    gm_ref[...] = mm_tn(scores, v)
    gp_ref[:, :STATE] = mm_tn(pairs, readout)
    gp_ref[:, STATE:] = mm(pairs, inject)


def scan_kernel(in_ref, out_ref):
    decay = [jnp.exp(-in_ref[k, 2 * ROWS:2 * ROWS + 1, :]) for k in range(ZN)]
    carry = jnp.zeros((ROWS, STATE), f32)
    for k in range(ZN):
        out_ref[k, 0:ROWS, :] = carry
        if k + 1 < ZN:
            carry = decay[k] * carry + in_ref[k, 0:ROWS, :]
    carry = jnp.zeros((ROWS, STATE), f32)
    for k in reversed(range(ZN)):
        out_ref[k, ROWS:, :] = carry
        if k:
            carry = decay[k] * carry + in_ref[k, ROWS:2 * ROWS, :]


def outer_kernel(scale, c_ref, in_ref, u_ref, v_ref, en_ref, ep_ref, te_ref, proj_ref,
                 yl_ref, gml_ref, gp_ref, gm_ref, pk_ref, ps_ref, yk_ref, ys_ref, y_ref):
    c = c_ref[0]
    carry = in_ref[:, 0:ROWS, :].reshape(HALF, STATE).astype(bf16)
    adjoint = in_ref[:, ROWS:, :].reshape(HALF, STATE).astype(bf16)
    inject = proj_ref[:, :STATE]
    readout = proj_ref[:, STATE:]
    gi = scale * (gp_ref[:, :STATE] + mm(u_ref[...], adjoint))
    gr = scale * (gp_ref[:, STATE:] + mm(v_ref[...], carry))
    pk_ref[...] = jnp.where(c == 0, gi, gr)
    ps_ref[...] = jnp.where(c == 0, gr, gi)
    grad = ep_ref[...] * gml_ref[...] + te_ref[...] * mm_nt(inject, adjoint)
    gm_ref[...] = (scale * grad).astype(bf16)
    y_ref[...] = en_ref[...] * (yl_ref[...] + mm_nt(readout, carry))
    yk_ref[...] = y_ref[pl.ds(pl.multiple_of(c * LD, LD), LD), :]
    ys_ref[...] = y_ref[pl.ds(pl.multiple_of((1 - c) * LD, LD), LD), :]


def weight_kernel(xt_ref, gm_ref, pk_ref, pr_ref, out_ref):
    xt = xt_ref[...]
    out_ref[:, :HALF] = mm(xt, gm_ref[...])
    out_ref[:, HALF:] = mm(xt, (pk_ref[...] + pr_ref[...]).astype(bf16))


def join_kernel(c_ref, yk_ref, yr_ref, out_ref):
    c = c_ref[0]
    yk = yk_ref[...].astype(bf16)
    yr = yr_ref[...].astype(bf16)

    @pl.when(c == 0)
    def _():
        out_ref[:, :HALF] = yk
        out_ref[:, HALF:] = yr

    @pl.when(c != 0)
    def _():
        out_ref[:, :HALF] = yr
        out_ref[:, HALF:] = yk


def whole(shape):
    return pl.BlockSpec(shape, lambda i, c: (0,) * len(shape))


def call(kernel, outs, ins, scratch=(), c=None, specs=None):
    params = pltpu.CompilerParams(vmem_limit_bytes=48 * 1024 * 1024)
    shapes = [jax.ShapeDtypeStruct(s, d) for s, d in outs]
    if c is None:
        return pl.pallas_call(kernel, out_shape=shapes, compiler_params=params)(*ins)
    specs = specs or [whole(a.shape) for a in ins]
    return pl.pallas_call(
        kernel,
        out_shape=shapes,
        grid_spec=pltpu.PrefetchScalarGridSpec(
            num_scalar_prefetch=1, grid=(1,), in_specs=specs,
            out_specs=[whole(s) for s, _ in outs], scratch_shapes=list(scratch)),
        compiler_params=params,
    )(c, *ins)


def body(records, x_weight, bc_weight, decay_codes, out_grad):
    x = records[0]
    g = out_grad[0]
    codes = decay_codes[0]
    d = x.shape[1]
    frames = LD * 2 * ZN
    unit = 1.0 / (32.0 * frames)
    out_scale = float((STATE * frames) ** -0.5)
    grad_scale = float((DP * frames) ** -0.5)
    core = lax.axis_index("c")
    c = core.astype(jnp.int32).reshape(1)
    swap = [(0, 1), (1, 0)]

    g_send = jnp.where(core == 0, g[:, HALF:], g[:, :HALF]).astype(f32)
    pad = jnp.zeros((LD, 128 - HEADS), f32)
    pack = jnp.concatenate([x.astype(f32), g_send, codes.astype(f32), pad], axis=1)
    pack = lax.ppermute(pack, "c", swap)

    ins = (x, g, codes, pack, x_weight, bc_weight)
    specs = [whole(x.shape), pl.BlockSpec((LD, HALF), lambda i, c: (0, c[0])), whole(codes.shape),
             whole(pack.shape), pl.BlockSpec((d, HALF), lambda i, c: (0, c[0])), whole(bc_weight.shape)]
    sq = (CHIP, HALF)
    pay, u, ue, v, en, ep, te, proj, xc = call(
        lambda *refs: local_kernel(unit, *refs),
        [((ZN, PAY, STATE), f32), (sq, bf16), (sq, bf16), (sq, bf16), (sq, f32), (sq, f32), (sq, f32),
         ((CHIP, 2 * STATE), bf16), ((CHIP, d), bf16)],
        ins, [pltpu.VMEM(sq, f32), pltpu.VMEM((CHIP, HEADS), f32)], c, specs)

    pay = lax.all_to_all(pay, "z", 0, 0, tiled=True)
    yl, gml, gpl = call(inner_kernel, [(sq, f32), (sq, f32), ((CHIP, 2 * STATE), f32)], (u, v, proj))
    xt = xc.T.reshape(ZN, 2, DP, 2, CHIP).transpose(2, 0, 1, 3, 4).reshape(d, CHIP)
    (pay,) = call(scan_kernel, [((ZN, 2 * ROWS, STATE), f32)], (pay,))
    pay = lax.all_to_all(pay, "z", 0, 0, tiled=True)

    gm, pk, ps, yk, ys = call(
        lambda *refs: outer_kernel(out_scale, *refs),
        [(sq, bf16), ((CHIP, STATE), f32), ((CHIP, STATE), f32), ((LD, HALF), f32), ((LD, HALF), f32)],
        (pay, ue, v, en, ep, te, proj, yl, gml, gpl), [pltpu.VMEM(sq, f32)], c)
    pr = lax.ppermute(ps, "c", swap)
    yr = lax.ppermute(ys, "c", swap)
    width = HALF + STATE
    (grad,) = call(weight_kernel, [((d, width), f32)], (xt, gm, pk, pr))
    (y,) = call(join_kernel, [((LD, 2 * HALF), bf16)], (yk, yr), (), c)

    part = lax.all_to_all(grad.reshape(DP, d // DP, width), "dp", 0, 0, tiled=True)
    part = jnp.sum(part, axis=0).reshape(ZN, d // DP // ZN, width)
    part = lax.all_to_all(part, "z", 0, 0, tiled=True)
    part = (jnp.sum(part, axis=0) * grad_scale).reshape(1, 2, 2, width)
    part = jnp.broadcast_to(part, (DP, 2, 2, width)).reshape(2 * DP, 2, width)
    part = lax.all_to_all(part, ("dp", "c"), 0, 0, tiled=True)
    part = part.reshape(DP, 2, 2, width).transpose(0, 2, 1, 3).reshape(2 * DP, 2, width)
    x_grad = part[:, :, :HALF].reshape(2 * DP, 2 * HALF)
    bc_grad = part[:, :, HALF:].reshape(2 * DP, 2 * STATE)
    return y[None], x_grad, bc_grad


def solution(mesh):
    mesh = Mesh(mesh.devices.reshape(DP, ZN, 2), ("dp", "z", "c"))
    frames = P("dp", ("z", "c"), None)
    rows = P(("z", "c"), None)
    return jax.shard_map(
        body,
        mesh=mesh,
        in_specs=(frames, P(), P(), frames, frames),
        out_specs=(frames, rows, rows),
        check_vma=False,
    )
```

```python
import jax
import jax.numpy as jnp
from jax import lax
from jax.experimental import pallas as pl
from jax.experimental.pallas import tpu as pltpu
from jax.sharding import Mesh, PartitionSpec as P

f32 = jnp.float32
bf16 = jnp.bfloat16

LD = 128
CHIP = 2 * LD
HEADS = 8
HEAD = 64
STATE = 128
HALF = HEADS * HEAD // 2
ZN = 16
DP = 16
ROWS = HALF // ZN
PAY = 2 * ROWS + 8


def mm(a, b):
    return jnp.dot(a, b, preferred_element_type=f32)


def mm_tn(a, b):
    return lax.dot_general(a, b, (((0,), (0,)), ((), ())), preferred_element_type=f32)


def mm_nt(a, b):
    return lax.dot_general(a, b, (((1,), (1,)), ((), ())), preferred_element_type=f32)


def causal(shape):
    return lax.broadcasted_iota(jnp.int32, shape, 0) >= lax.broadcasted_iota(jnp.int32, shape, 1)


def pack_kernel(x_ref, g_ref, codes_ref, out_ref):
    d = x_ref.shape[1]
    out_ref[:, :d] = x_ref[...].astype(f32)
    out_ref[:, d:d + HALF] = g_ref[...].astype(f32)
    out_ref[:, d + HALF:] = jnp.zeros((LD, LD), f32)
    out_ref[0:HEADS, d + HALF:] = codes_ref[...].astype(f32)


def own_kernel(x_ref, g_ref, codes_ref, wx_ref, wbc_ref,
               mix_ref, proj_ref, g_out_ref, codes_out_ref, x_out_ref, wx_out_ref, wbc_out_ref):
    x = x_ref[...]
    wx = wx_ref[...]
    wbc = wbc_ref[...]
    mix_ref[...] = mm(x, wx).astype(bf16)
    proj_ref[...] = mm(x, wbc).astype(bf16)
    g_out_ref[...] = g_ref[...]
    codes_out_ref[...] = codes_ref[...].astype(f32)
    x_out_ref[...] = x
    wx_out_ref[...] = wx
    wbc_out_ref[...] = wbc


def local_kernel(unit, c_ref, mix_ref, pj_ref, g_ref, codes_ref, x_ref, wx_ref, wbc_ref, pack_ref,
                 pay_ref, ue_ref, v_ref, en_ref, te_ref, proj_ref, xc_ref, yl_ref, gm_ref, gp_ref,
                 gs_ref, cs_ref, ms_ref):
    c = c_ref[0]
    own = pl.multiple_of(c * LD, LD)
    oth = pl.multiple_of((1 - c) * LD, LD)
    d = x_ref.shape[1]
    xo = pack_ref[:, :d].astype(bf16)
    xc_ref[pl.ds(own, LD), :] = x_ref[...]
    xc_ref[pl.ds(oth, LD), :] = xo
    gs_ref[pl.ds(own, LD), :] = g_ref[...].astype(f32)
    gs_ref[pl.ds(oth, LD), :] = pack_ref[:, d:d + HALF]
    cs_ref[:, pl.ds(own, LD)] = codes_ref[...]
    cs_ref[:, pl.ds(oth, LD)] = pack_ref[0:HEADS, d + HALF:]
    ms_ref[pl.ds(own, LD), :] = mix_ref[...]
    ms_ref[pl.ds(oth, LD), :] = mm(xo, wx_ref[...]).astype(bf16)
    proj_ref[pl.ds(own, LD), :] = pj_ref[...]
    proj_ref[pl.ds(oth, LD), :] = mm(xo, wbc_ref[...]).astype(bf16)
    codes = cs_ref[...]
    hi = jnp.floor(codes * (1.0 / 32.0))
    lo = codes - 32.0 * hi
    row = lax.broadcasted_iota(jnp.int32, (HEADS, HALF), 0)
    col = lax.broadcasted_iota(jnp.int32, (HEADS, HALF), 1)
    spread = jnp.where(row == col // HEAD + c * (HEADS // 2), 1.0, 0.0).astype(bf16)
    hi = mm_tn(hi.astype(bf16), spread).astype(bf16)
    lo = mm_tn(lo.astype(bf16), spread).astype(bf16)
    mask = causal((CHIP, CHIP))
    tri = jnp.where(mask, 1.0, 0.0).astype(bf16)
    running = unit * (32.0 * mm(tri, hi) + mm(tri, lo))
    last = running[CHIP - 1:CHIP, :]
    en = jnp.exp(-running)
    ep = jnp.exp(running)
    te = jnp.exp(running - last)
    en_ref[...] = en
    te_ref[...] = te
    mixer = ms_ref[...].astype(f32)
    inject = proj_ref[:, :STATE]
    readout = proj_ref[:, STATE:]
    v = (en * gs_ref[...]).astype(bf16)
    ue = (te * mixer).astype(bf16)
    u = (ep * mixer).astype(bf16)
    ue_ref[...] = ue
    v_ref[...] = v
    state = mm_tn(ue, inject)
    adjoint = mm_tn(v, readout)
    pay_ref[:, 0:ROWS, :] = state.reshape(ZN, ROWS, STATE)
    pay_ref[:, ROWS:2 * ROWS, :] = adjoint.reshape(ZN, ROWS, STATE)
    per = ZN // (HEADS // 2)
    for h in range(HEADS // 2):
        total = jnp.broadcast_to(last[:, h * HEAD:h * HEAD + 1], (8, STATE))
        for k in range(per):
            pay_ref[h * per + k, 2 * ROWS:, :] = total
    scores = jnp.where(mask, mm_nt(readout, inject), 0.0).astype(bf16)
    pairs = jnp.where(mask, mm_nt(v, u), 0.0).astype(bf16)
    yl_ref[...] = en * mm(scores, u)
    gm_ref[...] = ep * mm_tn(scores, v)
    gp_ref[:, :STATE] = mm_tn(pairs, readout)
    gp_ref[:, STATE:] = mm(pairs, inject)


def scan_kernel(in_ref, out_ref):
    decay = [jnp.exp(-in_ref[k, 2 * ROWS:2 * ROWS + 1, :]) for k in range(ZN)]
    carry = jnp.zeros((ROWS, STATE), f32)
    for k in range(ZN):
        out_ref[k, 0:ROWS, :] = carry
        if k + 1 < ZN:
            carry = decay[k] * carry + in_ref[k, 0:ROWS, :]
    carry = jnp.zeros((ROWS, STATE), f32)
    for k in reversed(range(ZN)):
        out_ref[k, ROWS:, :] = carry
        if k:
            carry = decay[k] * carry + in_ref[k, ROWS:2 * ROWS, :]


def outer_kernel(scale, c_ref, in_ref, u_ref, v_ref, en_ref, te_ref, proj_ref,
                 yl_ref, gml_ref, gp_ref, gm_ref, pk_ref, ps_ref, yk_ref, ys_ref, y_ref):
    c = c_ref[0]
    carry = in_ref[:, 0:ROWS, :].reshape(HALF, STATE).astype(bf16)
    adjoint = in_ref[:, ROWS:, :].reshape(HALF, STATE).astype(bf16)
    inject = proj_ref[:, :STATE]
    readout = proj_ref[:, STATE:]
    gi = scale * (gp_ref[:, :STATE] + mm(u_ref[...], adjoint))
    gr = scale * (gp_ref[:, STATE:] + mm(v_ref[...], carry))
    pk_ref[...] = jnp.where(c == 0, gi, gr)
    ps_ref[...] = jnp.where(c == 0, gr, gi)
    grad = gml_ref[...] + te_ref[...] * mm_nt(inject, adjoint)
    gm_ref[...] = (scale * grad).astype(bf16)
    y_ref[...] = yl_ref[...] + en_ref[...] * mm_nt(readout, carry)
    yk_ref[...] = y_ref[pl.ds(pl.multiple_of(c * LD, LD), LD), :]
    ys_ref[...] = y_ref[pl.ds(pl.multiple_of((1 - c) * LD, LD), LD), :]


def fold_kernel(in_ref, out_ref):
    total = jnp.sum(in_ref[...], axis=0)
    step = out_ref.shape[1]
    for k in range(ZN):
        out_ref[k] = total[k * step:(k + 1) * step, :]


def spread_kernel(scale, in_ref, out_ref):
    total = scale * jnp.sum(in_ref[...], axis=0)
    for k in range(2 * DP):
        half = k % 2
        out_ref[k] = total[2 * half:2 * half + 2, :]


def place_kernel(in_ref, x_ref, bc_ref):
    for k in range(DP):
        for half in range(2):
            piece = in_ref[2 * k + half]
            x_ref[2 * k:2 * k + 2, half * HALF:(half + 1) * HALF] = piece[:, :HALF]
            bc_ref[2 * k:2 * k + 2, half * STATE:(half + 1) * STATE] = piece[:, HALF:]


def weight_kernel(xt_ref, gm_ref, pk_ref, pr_ref, out_ref):
    xt = xt_ref[...]
    out_ref[:, :HALF] = mm(xt, gm_ref[...])
    out_ref[:, HALF:] = mm(xt, (pk_ref[...] + pr_ref[...]).astype(bf16))


def join_kernel(c_ref, yk_ref, yr_ref, out_ref):
    c = c_ref[0]
    yk = yk_ref[...].astype(bf16)
    yr = yr_ref[...].astype(bf16)

    @pl.when(c == 0)
    def _():
        out_ref[:, :HALF] = yk
        out_ref[:, HALF:] = yr

    @pl.when(c != 0)
    def _():
        out_ref[:, :HALF] = yr
        out_ref[:, HALF:] = yk


def whole(shape):
    return pl.BlockSpec(shape, lambda i, c: (0,) * len(shape))


def call(kernel, outs, ins, scratch=(), c=None, specs=None):
    params = pltpu.CompilerParams(vmem_limit_bytes=16 * 1024 * 1024)
    shapes = [jax.ShapeDtypeStruct(s, d) for s, d in outs]
    if c is None:
        return pl.pallas_call(kernel, out_shape=shapes, compiler_params=params)(*ins)
    specs = specs or [whole(a.shape) for a in ins]
    return pl.pallas_call(
        kernel,
        out_shape=shapes,
        grid_spec=pltpu.PrefetchScalarGridSpec(
            num_scalar_prefetch=1, grid=(1,), in_specs=specs,
            out_specs=[whole(s) for s, _ in outs], scratch_shapes=list(scratch)),
        compiler_params=params,
    )(c, *ins)


def body(records, x_weight, bc_weight, decay_codes, out_grad):
    x = records[0]
    g = out_grad[0]
    codes = decay_codes[0]
    d = x.shape[1]
    frames = LD * 2 * ZN
    unit = 1.0 / (32.0 * frames)
    out_scale = float((STATE * frames) ** -0.5)
    grad_scale = float((DP * frames) ** -0.5)
    core = lax.axis_index("c")
    c = core.astype(jnp.int32).reshape(1)
    swap = [(0, 1), (1, 0)]

    codes = codes.T
    here = pl.BlockSpec((LD, HALF), lambda i, c: (0, c[0]))
    there = pl.BlockSpec((LD, HALF), lambda i, c: (0, 1 - c[0]))
    x, g, codes, wx, wbc = (
        pltpu.with_memory_space_constraint(a, pltpu.MemorySpace.HBM)
        for a in (x, g, codes, x_weight, bc_weight))
    (pack,) = call(
        lambda c_ref, *refs: pack_kernel(*refs), [((LD, d + HALF + LD), f32)], (x, g, codes), (), c,
        [whole(x.shape), there, whole(codes.shape)])
    pack = lax.ppermute(pack, "c", swap)
    half = (LD, HALF)
    owned = call(
        lambda c_ref, *refs: own_kernel(*refs),
        [(half, bf16), ((LD, 2 * STATE), bf16), (half, bf16), ((HEADS, LD), f32), ((LD, d), bf16),
         ((d, HALF), bf16), ((d, 2 * STATE), bf16)],
        (x, g, codes, wx, wbc), (), c,
        [whole(x.shape), here, whole(codes.shape), pl.BlockSpec((d, HALF), lambda i, c: (0, c[0])),
         whole(wbc.shape)])

    sq = (CHIP, HALF)
    pay, ue, v, en, te, proj, xc, yl, gml, gpl = call(
        lambda *refs: local_kernel(unit, *refs),
        [((ZN, PAY, STATE), f32), (sq, bf16), (sq, bf16), (sq, f32), (sq, f32), ((CHIP, 2 * STATE), bf16),
         ((CHIP, d), bf16), (sq, f32), (sq, f32), ((CHIP, 2 * STATE), f32)],
        (*owned, pack), [pltpu.VMEM(sq, f32), pltpu.VMEM((HEADS, CHIP), f32), pltpu.VMEM(sq, bf16)], c)

    pay = lax.all_to_all(pay, "z", 0, 0, tiled=True)
    (pay,) = call(scan_kernel, [((ZN, 2 * ROWS, STATE), f32)], (pay,))
    pay = lax.all_to_all(pay, "z", 0, 0, tiled=True)

    gm, pk, ps, yk, ys = call(
        lambda *refs: outer_kernel(out_scale, *refs),
        [(sq, bf16), ((CHIP, STATE), f32), ((CHIP, STATE), f32), ((LD, HALF), f32), ((LD, HALF), f32)],
        (pay, ue, v, en, te, proj, yl, gml, gpl), [pltpu.VMEM(sq, f32)], c)
    pr = lax.ppermute(ps, "c", swap)
    yr = lax.ppermute(ys, "c", swap)
    xt = xc.T.reshape(ZN, 2, DP, 2, CHIP).transpose(2, 0, 1, 3, 4).reshape(d, CHIP)
    width = HALF + STATE
    (grad,) = call(weight_kernel, [((d, width), f32)], (xt, gm, pk, pr))
    (y,) = call(join_kernel, [((LD, 2 * HALF), bf16)], (yk, yr), (), c)

    part = lax.all_to_all(grad.reshape(DP, d // DP, width), "dp", 0, 0, tiled=True)
    (part,) = call(fold_kernel, [((ZN, d // DP // ZN, width), f32)], (part,))
    part = lax.all_to_all(part, "z", 0, 0, tiled=True)
    (part,) = call(lambda *refs: spread_kernel(grad_scale, *refs), [((2 * DP, 2, width), f32)], (part,))
    part = lax.all_to_all(part, ("dp", "c"), 0, 0, tiled=True)
    x_grad, bc_grad = call(place_kernel, [((2 * DP, 2 * HALF), f32), ((2 * DP, 2 * STATE), f32)], (part,))
    return y[None], x_grad, bc_grad


def solution(mesh):
    mesh = Mesh(mesh.devices.reshape(DP, ZN, 2), ("dp", "z", "c"))
    frames = P("dp", ("z", "c"), None)
    rows = P(("z", "c"), None)
    return jax.shard_map(
        body,
        mesh=mesh,
        in_specs=(frames, P(), P(), frames, frames),
        out_specs=(frames, rows, rows),
        check_vma=False,
    )
```

```python
import jax
import jax.numpy as jnp
from jax import lax
from jax.experimental import pallas as pl
from jax.experimental.pallas import tpu as pltpu
from jax.sharding import Mesh, PartitionSpec as P

f32 = jnp.float32
bf16 = jnp.bfloat16

LD = 128
CHIP = 2 * LD
HEADS = 8
HEAD = 64
STATE = 128
HALF = HEADS * HEAD // 2
ZN = 16
DP = 16
GROUP = 4
GROUPS = ZN // GROUP


def mm(a, b):
    return jnp.dot(a, b, preferred_element_type=f32)


def mm_tn(a, b):
    return lax.dot_general(a, b, (((0,), (0,)), ((), ())), preferred_element_type=f32)


def mm_nt(a, b):
    return lax.dot_general(a, b, (((1,), (1,)), ((), ())), preferred_element_type=f32)


def causal(shape):
    return lax.broadcasted_iota(jnp.int32, shape, 0) >= lax.broadcasted_iota(jnp.int32, shape, 1)


def pack_kernel(x_ref, g_ref, codes_ref, out_ref):
    d = x_ref.shape[1]
    out_ref[:, :d] = x_ref[...].astype(f32)
    out_ref[:, d:d + HALF] = g_ref[...].astype(f32)
    out_ref[:, d + HALF:] = jnp.zeros((LD, LD), f32)
    out_ref[0:HEADS, d + HALF:] = codes_ref[...].astype(f32)


def own_kernel(x_ref, g_ref, codes_ref, wx_ref, wbc_ref,
               mix_ref, proj_ref, g_out_ref, codes_out_ref, x_out_ref, wx_out_ref, wbc_out_ref):
    x = x_ref[...]
    wx = wx_ref[...]
    wbc = wbc_ref[...]
    mix_ref[...] = mm(x, wx).astype(bf16)
    proj_ref[...] = mm(x, wbc).astype(bf16)
    g_out_ref[...] = g_ref[...]
    codes_out_ref[...] = codes_ref[...].astype(f32)
    x_out_ref[...] = x
    wx_out_ref[...] = wx
    wbc_out_ref[...] = wbc


def local_kernel(unit, c_ref, mix_ref, pj_ref, g_ref, codes_ref, x_ref, wx_ref, wbc_ref, pack_ref,
                 pay_ref, ue_ref, v_ref, en_ref, te_ref, proj_ref, xc_ref, yl_ref, gm_ref, gp_ref,
                 gs_ref, cs_ref, ms_ref):
    c = c_ref[0]
    own = pl.multiple_of(c * LD, LD)
    oth = pl.multiple_of((1 - c) * LD, LD)
    d = x_ref.shape[1]
    xo = pack_ref[:, :d].astype(bf16)
    xc_ref[pl.ds(own, LD), :] = x_ref[...]
    xc_ref[pl.ds(oth, LD), :] = xo
    gs_ref[pl.ds(own, LD), :] = g_ref[...].astype(f32)
    gs_ref[pl.ds(oth, LD), :] = pack_ref[:, d:d + HALF]
    cs_ref[:, pl.ds(own, LD)] = codes_ref[...]
    cs_ref[:, pl.ds(oth, LD)] = pack_ref[0:HEADS, d + HALF:]
    ms_ref[pl.ds(own, LD), :] = mix_ref[...]
    ms_ref[pl.ds(oth, LD), :] = mm(xo, wx_ref[...]).astype(bf16)
    proj_ref[pl.ds(own, LD), :] = pj_ref[...]
    proj_ref[pl.ds(oth, LD), :] = mm(xo, wbc_ref[...]).astype(bf16)
    codes = cs_ref[...]
    hi = jnp.floor(codes * (1.0 / 32.0))
    lo = codes - 32.0 * hi
    row = lax.broadcasted_iota(jnp.int32, (HEADS, HALF), 0)
    col = lax.broadcasted_iota(jnp.int32, (HEADS, HALF), 1)
    spread = jnp.where(row == col // HEAD + c * (HEADS // 2), 1.0, 0.0).astype(bf16)
    hi = mm_tn(hi.astype(bf16), spread).astype(bf16)
    lo = mm_tn(lo.astype(bf16), spread).astype(bf16)
    mask = causal((CHIP, CHIP))
    tri = jnp.where(mask, 1.0, 0.0).astype(bf16)
    running = unit * (32.0 * mm(tri, hi) + mm(tri, lo))
    last = running[CHIP - 1:CHIP, :]
    en = jnp.exp(-running)
    ep = jnp.exp(running)
    te = jnp.exp(running - last)
    en_ref[...] = en
    te_ref[...] = te
    mixer = ms_ref[...].astype(f32)
    inject = proj_ref[:, :STATE]
    readout = proj_ref[:, STATE:]
    v = (en * gs_ref[...]).astype(bf16)
    ue = (te * mixer).astype(bf16)
    u = (ep * mixer).astype(bf16)
    ue_ref[...] = ue
    v_ref[...] = v
    state = mm_tn(ue, inject)
    adjoint = mm_tn(v, readout)
    for h in range(GROUP):
        pay_ref[h, 0:HEAD, :] = state[h * HEAD:(h + 1) * HEAD, :]
        pay_ref[h, HEAD:2 * HEAD, :] = adjoint[h * HEAD:(h + 1) * HEAD, :]
        pay_ref[h, 2 * HEAD:, :] = jnp.broadcast_to(last[:, h * HEAD:h * HEAD + 1], (8, STATE))
    scores = jnp.where(mask, mm_nt(readout, inject), 0.0).astype(bf16)
    pairs = jnp.where(mask, mm_nt(v, u), 0.0).astype(bf16)
    yl_ref[...] = en * mm(scores, u)
    gm_ref[...] = ep * mm_tn(scores, v)
    gp_ref[:, :STATE] = mm_tn(pairs, readout)
    gp_ref[:, STATE:] = mm(pairs, inject)


def total_kernel(c_ref, in_ref, out_ref):
    group = c_ref[0]
    logs = [in_ref[k, 2 * HEAD:, :] for k in range(GROUP)]
    decay = [jnp.exp(-a[0:1, :]) for a in logs]
    state = in_ref[0, 0:HEAD, :]
    for k in range(1, GROUP):
        state = decay[k] * state + in_ref[k, 0:HEAD, :]
    adjoint = in_ref[GROUP - 1, HEAD:2 * HEAD, :]
    for k in reversed(range(GROUP - 1)):
        adjoint = decay[k] * adjoint + in_ref[k, HEAD:2 * HEAD, :]
    total = logs[0] + logs[1] + logs[2] + logs[3]
    for k in range(GROUPS):
        out_ref[k, 0:HEAD, :] = jnp.where(k > group, state, adjoint)
        out_ref[k, HEAD:, :] = total


def prefix_kernel(c_ref, in_ref, far_ref, out_ref):
    group = c_ref[0]
    far = [jnp.exp(-far_ref[k, HEAD:HEAD + 1, :]) for k in range(GROUPS)]
    decay = [jnp.exp(-in_ref[k, 2 * HEAD:2 * HEAD + 1, :]) for k in range(GROUP)]
    carry = jnp.zeros((HEAD, STATE), f32)
    for k in range(GROUPS - 1):
        carry = jnp.where(k < group, far[k] * carry + far_ref[k, 0:HEAD, :], carry)
    for k in range(GROUP):
        out_ref[k, 0:HEAD, :] = carry
        if k + 1 < GROUP:
            carry = decay[k] * carry + in_ref[k, 0:HEAD, :]
    carry = jnp.zeros((HEAD, STATE), f32)
    for k in reversed(range(1, GROUPS)):
        carry = jnp.where(k > group, far[k] * carry + far_ref[k, 0:HEAD, :], carry)
    for k in reversed(range(GROUP)):
        out_ref[k, HEAD:, :] = carry
        if k:
            carry = decay[k] * carry + in_ref[k, HEAD:2 * HEAD, :]


def outer_kernel(scale, c_ref, in_ref, u_ref, v_ref, en_ref, te_ref, proj_ref,
                 yl_ref, gml_ref, gp_ref, gm_ref, pk_ref, yk_ref, send_ref, y_ref):
    c = c_ref[0]
    carry = in_ref[:, 0:HEAD, :].reshape(HALF, STATE).astype(bf16)
    adjoint = in_ref[:, HEAD:, :].reshape(HALF, STATE).astype(bf16)
    inject = proj_ref[:, :STATE]
    readout = proj_ref[:, STATE:]
    gi = scale * (gp_ref[:, :STATE] + mm(u_ref[...], adjoint))
    gr = scale * (gp_ref[:, STATE:] + mm(v_ref[...], carry))
    pk_ref[...] = jnp.where(c == 0, gi, gr)
    send_ref[0:CHIP, :] = jnp.where(c == 0, gr, gi)
    grad = gml_ref[...] + te_ref[...] * mm_nt(inject, adjoint)
    gm_ref[...] = (scale * grad).astype(bf16)
    y_ref[...] = yl_ref[...] + en_ref[...] * mm_nt(readout, carry)
    yk_ref[...] = y_ref[pl.ds(pl.multiple_of(c * LD, LD), LD), :]
    there = y_ref[pl.ds(pl.multiple_of((1 - c) * LD, LD), LD), :]
    send_ref[CHIP:CHIP + LD, :] = there[:, :LD]
    send_ref[CHIP + LD:, :] = there[:, LD:]


def fold_kernel(in_ref, out_ref):
    total = jnp.sum(in_ref[...], axis=0)
    step = out_ref.shape[1]
    for k in range(ZN):
        out_ref[k] = total[k * step:(k + 1) * step, :]


def spread_kernel(scale, in_ref, out_ref):
    total = scale * jnp.sum(in_ref[...], axis=0)
    for k in range(2 * DP):
        half = k % 2
        out_ref[k] = total[2 * half:2 * half + 2, :]


def place_kernel(in_ref, x_ref, bc_ref):
    for k in range(DP):
        for half in range(2):
            piece = in_ref[2 * k + half]
            x_ref[2 * k:2 * k + 2, half * HALF:(half + 1) * HALF] = piece[:, :HALF]
            bc_ref[2 * k:2 * k + 2, half * STATE:(half + 1) * STATE] = piece[:, HALF:]


def weight_kernel(c_ref, xt_ref, gm_ref, pk_ref, yk_ref, recv_ref, out_ref, y_ref):
    xt = xt_ref[...]
    out_ref[:, :HALF] = mm(xt, gm_ref[...])
    out_ref[:, HALF:] = mm(xt, (pk_ref[...] + recv_ref[0:CHIP, :]).astype(bf16))
    c = c_ref[0]
    own = pl.multiple_of(c * HALF, LD)
    oth = pl.multiple_of((1 - c) * HALF, LD)
    y_ref[:, pl.ds(own, HALF)] = yk_ref[...].astype(bf16)
    y_ref[:, pl.ds(oth, LD)] = recv_ref[CHIP:CHIP + LD, :].astype(bf16)
    y_ref[:, pl.ds(pl.multiple_of(oth + LD, LD), LD)] = recv_ref[CHIP + LD:, :].astype(bf16)


def whole(shape):
    return pl.BlockSpec(shape, lambda i, c: (0,) * len(shape))


def call(kernel, outs, ins, scratch=(), c=None, specs=None):
    params = pltpu.CompilerParams(vmem_limit_bytes=16 * 1024 * 1024)
    shapes = [jax.ShapeDtypeStruct(s, d) for s, d in outs]
    if c is None:
        return pl.pallas_call(kernel, out_shape=shapes, compiler_params=params)(*ins)
    specs = specs or [whole(a.shape) for a in ins]
    return pl.pallas_call(
        kernel,
        out_shape=shapes,
        grid_spec=pltpu.PrefetchScalarGridSpec(
            num_scalar_prefetch=1, grid=(1,), in_specs=specs,
            out_specs=[whole(s) for s, _ in outs], scratch_shapes=list(scratch)),
        compiler_params=params,
    )(c, *ins)


def body(records, x_weight, bc_weight, decay_codes, out_grad):
    x = records[0]
    g = out_grad[0]
    codes = decay_codes[0]
    d = x.shape[1]
    frames = LD * 2 * ZN
    unit = 1.0 / (32.0 * frames)
    out_scale = float((STATE * frames) ** -0.5)
    grad_scale = float((DP * frames) ** -0.5)
    core = lax.axis_index("c")
    c = core.astype(jnp.int32).reshape(1)
    group = lax.axis_index("zh").astype(jnp.int32).reshape(1)
    swap = [(0, 1), (1, 0)]

    codes = codes.T
    here = pl.BlockSpec((LD, HALF), lambda i, c: (0, c[0]))
    there = pl.BlockSpec((LD, HALF), lambda i, c: (0, 1 - c[0]))
    x, g, codes, wx, wbc = (
        pltpu.with_memory_space_constraint(a, pltpu.MemorySpace.HBM)
        for a in (x, g, codes, x_weight, bc_weight))
    (pack,) = call(
        lambda c_ref, *refs: pack_kernel(*refs), [((LD, d + HALF + LD), f32)], (x, g, codes), (), c,
        [whole(x.shape), there, whole(codes.shape)])
    pack = lax.ppermute(pack, "c", swap)
    half = (LD, HALF)
    owned = call(
        lambda c_ref, *refs: own_kernel(*refs),
        [(half, bf16), ((LD, 2 * STATE), bf16), (half, bf16), ((HEADS, LD), f32), ((LD, d), bf16),
         ((d, HALF), bf16), ((d, 2 * STATE), bf16)],
        (x, g, codes, wx, wbc), (), c,
        [whole(x.shape), here, whole(codes.shape), pl.BlockSpec((d, HALF), lambda i, c: (0, c[0])),
         whole(wbc.shape)])

    sq = (CHIP, HALF)
    pay, ue, v, en, te, proj, xc, yl, gml, gpl = call(
        lambda *refs: local_kernel(unit, *refs),
        [((GROUP, 2 * HEAD + 8, STATE), f32), (sq, bf16), (sq, bf16), (sq, f32), (sq, f32), ((CHIP, 2 * STATE), bf16),
         ((CHIP, d), bf16), (sq, f32), (sq, f32), ((CHIP, 2 * STATE), f32)],
        (*owned, pack), [pltpu.VMEM(sq, f32), pltpu.VMEM((HEADS, CHIP), f32), pltpu.VMEM(sq, bf16)], c)

    pay = lax.all_to_all(pay, "zl", 0, 0, tiled=True)
    (far,) = call(total_kernel, [((GROUPS, HEAD + 8, STATE), f32)], (pay,), (), group)
    far = lax.all_to_all(far, "zh", 0, 0, tiled=True)
    (pay,) = call(prefix_kernel, [((GROUP, 2 * HEAD, STATE), f32)], (pay, far), (), group)
    pay = lax.all_to_all(pay, "zl", 0, 0, tiled=True)

    gm, pk, yk, send = call(
        lambda *refs: outer_kernel(out_scale, *refs),
        [(sq, bf16), ((CHIP, STATE), f32), ((LD, HALF), f32), ((2 * CHIP, LD), f32)],
        (pay, ue, v, en, te, proj, yl, gml, gpl), [pltpu.VMEM(sq, f32)], c)
    recv = lax.ppermute(send, "c", swap)
    xt = xc.T.reshape(ZN, 2, DP, 2, CHIP).transpose(2, 0, 1, 3, 4).reshape(d, CHIP)
    width = HALF + STATE
    grad, y = call(weight_kernel, [((d, width), f32), ((LD, 2 * HALF), bf16)], (xt, gm, pk, yk, recv), (), c)

    part = lax.all_to_all(grad.reshape(DP, d // DP, width), "dp", 0, 0, tiled=True)
    (part,) = call(fold_kernel, [((ZN, d // DP // ZN, width), f32)], (part,))
    part = lax.all_to_all(part, ("zh", "zl"), 0, 0, tiled=True)
    (part,) = call(lambda *refs: spread_kernel(grad_scale, *refs), [((2 * DP, 2, width), f32)], (part,))
    part = lax.all_to_all(part, ("dp", "c"), 0, 0, tiled=True)
    x_grad, bc_grad = call(place_kernel, [((2 * DP, 2 * HALF), f32), ((2 * DP, 2 * STATE), f32)], (part,))
    return y[None], x_grad, bc_grad


def solution(mesh):
    mesh = Mesh(mesh.devices.reshape(DP, GROUPS, GROUP, 2), ("dp", "zh", "zl", "c"))
    frames = P("dp", ("zh", "zl", "c"), None)
    rows = P(("zh", "zl", "c"), None)
    return jax.shard_map(
        body,
        mesh=mesh,
        in_specs=(frames, P(), P(), frames, frames),
        out_specs=(frames, rows, rows),
        check_vma=False,
    )
```

```python
import jax
import jax.numpy as jnp
from jax import lax
from jax.experimental import pallas as pl
from jax.experimental.pallas import tpu as pltpu
from jax.sharding import Mesh, PartitionSpec as P

f32 = jnp.float32
bf16 = jnp.bfloat16

LD = 128
CHIP = 2 * LD
HEADS = 8
HEAD = 64
STATE = 128
HALF = HEADS * HEAD // 2
ZN = 16
DP = 16
GROUP = 4
GROUPS = ZN // GROUP


def mm(a, b):
    return jnp.dot(a, b, preferred_element_type=f32)


def mm_tn(a, b):
    return lax.dot_general(a, b, (((0,), (0,)), ((), ())), preferred_element_type=f32)


def mm_nt(a, b):
    return lax.dot_general(a, b, (((1,), (1,)), ((), ())), preferred_element_type=f32)


def causal(shape):
    return lax.broadcasted_iota(jnp.int32, shape, 0) >= lax.broadcasted_iota(jnp.int32, shape, 1)


def pack_kernel(c_ref, group_ref, x_ref, g_ref, codes_ref, out_ref):
    d = x_ref.shape[1]
    out_ref[:, :d] = x_ref[...].astype(f32)
    out_ref[:, d:d + HALF] = g_ref[...].astype(f32)
    out_ref[:, d + HALF:] = jnp.zeros((LD, LD), f32)
    out_ref[0:HEADS, d + HALF:] = codes_ref[...].astype(f32)


def own_kernel(c_ref, group_ref, x_ref, g_ref, codes_ref, wx_ref, wbc_ref,
               mix_ref, proj_ref, g_out_ref, codes_out_ref, x_out_ref, wx_out_ref, wbc_out_ref):
    x = x_ref[...]
    wx = wx_ref[...]
    wbc = wbc_ref[...]
    mix_ref[...] = mm(x, wx).astype(bf16)
    proj_ref[...] = mm(x, wbc).astype(bf16)
    g_out_ref[...] = g_ref[...]
    codes_out_ref[...] = codes_ref[...].astype(f32)
    x_out_ref[...] = x
    wx_out_ref[...] = wx
    wbc_out_ref[...] = wbc


def local_kernel(unit, c_ref, group_ref, mix_ref, pj_ref, g_ref, codes_ref, x_ref, wx_ref, wbc_ref, pack_ref,
                 pay_ref, ue_ref, v_ref, en_ref, te_ref, proj_ref, xc_ref, yl_ref, gm_ref, gp_ref,
                 gs_ref, cs_ref, ms_ref):
    c = c_ref[0]
    own = pl.multiple_of(c * LD, LD)
    oth = pl.multiple_of((1 - c) * LD, LD)
    d = x_ref.shape[1]
    xo = pack_ref[:, :d].astype(bf16)
    xc_ref[pl.ds(own, LD), :] = x_ref[...]
    xc_ref[pl.ds(oth, LD), :] = xo
    gs_ref[pl.ds(own, LD), :] = g_ref[...].astype(f32)
    gs_ref[pl.ds(oth, LD), :] = pack_ref[:, d:d + HALF]
    cs_ref[:, pl.ds(own, LD)] = codes_ref[...]
    cs_ref[:, pl.ds(oth, LD)] = pack_ref[0:HEADS, d + HALF:]
    ms_ref[pl.ds(own, LD), :] = mix_ref[...]
    ms_ref[pl.ds(oth, LD), :] = mm(xo, wx_ref[...]).astype(bf16)
    proj_ref[pl.ds(own, LD), :] = pj_ref[...]
    proj_ref[pl.ds(oth, LD), :] = mm(xo, wbc_ref[...]).astype(bf16)
    codes = cs_ref[...]
    hi = jnp.floor(codes * (1.0 / 32.0))
    lo = codes - 32.0 * hi
    row = lax.broadcasted_iota(jnp.int32, (HEADS, HALF), 0)
    col = lax.broadcasted_iota(jnp.int32, (HEADS, HALF), 1)
    spread = jnp.where(row == col // HEAD + c * (HEADS // 2), 1.0, 0.0).astype(bf16)
    hi = mm_tn(hi.astype(bf16), spread).astype(bf16)
    lo = mm_tn(lo.astype(bf16), spread).astype(bf16)
    mask = causal((CHIP, CHIP))
    tri = jnp.where(mask, 1.0, 0.0).astype(bf16)
    running = unit * (32.0 * mm(tri, hi) + mm(tri, lo))
    last = running[CHIP - 1:CHIP, :]
    en = jnp.exp(-running)
    ep = jnp.exp(running)
    te = jnp.exp(running - last)
    en_ref[...] = en
    te_ref[...] = te
    mixer = ms_ref[...].astype(f32)
    inject = proj_ref[:, :STATE]
    readout = proj_ref[:, STATE:]
    v = (en * gs_ref[...]).astype(bf16)
    ue = (te * mixer).astype(bf16)
    u = (ep * mixer).astype(bf16)
    ue_ref[...] = ue
    v_ref[...] = v
    state = mm_tn(ue, inject)
    adjoint = mm_tn(v, readout)
    for h in range(GROUP):
        at = (group_ref[0] + h) & (GROUP - 1)
        pay_ref[at, 0:HEAD, :] = state[h * HEAD:(h + 1) * HEAD, :]
        pay_ref[at, HEAD:2 * HEAD, :] = adjoint[h * HEAD:(h + 1) * HEAD, :]
        pay_ref[at, 2 * HEAD:, :] = jnp.broadcast_to(last[:, h * HEAD:h * HEAD + 1], (8, STATE))
    scores = jnp.where(mask, mm_nt(readout, inject), 0.0).astype(bf16)
    pairs = jnp.where(mask, mm_nt(v, u), 0.0).astype(bf16)
    yl_ref[...] = en * mm(scores, u)
    gm_ref[...] = ep * mm_tn(scores, v)
    gp_ref[:, :STATE] = mm_tn(pairs, readout)
    gp_ref[:, STATE:] = mm(pairs, inject)


def total_kernel(c_ref, group_ref, in_ref, out_ref):
    group = group_ref[0]
    logs = [in_ref[k, 2 * HEAD:, :] for k in range(GROUP)]
    decay = [jnp.exp(-a[0:1, :]) for a in logs]
    state = in_ref[0, 0:HEAD, :]
    for k in range(1, GROUP):
        state = decay[k] * state + in_ref[k, 0:HEAD, :]
    adjoint = in_ref[GROUP - 1, HEAD:2 * HEAD, :]
    for k in reversed(range(GROUP - 1)):
        adjoint = decay[k] * adjoint + in_ref[k, HEAD:2 * HEAD, :]
    total = logs[0] + logs[1] + logs[2] + logs[3]
    for k in range(GROUPS):
        out_ref[k, 0:HEAD, :] = jnp.where(k > group, state, adjoint)
        out_ref[k, HEAD:, :] = total


def prefix_kernel(c_ref, group_ref, in_ref, far_ref, out_ref):
    group = group_ref[0]
    far = [jnp.exp(-far_ref[k, HEAD:HEAD + 1, :]) for k in range(GROUPS)]
    decay = [jnp.exp(-in_ref[k, 2 * HEAD:2 * HEAD + 1, :]) for k in range(GROUP)]
    carry = jnp.zeros((HEAD, STATE), f32)
    for k in range(GROUPS - 1):
        carry = jnp.where(k < group, far[k] * carry + far_ref[k, 0:HEAD, :], carry)
    for k in range(GROUP):
        out_ref[k, 0:HEAD, :] = carry
        if k + 1 < GROUP:
            carry = decay[k] * carry + in_ref[k, 0:HEAD, :]
    carry = jnp.zeros((HEAD, STATE), f32)
    for k in reversed(range(1, GROUPS)):
        carry = jnp.where(k > group, far[k] * carry + far_ref[k, 0:HEAD, :], carry)
    for k in reversed(range(GROUP)):
        out_ref[k, HEAD:, :] = carry
        if k:
            carry = decay[k] * carry + in_ref[k, HEAD:2 * HEAD, :]


def outer_kernel(scale, c_ref, group_ref, in_ref, u_ref, v_ref, en_ref, te_ref, proj_ref,
                 yl_ref, gml_ref, gp_ref, gm_ref, pk_ref, yk_ref, send_ref, y_ref):
    c = c_ref[0]
    pieces = [in_ref[(group_ref[0] + h) & (GROUP - 1)] for h in range(GROUP)]
    carry = jnp.concatenate([a[:HEAD] for a in pieces], axis=0).astype(bf16)
    adjoint = jnp.concatenate([a[HEAD:] for a in pieces], axis=0).astype(bf16)
    inject = proj_ref[:, :STATE]
    readout = proj_ref[:, STATE:]
    gi = scale * (gp_ref[:, :STATE] + mm(u_ref[...], adjoint))
    gr = scale * (gp_ref[:, STATE:] + mm(v_ref[...], carry))
    pk_ref[...] = jnp.where(c == 0, gi, gr)
    send_ref[0:CHIP, :] = jnp.where(c == 0, gr, gi)
    grad = gml_ref[...] + te_ref[...] * mm_nt(inject, adjoint)
    gm_ref[...] = (scale * grad).astype(bf16)
    y_ref[...] = yl_ref[...] + en_ref[...] * mm_nt(readout, carry)
    yk_ref[...] = y_ref[pl.ds(pl.multiple_of(c * LD, LD), LD), :]
    there = y_ref[pl.ds(pl.multiple_of((1 - c) * LD, LD), LD), :]
    send_ref[CHIP:CHIP + LD, :] = there[:, :LD]
    send_ref[CHIP + LD:, :] = there[:, LD:]


def weight_kernel(c_ref, group_ref, xt_ref, gm_ref, pk_ref, recv_ref, out_ref):
    xt = xt_ref[...]
    out_ref[:, :HALF] = mm(xt, gm_ref[...])
    out_ref[:, HALF:] = mm(xt, (pk_ref[...] + recv_ref[...]).astype(bf16))


def fold_kernel(c_ref, group_ref, in_ref, out_ref):
    total = jnp.sum(in_ref[...], axis=0)
    step = out_ref.shape[1]
    for k in range(ZN):
        out_ref[k] = total[k * step:(k + 1) * step, :]


def spread_kernel(scale, c_ref, group_ref, in_ref, out_ref):
    total = scale * jnp.sum(in_ref[...], axis=0)
    for k in range(2 * DP):
        half = k % 2
        out_ref[k] = total[2 * half:2 * half + 2, :]


def place_kernel(c_ref, group_ref, in_ref, yk_ref, recv_ref, x_ref, bc_ref, y_ref):
    for k in range(DP):
        for half in range(2):
            piece = in_ref[2 * k + half]
            x_ref[2 * k:2 * k + 2, half * HALF:(half + 1) * HALF] = piece[:, :HALF]
            bc_ref[2 * k:2 * k + 2, half * STATE:(half + 1) * STATE] = piece[:, HALF:]
    c = c_ref[0]
    own = pl.multiple_of(c * HALF, LD)
    oth = pl.multiple_of((1 - c) * HALF, LD)
    y_ref[:, pl.ds(own, HALF)] = yk_ref[...].astype(bf16)
    y_ref[:, pl.ds(oth, LD)] = recv_ref[0:LD, :].astype(bf16)
    y_ref[:, pl.ds(pl.multiple_of(oth + LD, LD), LD)] = recv_ref[LD:, :].astype(bf16)


def whole(shape):
    return pl.BlockSpec(shape, lambda i, c, g: (0,) * len(shape))


def call(kernel, place, outs, ins, scratch=(), specs=None):
    return pl.pallas_call(
        kernel,
        out_shape=[jax.ShapeDtypeStruct(s, d) for s, d in outs],
        grid_spec=pltpu.PrefetchScalarGridSpec(
            num_scalar_prefetch=2, grid=(1,), in_specs=specs or [whole(a.shape) for a in ins],
            out_specs=[whole(s) for s, _ in outs], scratch_shapes=list(scratch)),
        compiler_params=pltpu.CompilerParams(vmem_limit_bytes=16 * 1024 * 1024),
    )(*place, *ins)


def body(records, x_weight, bc_weight, decay_codes, out_grad):
    x = records[0]
    g = out_grad[0]
    codes = decay_codes[0].T
    d = x.shape[1]
    frames = LD * 2 * ZN
    unit = 1.0 / (32.0 * frames)
    out_scale = float((STATE * frames) ** -0.5)
    grad_scale = float((DP * frames) ** -0.5)
    place = lax.optimization_barrier((
        lax.axis_index("c").astype(jnp.int32).reshape(1),
        lax.div(lax.axis_index("z"), GROUP).astype(jnp.int32).reshape(1)))
    swap = [(0, 1), (1, 0)]
    near = [[GROUP * a + b for b in range(GROUP)] for a in range(GROUPS)]
    across = [[GROUP * a + (a + b) % GROUP for a in range(GROUPS)] for b in range(GROUP)]

    here = pl.BlockSpec((LD, HALF), lambda i, c, g: (0, c[0]))
    there = pl.BlockSpec((LD, HALF), lambda i, c, g: (0, 1 - c[0]))
    x, g, codes, wx, wbc = (
        pltpu.with_memory_space_constraint(a, pltpu.MemorySpace.HBM)
        for a in (x, g, codes, x_weight, bc_weight))
    (pack,) = call(
        pack_kernel, place, [((LD, d + HALF + LD), f32)], (x, g, codes), (),
        [whole(x.shape), there, whole(codes.shape)])
    pack = lax.ppermute(pack, "c", swap)
    half = (LD, HALF)
    owned = call(
        own_kernel, place,
        [(half, bf16), ((LD, 2 * STATE), bf16), (half, bf16), ((HEADS, LD), f32), ((LD, d), bf16),
         ((d, HALF), bf16), ((d, 2 * STATE), bf16)],
        (x, g, codes, wx, wbc), (),
        [whole(x.shape), here, whole(codes.shape), pl.BlockSpec((d, HALF), lambda i, c, g: (0, c[0])),
         whole(wbc.shape)])

    sq = (CHIP, HALF)
    pay, ue, v, en, te, proj, xc, yl, gml, gpl = call(
        lambda *refs: local_kernel(unit, *refs), place,
        [((GROUP, 2 * HEAD + 8, STATE), f32), (sq, bf16), (sq, bf16), (sq, f32), (sq, f32),
         ((CHIP, 2 * STATE), bf16), ((CHIP, d), bf16), (sq, f32), (sq, f32), ((CHIP, 2 * STATE), f32)],
        (*owned, pack), [pltpu.VMEM(sq, f32), pltpu.VMEM((HEADS, CHIP), f32), pltpu.VMEM(sq, bf16)])

    pay = lax.all_to_all(pay, "z", 0, 0, tiled=True, axis_index_groups=near)
    (far,) = call(total_kernel, place, [((GROUPS, HEAD + 8, STATE), f32)], (pay,))
    far = lax.all_to_all(far, "z", 0, 0, tiled=True, axis_index_groups=across)
    (pay,) = call(prefix_kernel, place, [((GROUP, 2 * HEAD, STATE), f32)], (pay, far))
    pay = lax.all_to_all(pay, "z", 0, 0, tiled=True, axis_index_groups=near)

    gm, pk, yk, send = call(
        lambda *refs: outer_kernel(out_scale, *refs), place,
        [(sq, bf16), ((CHIP, STATE), f32), ((LD, HALF), f32), ((2 * CHIP, LD), f32)],
        (pay, ue, v, en, te, proj, yl, gml, gpl), [pltpu.VMEM(sq, f32)])
    recv = lax.ppermute(send, "c", swap)
    xt = xc.T.reshape(ZN, 2, DP, 2, CHIP).transpose(2, 0, 1, 3, 4).reshape(d, CHIP)
    width = HALF + STATE
    top = pl.BlockSpec((CHIP, LD), lambda i, c, g: (0, 0))
    low = pl.BlockSpec((CHIP, LD), lambda i, c, g: (1, 0))
    (grad,) = call(
        weight_kernel, place, [((d, width), f32)], (xt, gm, pk, recv), (),
        [whole(xt.shape), whole(gm.shape), whole(pk.shape), top])

    part = lax.all_to_all(grad.reshape(DP, d // DP, width), "dp", 0, 0, tiled=True)
    (part,) = call(fold_kernel, place, [((ZN, d // DP // ZN, width), f32)], (part,))
    part = lax.all_to_all(part, "z", 0, 0, tiled=True)
    (part,) = call(lambda *refs: spread_kernel(grad_scale, *refs), place, [((2 * DP, 2, width), f32)], (part,))
    part = lax.all_to_all(part, ("dp", "c"), 0, 0, tiled=True)
    x_grad, bc_grad, y = call(
        place_kernel, place,
        [((2 * DP, 2 * HALF), f32), ((2 * DP, 2 * STATE), f32), ((LD, 2 * HALF), bf16)], (part, yk, recv), (),
        [whole(part.shape), whole(yk.shape), low])
    return y[None], x_grad, bc_grad


def solution(mesh):
    mesh = Mesh(mesh.devices.reshape(DP, ZN, 2), ("dp", "z", "c"))
    frames = P("dp", ("z", "c"), None)
    rows = P(("z", "c"), None)
    return jax.shard_map(
        body,
        mesh=mesh,
        in_specs=(frames, P(), P(), frames, frames),
        out_specs=(frames, rows, rows),
        check_vma=False,
    )
```

```python
import jax
import jax.numpy as jnp
from jax import lax
from jax.experimental import pallas as pl
from jax.experimental.pallas import tpu as pltpu
from jax.sharding import Mesh, PartitionSpec as P

f32 = jnp.float32
bf16 = jnp.bfloat16

LD = 128
CHIP = 2 * LD
HEADS = 8
HEAD = 64
STATE = 128
HALF = HEADS * HEAD // 2
ZN = 16
DP = 16
GROUP = 4
GROUPS = ZN // GROUP


def mm(a, b):
    return jnp.dot(a, b, preferred_element_type=f32)


def mm_tn(a, b):
    return lax.dot_general(a, b, (((0,), (0,)), ((), ())), preferred_element_type=f32)


def mm_nt(a, b):
    return lax.dot_general(a, b, (((1,), (1,)), ((), ())), preferred_element_type=f32)


def causal(shape):
    return lax.broadcasted_iota(jnp.int32, shape, 0) >= lax.broadcasted_iota(jnp.int32, shape, 1)


def pack_kernel(c_ref, group_ref, x_hbm, g_hbm, codes_hbm, out_ref, x_ref, g_ref, codes_ref,
                there_ref, int_ref, sems):
    c = c_ref[0]
    d = x_ref.shape[1]
    own = pl.multiple_of(c * HALF, HALF)
    oth = pl.multiple_of((1 - c) * HALF, HALF)
    copies = [
        pltpu.make_async_copy(x_hbm, x_ref, sems.at[0]),
        pltpu.make_async_copy(g_hbm.at[:, pl.ds(oth, HALF)], there_ref, sems.at[1]),
        pltpu.make_async_copy(codes_hbm, int_ref, sems.at[2]),
        pltpu.make_async_copy(g_hbm.at[:, pl.ds(own, HALF)], g_ref, sems.at[3]),
    ]
    for copy in copies:
        copy.start()
    for copy in copies:
        copy.wait()
    codes = int_ref[...].astype(f32)
    codes_ref[...] = codes
    out_ref[:, :d] = x_ref[...].astype(f32)
    out_ref[:, d:d + HALF] = there_ref[...].astype(f32)
    out_ref[HEADS:, d + HALF:] = jnp.zeros((LD - HEADS, LD), f32)
    out_ref[0:HEADS, d + HALF:] = codes


def own_kernel(c_ref, group_ref, x_ref, wx_hbm, wbc_hbm, mix_ref, proj_ref, wx_ref, wbc_ref, sems):
    own = pl.multiple_of(c_ref[0] * HALF, HALF)
    first = pltpu.make_async_copy(wx_hbm.at[:, pl.ds(own, HALF)], wx_ref, sems.at[0])
    second = pltpu.make_async_copy(wbc_hbm, wbc_ref, sems.at[1])
    first.start()
    second.start()
    x = x_ref[...]
    first.wait()
    mix_ref[...] = mm(x, wx_ref[...]).astype(bf16)
    second.wait()
    proj_ref[...] = mm(x, wbc_ref[...]).astype(bf16)


def local_kernel(unit, c_ref, group_ref, mix_ref, pj_ref, wx_ref, wbc_ref, x_ref, g_ref, codes_ref, pack_ref,
                 pay_ref, ue_ref, v_ref, en_ref, te_ref, proj_ref, xc_ref, yl_ref, gm_ref, gp_ref,
                 gs_ref, cs_ref, ms_ref):
    c = c_ref[0]
    own = pl.multiple_of(c * LD, LD)
    oth = pl.multiple_of((1 - c) * LD, LD)
    d = x_ref.shape[1]
    xo = pack_ref[:, :d].astype(bf16)
    xc_ref[pl.ds(own, LD), :] = x_ref[...]
    xc_ref[pl.ds(oth, LD), :] = xo
    gs_ref[pl.ds(own, LD), :] = g_ref[...].astype(f32)
    gs_ref[pl.ds(oth, LD), :] = pack_ref[:, d:d + HALF]
    cs_ref[:, pl.ds(own, LD)] = codes_ref[...]
    cs_ref[:, pl.ds(oth, LD)] = pack_ref[0:HEADS, d + HALF:]
    ms_ref[pl.ds(own, LD), :] = mix_ref[...]
    ms_ref[pl.ds(oth, LD), :] = mm(xo, wx_ref[...]).astype(bf16)
    proj_ref[pl.ds(own, LD), :] = pj_ref[...]
    proj_ref[pl.ds(oth, LD), :] = mm(xo, wbc_ref[...]).astype(bf16)
    codes = cs_ref[...]
    hi = jnp.floor(codes * (1.0 / 32.0))
    lo = codes - 32.0 * hi
    row = lax.broadcasted_iota(jnp.int32, (HEADS, HALF), 0)
    col = lax.broadcasted_iota(jnp.int32, (HEADS, HALF), 1)
    spread = jnp.where(row == col // HEAD + c * (HEADS // 2), 1.0, 0.0).astype(bf16)
    hi = mm_tn(hi.astype(bf16), spread).astype(bf16)
    lo = mm_tn(lo.astype(bf16), spread).astype(bf16)
    mask = causal((CHIP, CHIP))
    tri = jnp.where(mask, 1.0, 0.0).astype(bf16)
    running = unit * (32.0 * mm(tri, hi) + mm(tri, lo))
    last = running[CHIP - 1:CHIP, :]
    en = jnp.exp(-running)
    ep = jnp.exp(running)
    te = jnp.exp(running - last)
    en_ref[...] = en
    te_ref[...] = te
    mixer = ms_ref[...].astype(f32)
    inject = proj_ref[:, :STATE]
    readout = proj_ref[:, STATE:]
    v = (en * gs_ref[...]).astype(bf16)
    ue = (te * mixer).astype(bf16)
    u = (ep * mixer).astype(bf16)
    ue_ref[...] = ue
    v_ref[...] = v
    state = mm_tn(ue, inject)
    adjoint = mm_tn(v, readout)
    for h in range(GROUP):
        at = (group_ref[0] + h) & (GROUP - 1)
        pay_ref[at, 0:HEAD, :] = state[h * HEAD:(h + 1) * HEAD, :]
        pay_ref[at, HEAD:2 * HEAD, :] = adjoint[h * HEAD:(h + 1) * HEAD, :]
        pay_ref[at, 2 * HEAD:, :] = jnp.broadcast_to(last[:, h * HEAD:h * HEAD + 1], (8, STATE))
    scores = jnp.where(mask, mm_nt(readout, inject), 0.0).astype(bf16)
    pairs = jnp.where(mask, mm_nt(v, u), 0.0).astype(bf16)
    yl_ref[...] = en * mm(scores, u)
    gm_ref[...] = ep * mm_tn(scores, v)
    gp_ref[:, :STATE] = mm_tn(pairs, readout)
    gp_ref[:, STATE:] = mm(pairs, inject)


def total_kernel(c_ref, group_ref, in_ref, out_ref):
    group = group_ref[0]
    logs = [in_ref[k, 2 * HEAD:, :] for k in range(GROUP)]
    decay = [jnp.exp(-a[0:1, :]) for a in logs]
    state = in_ref[0, 0:HEAD, :]
    for k in range(1, GROUP):
        state = decay[k] * state + in_ref[k, 0:HEAD, :]
    adjoint = in_ref[GROUP - 1, HEAD:2 * HEAD, :]
    for k in reversed(range(GROUP - 1)):
        adjoint = decay[k] * adjoint + in_ref[k, HEAD:2 * HEAD, :]
    total = logs[0] + logs[1] + logs[2] + logs[3]
    for k in range(GROUPS):
        out_ref[k, 0:HEAD, :] = jnp.where(k > group, state, adjoint)
        out_ref[k, HEAD:, :] = total


def prefix_kernel(c_ref, group_ref, in_ref, far_ref, out_ref):
    group = group_ref[0]
    far = [jnp.exp(-far_ref[k, HEAD:HEAD + 1, :]) for k in range(GROUPS)]
    decay = [jnp.exp(-in_ref[k, 2 * HEAD:2 * HEAD + 1, :]) for k in range(GROUP)]
    carry = jnp.zeros((HEAD, STATE), f32)
    for k in range(GROUPS - 1):
        carry = jnp.where(k < group, far[k] * carry + far_ref[k, 0:HEAD, :], carry)
    for k in range(GROUP):
        out_ref[k, 0:HEAD, :] = carry
        if k + 1 < GROUP:
            carry = decay[k] * carry + in_ref[k, 0:HEAD, :]
    carry = jnp.zeros((HEAD, STATE), f32)
    for k in reversed(range(1, GROUPS)):
        carry = jnp.where(k > group, far[k] * carry + far_ref[k, 0:HEAD, :], carry)
    for k in reversed(range(GROUP)):
        out_ref[k, HEAD:, :] = carry
        if k:
            carry = decay[k] * carry + in_ref[k, HEAD:2 * HEAD, :]


def outer_kernel(scale, c_ref, group_ref, in_ref, u_ref, v_ref, en_ref, te_ref, proj_ref,
                 yl_ref, gml_ref, gp_ref, gm_ref, pk_ref, yk_ref, send_ref, y_ref):
    c = c_ref[0]
    pieces = [in_ref[(group_ref[0] + h) & (GROUP - 1)] for h in range(GROUP)]
    carry = jnp.concatenate([a[:HEAD] for a in pieces], axis=0).astype(bf16)
    adjoint = jnp.concatenate([a[HEAD:] for a in pieces], axis=0).astype(bf16)
    inject = proj_ref[:, :STATE]
    readout = proj_ref[:, STATE:]
    gi = scale * (gp_ref[:, :STATE] + mm(u_ref[...], adjoint))
    gr = scale * (gp_ref[:, STATE:] + mm(v_ref[...], carry))
    pk_ref[...] = jnp.where(c == 0, gi, gr)
    send_ref[0:CHIP, :] = jnp.where(c == 0, gr, gi)
    grad = gml_ref[...] + te_ref[...] * mm_nt(inject, adjoint)
    gm_ref[...] = (scale * grad).astype(bf16)
    y_ref[...] = yl_ref[...] + en_ref[...] * mm_nt(readout, carry)
    yk_ref[...] = y_ref[pl.ds(pl.multiple_of(c * LD, LD), LD), :]
    there = y_ref[pl.ds(pl.multiple_of((1 - c) * LD, LD), LD), :]
    send_ref[CHIP:CHIP + LD, :] = there[:, :LD]
    send_ref[CHIP + LD:, :] = there[:, LD:]


def weight_kernel(c_ref, group_ref, xt_ref, gm_ref, pk_ref, recv_ref, out_ref):
    xt = xt_ref[...]
    out_ref[:, :HALF] = mm(xt, gm_ref[...])
    out_ref[:, HALF:] = mm(xt, (pk_ref[...] + recv_ref[0:CHIP, :]).astype(bf16))


def fold_kernel(c_ref, group_ref, in_ref, out_ref):
    total = jnp.sum(in_ref[...], axis=0)
    step = out_ref.shape[1]
    for k in range(ZN):
        out_ref[k] = total[k * step:(k + 1) * step, :]


def spread_kernel(scale, c_ref, group_ref, in_ref, out_ref):
    total = scale * jnp.sum(in_ref[...], axis=0)
    for k in range(2 * DP):
        half = k % 2
        out_ref[k] = total[2 * half:2 * half + 2, :]


def place_kernel(c_ref, group_ref, in_ref, yk_ref, recv_ref, x_hbm, bc_hbm, y_hbm,
                 x_ref, bc_ref, y_ref, sems):
    c = c_ref[0]
    own = pl.multiple_of(c * HALF, LD)
    oth = pl.multiple_of((1 - c) * HALF, LD)
    y_ref[:, pl.ds(own, HALF)] = yk_ref[...].astype(bf16)
    y_ref[:, pl.ds(oth, LD)] = recv_ref[CHIP:CHIP + LD, :].astype(bf16)
    y_ref[:, pl.ds(pl.multiple_of(oth + LD, LD), LD)] = recv_ref[CHIP + LD:, :].astype(bf16)
    copies = [pltpu.make_async_copy(y_ref, y_hbm, sems.at[0])]
    copies[0].start()
    for k in range(DP):
        for half in range(2):
            piece = in_ref[2 * k + half]
            x_ref[2 * k:2 * k + 2, half * HALF:(half + 1) * HALF] = piece[:, :HALF]
            bc_ref[2 * k:2 * k + 2, half * STATE:(half + 1) * STATE] = piece[:, HALF:]
    copies.append(pltpu.make_async_copy(x_ref, x_hbm, sems.at[1]))
    copies.append(pltpu.make_async_copy(bc_ref, bc_hbm, sems.at[2]))
    for copy in copies[1:]:
        copy.start()
    for copy in copies:
        copy.wait()


vmem = pl.BlockSpec(memory_space=pltpu.VMEM)
smem = pl.BlockSpec(memory_space=pltpu.SMEM)
anywhere = pl.BlockSpec(memory_space=pl.ANY)


def call(kernel, place, outs, ins, scratch=(), in_hbm=(), out_hbm=False):
    return pl.pallas_call(
        kernel,
        out_shape=[jax.ShapeDtypeStruct(s, d) for s, d in outs],
        in_specs=[smem, smem] + [anywhere if k in in_hbm else vmem for k in range(len(ins))],
        out_specs=[anywhere if out_hbm else vmem for _ in outs],
        scratch_shapes=list(scratch),
        compiler_params=pltpu.CompilerParams(vmem_limit_bytes=16 * 1024 * 1024),
    )(*place, *ins)


def body(records, x_weight, bc_weight, decay_codes, out_grad):
    x = records[0]
    g = out_grad[0]
    codes = decay_codes[0].T
    d = x.shape[1]
    frames = LD * 2 * ZN
    unit = 1.0 / (32.0 * frames)
    out_scale = float((STATE * frames) ** -0.5)
    grad_scale = float((DP * frames) ** -0.5)
    place = lax.optimization_barrier((
        lax.axis_index("c").astype(jnp.int32).reshape(1),
        lax.div(lax.axis_index("z"), GROUP).astype(jnp.int32).reshape(1)))
    swap = [(0, 1), (1, 0)]
    near = [[GROUP * a + b for b in range(GROUP)] for a in range(GROUPS)]
    across = [[GROUP * a + (a + b) % GROUP for a in range(GROUPS)] for b in range(GROUP)]

    x, g, codes, wx, wbc = (
        pltpu.with_memory_space_constraint(a, pltpu.MemorySpace.HBM)
        for a in (x, g, codes, x_weight, bc_weight))
    half = (LD, HALF)
    pack, xv, gv, cv = call(
        pack_kernel, place,
        [((LD, d + HALF + LD), f32), ((LD, d), bf16), (half, bf16), ((HEADS, LD), f32)], (x, g, codes),
        [pltpu.VMEM(half, bf16), pltpu.VMEM((HEADS, LD), jnp.int32), pltpu.SemaphoreType.DMA((4,))],
        (0, 1, 2))
    pack = lax.ppermute(pack, "c", swap)
    owned = call(
        own_kernel, place,
        [(half, bf16), ((LD, 2 * STATE), bf16), ((d, HALF), bf16), ((d, 2 * STATE), bf16)],
        (xv, wx, wbc), [pltpu.SemaphoreType.DMA((2,))], (1, 2))

    sq = (CHIP, HALF)
    pay, ue, v, en, te, proj, xc, yl, gml, gpl = call(
        lambda *refs: local_kernel(unit, *refs), place,
        [((GROUP, 2 * HEAD + 8, STATE), f32), (sq, bf16), (sq, bf16), (sq, f32), (sq, f32),
         ((CHIP, 2 * STATE), bf16), ((CHIP, d), bf16), (sq, f32), (sq, f32), ((CHIP, 2 * STATE), f32)],
        (*owned, xv, gv, cv, pack), [pltpu.VMEM(sq, f32), pltpu.VMEM((HEADS, CHIP), f32), pltpu.VMEM(sq, bf16)])

    pay = lax.all_to_all(pay, "z", 0, 0, tiled=True, axis_index_groups=near)
    (far,) = call(total_kernel, place, [((GROUPS, HEAD + 8, STATE), f32)], (pay,))
    far = lax.all_to_all(far, "z", 0, 0, tiled=True, axis_index_groups=across)
    (pay,) = call(prefix_kernel, place, [((GROUP, 2 * HEAD, STATE), f32)], (pay, far))
    pay = lax.all_to_all(pay, "z", 0, 0, tiled=True, axis_index_groups=near)

    gm, pk, yk, send = call(
        lambda *refs: outer_kernel(out_scale, *refs), place,
        [(sq, bf16), ((CHIP, STATE), f32), ((LD, HALF), f32), ((2 * CHIP, LD), f32)],
        (pay, ue, v, en, te, proj, yl, gml, gpl), [pltpu.VMEM(sq, f32)])
    recv = lax.ppermute(send, "c", swap)
    xt = xc.T.reshape(ZN, 2, DP, 2, CHIP).transpose(2, 0, 1, 3, 4).reshape(d, CHIP)
    width = HALF + STATE
    (grad,) = call(weight_kernel, place, [((d, width), f32)], (xt, gm, pk, recv))

    part = lax.all_to_all(grad.reshape(DP, d // DP, width), "dp", 0, 0, tiled=True)
    (part,) = call(fold_kernel, place, [((ZN, d // DP // ZN, width), f32)], (part,))
    part = lax.all_to_all(part, "z", 0, 0, tiled=True)
    (part,) = call(lambda *refs: spread_kernel(grad_scale, *refs), place, [((2 * DP, 2, width), f32)], (part,))
    part = lax.all_to_all(part, ("dp", "c"), 0, 0, tiled=True)
    outs = [((2 * DP, 2 * HALF), f32), ((2 * DP, 2 * STATE), f32), ((LD, 2 * HALF), bf16)]
    x_grad, bc_grad, y = call(
        place_kernel, place, outs, (part, yk, recv),
        [pltpu.VMEM(s, t) for s, t in outs] + [pltpu.SemaphoreType.DMA((3,))], (), True)
    return y[None], x_grad, bc_grad


def solution(mesh):
    mesh = Mesh(mesh.devices.reshape(DP, ZN, 2), ("dp", "z", "c"))
    frames = P("dp", ("z", "c"), None)
    rows = P(("z", "c"), None)
    return jax.shard_map(
        body,
        mesh=mesh,
        in_specs=(frames, P(), P(), frames, frames),
        out_specs=(frames, rows, rows),
        check_vma=False,
    )
```

```python
import jax
import jax.numpy as jnp
from jax import lax
from jax.experimental import pallas as pl
from jax.experimental.pallas import tpu as pltpu
from jax.sharding import Mesh, PartitionSpec as P

f32 = jnp.float32
bf16 = jnp.bfloat16

LD = 128
CHIP = 2 * LD
HEADS = 8
HEAD = 64
STATE = 128
HALF = HEADS * HEAD // 2
ZN = 16
DP = 16
GROUP = 4
GROUPS = ZN // GROUP


def mm(a, b):
    return jnp.dot(a, b, preferred_element_type=f32)


def mm_tn(a, b):
    return lax.dot_general(a, b, (((0,), (0,)), ((), ())), preferred_element_type=f32)


def mm_nt(a, b):
    return lax.dot_general(a, b, (((1,), (1,)), ((), ())), preferred_element_type=f32)


def causal(shape):
    return lax.broadcasted_iota(jnp.int32, shape, 0) >= lax.broadcasted_iota(jnp.int32, shape, 1)


def pack_kernel(c_ref, group_ref, x_ref, g_ref, codes_ref, out_ref):
    d = x_ref.shape[1]
    out_ref[:, :d] = x_ref[...].astype(f32)
    out_ref[:, d:d + HALF] = g_ref[...].astype(f32)
    out_ref[:, d + HALF:] = jnp.zeros((LD, LD), f32)
    out_ref[0:HEADS, d + HALF:] = codes_ref[...].astype(f32)


def own_kernel(c_ref, group_ref, x_ref, g_ref, codes_ref, wx_ref, wbc_ref,
               mix_ref, proj_ref, g_out_ref, codes_out_ref, x_out_ref, wx_out_ref, wbc_out_ref):
    x = x_ref[...]
    wx = wx_ref[...]
    wbc = wbc_ref[...]
    mix_ref[...] = mm(x, wx).astype(bf16)
    proj_ref[...] = mm(x, wbc).astype(bf16)
    g_out_ref[...] = g_ref[...]
    codes_out_ref[...] = codes_ref[...].astype(f32)
    x_out_ref[...] = x
    wx_out_ref[...] = wx
    wbc_out_ref[...] = wbc


def local_kernel(unit, c_ref, group_ref, mix_ref, pj_ref, g_ref, codes_ref, x_ref, wx_ref, wbc_ref, pack_ref,
                 pay_ref, ue_ref, v_ref, en_ref, te_ref, proj_ref, xc_ref, yl_ref, gm_ref, gp_ref,
                 gs_ref, cs_ref, ms_ref):
    c = c_ref[0]
    own = pl.multiple_of(c * LD, LD)
    oth = pl.multiple_of((1 - c) * LD, LD)
    d = x_ref.shape[1]
    xo = pack_ref[:, :d].astype(bf16)
    xc_ref[pl.ds(own, LD), :] = x_ref[...]
    xc_ref[pl.ds(oth, LD), :] = xo
    gs_ref[pl.ds(own, LD), :] = g_ref[...].astype(f32)
    gs_ref[pl.ds(oth, LD), :] = pack_ref[:, d:d + HALF]
    cs_ref[:, pl.ds(own, LD)] = codes_ref[...]
    cs_ref[:, pl.ds(oth, LD)] = pack_ref[0:HEADS, d + HALF:]
    ms_ref[pl.ds(own, LD), :] = mix_ref[...]
    ms_ref[pl.ds(oth, LD), :] = mm(xo, wx_ref[...]).astype(bf16)
    proj_ref[pl.ds(own, LD), :] = pj_ref[...]
    proj_ref[pl.ds(oth, LD), :] = mm(xo, wbc_ref[...]).astype(bf16)
    codes = cs_ref[...]
    hi = jnp.floor(codes * (1.0 / 32.0))
    lo = codes - 32.0 * hi
    row = lax.broadcasted_iota(jnp.int32, (HEADS, HALF), 0)
    col = lax.broadcasted_iota(jnp.int32, (HEADS, HALF), 1)
    spread = jnp.where(row == col // HEAD + c * (HEADS // 2), 1.0, 0.0).astype(bf16)
    hi = mm_tn(hi.astype(bf16), spread).astype(bf16)
    lo = mm_tn(lo.astype(bf16), spread).astype(bf16)
    mask = causal((CHIP, CHIP))
    tri = jnp.where(mask, 1.0, 0.0).astype(bf16)
    running = unit * (32.0 * mm(tri, hi) + mm(tri, lo))
    last = running[CHIP - 1:CHIP, :]
    en = jnp.exp(-running)
    ep = jnp.exp(running)
    te = jnp.exp(running - last)
    en_ref[...] = en
    te_ref[...] = te
    mixer = ms_ref[...].astype(f32)
    inject = proj_ref[:, :STATE]
    readout = proj_ref[:, STATE:]
    v = (en * gs_ref[...]).astype(bf16)
    ue = (te * mixer).astype(bf16)
    u = (ep * mixer).astype(bf16)
    ue_ref[...] = ue
    v_ref[...] = v
    state = mm_tn(ue, inject)
    adjoint = mm_tn(v, readout)
    for h in range(GROUP):
        at = (group_ref[0] + h) & (GROUP - 1)
        pay_ref[at, 0:HEAD, :] = state[h * HEAD:(h + 1) * HEAD, :]
        pay_ref[at, HEAD:2 * HEAD, :] = adjoint[h * HEAD:(h + 1) * HEAD, :]
        pay_ref[at, 2 * HEAD:, :] = jnp.broadcast_to(last[:, h * HEAD:h * HEAD + 1], (8, STATE))
    scores = jnp.where(mask, mm_nt(readout, inject), 0.0).astype(bf16)
    pairs = jnp.where(mask, mm_nt(v, u), 0.0).astype(bf16)
    yl_ref[...] = en * mm(scores, u)
    gm_ref[...] = ep * mm_tn(scores, v)
    gp_ref[:, :STATE] = mm_tn(pairs, readout)
    gp_ref[:, STATE:] = mm(pairs, inject)


def total_kernel(c_ref, group_ref, in_ref, out_ref):
    group = group_ref[0]
    logs = [in_ref[k, 2 * HEAD:, :] for k in range(GROUP)]
    decay = [jnp.exp(-a[0:1, :]) for a in logs]
    state = in_ref[0, 0:HEAD, :]
    for k in range(1, GROUP):
        state = decay[k] * state + in_ref[k, 0:HEAD, :]
    adjoint = in_ref[GROUP - 1, HEAD:2 * HEAD, :]
    for k in reversed(range(GROUP - 1)):
        adjoint = decay[k] * adjoint + in_ref[k, HEAD:2 * HEAD, :]
    total = logs[0] + logs[1] + logs[2] + logs[3]
    for k in range(GROUPS):
        out_ref[k, 0:HEAD, :] = jnp.where(k > group, state, adjoint)
        out_ref[k, HEAD:, :] = total


def prefix_kernel(c_ref, group_ref, in_ref, far_ref, out_ref):
    group = group_ref[0]
    far = [jnp.exp(-far_ref[k, HEAD:HEAD + 1, :]) for k in range(GROUPS)]
    decay = [jnp.exp(-in_ref[k, 2 * HEAD:2 * HEAD + 1, :]) for k in range(GROUP)]
    carry = jnp.zeros((HEAD, STATE), f32)
    for k in range(GROUPS - 1):
        carry = jnp.where(k < group, far[k] * carry + far_ref[k, 0:HEAD, :], carry)
    for k in range(GROUP):
        out_ref[k, 0:HEAD, :] = carry
        if k + 1 < GROUP:
            carry = decay[k] * carry + in_ref[k, 0:HEAD, :]
    carry = jnp.zeros((HEAD, STATE), f32)
    for k in reversed(range(1, GROUPS)):
        carry = jnp.where(k > group, far[k] * carry + far_ref[k, 0:HEAD, :], carry)
    for k in reversed(range(GROUP)):
        out_ref[k, HEAD:, :] = carry
        if k:
            carry = decay[k] * carry + in_ref[k, HEAD:2 * HEAD, :]


def outer_kernel(scale, c_ref, group_ref, in_ref, u_ref, v_ref, en_ref, te_ref, proj_ref,
                 yl_ref, gml_ref, gp_ref, gm_ref, pk_ref, yk_ref, send_ref, y_ref):
    c = c_ref[0]
    pieces = [in_ref[(group_ref[0] + h) & (GROUP - 1)] for h in range(GROUP)]
    carry = jnp.concatenate([a[:HEAD] for a in pieces], axis=0).astype(bf16)
    adjoint = jnp.concatenate([a[HEAD:] for a in pieces], axis=0).astype(bf16)
    inject = proj_ref[:, :STATE]
    readout = proj_ref[:, STATE:]
    gi = scale * (gp_ref[:, :STATE] + mm(u_ref[...], adjoint))
    gr = scale * (gp_ref[:, STATE:] + mm(v_ref[...], carry))
    pk_ref[...] = jnp.where(c == 0, gi, gr)
    send_ref[0:CHIP, :] = jnp.where(c == 0, gr, gi)
    grad = gml_ref[...] + te_ref[...] * mm_nt(inject, adjoint)
    gm_ref[...] = (scale * grad).astype(bf16)
    y_ref[...] = yl_ref[...] + en_ref[...] * mm_nt(readout, carry)
    yk_ref[...] = y_ref[pl.ds(pl.multiple_of(c * LD, LD), LD), :]
    there = y_ref[pl.ds(pl.multiple_of((1 - c) * LD, LD), LD), :]
    send_ref[CHIP:CHIP + LD, :] = there[:, :LD]
    send_ref[CHIP + LD:, :] = there[:, LD:]


def weight_kernel(c_ref, group_ref, xt_ref, gm_ref, pk_ref, recv_ref, out_ref):
    xt = xt_ref[...]
    out_ref[:, :HALF] = mm(xt, gm_ref[...])
    out_ref[:, HALF:] = mm(xt, (pk_ref[...] + recv_ref[...]).astype(bf16))


def fold_kernel(c_ref, group_ref, in_ref, out_ref):
    width = in_ref.shape[2]
    step = out_ref.shape[1]
    for half in range(2):
        total = in_ref[half]
        for k in range(1, DP):
            total = total + in_ref[2 * k + half]
        for k in range(ZN):
            out_ref[k, :, half * width:(half + 1) * width] = total[k * step:(k + 1) * step, :]


def spread_kernel(scale, c_ref, group_ref, in_ref, out_ref):
    total = scale * jnp.sum(in_ref[...], axis=0)
    for k in range(DP):
        out_ref[k] = total


def place_kernel(c_ref, group_ref, in_ref, yk_ref, recv_ref, x_ref, bc_ref, y_ref):
    width = HALF + STATE
    for k in range(DP):
        piece = in_ref[k]
        for half in range(2):
            at = half * width
            x_ref[2 * k:2 * k + 2, half * HALF:(half + 1) * HALF] = piece[:, at:at + HALF]
            bc_ref[2 * k:2 * k + 2, half * STATE:(half + 1) * STATE] = piece[:, at + HALF:at + width]
    c = c_ref[0]
    own = pl.multiple_of(c * HALF, LD)
    oth = pl.multiple_of((1 - c) * HALF, LD)
    y_ref[:, pl.ds(own, HALF)] = yk_ref[...].astype(bf16)
    y_ref[:, pl.ds(oth, LD)] = recv_ref[0:LD, :].astype(bf16)
    y_ref[:, pl.ds(pl.multiple_of(oth + LD, LD), LD)] = recv_ref[LD:, :].astype(bf16)


def whole(shape):
    return pl.BlockSpec(shape, lambda i, c, g: (0,) * len(shape))


def call(kernel, place, outs, ins, scratch=(), specs=None):
    return pl.pallas_call(
        kernel,
        out_shape=[jax.ShapeDtypeStruct(s, d) for s, d in outs],
        grid_spec=pltpu.PrefetchScalarGridSpec(
            num_scalar_prefetch=2, grid=(1,), in_specs=specs or [whole(a.shape) for a in ins],
            out_specs=[whole(s) for s, _ in outs], scratch_shapes=list(scratch)),
        compiler_params=pltpu.CompilerParams(vmem_limit_bytes=16 * 1024 * 1024),
    )(*place, *ins)


def body(records, x_weight, bc_weight, decay_codes, out_grad):
    x = records[0]
    g = out_grad[0]
    codes = decay_codes[0].T
    d = x.shape[1]
    frames = LD * 2 * ZN
    unit = 1.0 / (32.0 * frames)
    out_scale = float((STATE * frames) ** -0.5)
    grad_scale = float((DP * frames) ** -0.5)
    place = lax.optimization_barrier((
        lax.axis_index("c").astype(jnp.int32).reshape(1),
        lax.div(lax.axis_index("z"), GROUP).astype(jnp.int32).reshape(1)))
    swap = [(0, 1), (1, 0)]
    near = [[GROUP * a + b for b in range(GROUP)] for a in range(GROUPS)]
    across = [[GROUP * a + (a + b) % GROUP for a in range(GROUPS)] for b in range(GROUP)]

    here = pl.BlockSpec((LD, HALF), lambda i, c, g: (0, c[0]))
    there = pl.BlockSpec((LD, HALF), lambda i, c, g: (0, 1 - c[0]))
    x, g, codes, wx, wbc = (
        pltpu.with_memory_space_constraint(a, pltpu.MemorySpace.HBM)
        for a in (x, g, codes, x_weight, bc_weight))
    (pack,) = call(
        pack_kernel, place, [((LD, d + HALF + LD), f32)], (x, g, codes), (),
        [whole(x.shape), there, whole(codes.shape)])
    pack = lax.ppermute(pack, "c", swap)
    half = (LD, HALF)
    owned = call(
        own_kernel, place,
        [(half, bf16), ((LD, 2 * STATE), bf16), (half, bf16), ((HEADS, LD), f32), ((LD, d), bf16),
         ((d, HALF), bf16), ((d, 2 * STATE), bf16)],
        (x, g, codes, wx, wbc), (),
        [whole(x.shape), here, whole(codes.shape), pl.BlockSpec((d, HALF), lambda i, c, g: (0, c[0])),
         whole(wbc.shape)])

    sq = (CHIP, HALF)
    pay, ue, v, en, te, proj, xc, yl, gml, gpl = call(
        lambda *refs: local_kernel(unit, *refs), place,
        [((GROUP, 2 * HEAD + 8, STATE), f32), (sq, bf16), (sq, bf16), (sq, f32), (sq, f32),
         ((CHIP, 2 * STATE), bf16), ((CHIP, d), bf16), (sq, f32), (sq, f32), ((CHIP, 2 * STATE), f32)],
        (*owned, pack), [pltpu.VMEM(sq, f32), pltpu.VMEM((HEADS, CHIP), f32), pltpu.VMEM(sq, bf16)])

    pay = lax.all_to_all(pay, "z", 0, 0, tiled=True, axis_index_groups=near)
    (far,) = call(total_kernel, place, [((GROUPS, HEAD + 8, STATE), f32)], (pay,))
    far = lax.all_to_all(far, "z", 0, 0, tiled=True, axis_index_groups=across)
    (pay,) = call(prefix_kernel, place, [((GROUP, 2 * HEAD, STATE), f32)], (pay, far))
    pay = lax.all_to_all(pay, "z", 0, 0, tiled=True, axis_index_groups=near)

    gm, pk, yk, send = call(
        lambda *refs: outer_kernel(out_scale, *refs), place,
        [(sq, bf16), ((CHIP, STATE), f32), ((LD, HALF), f32), ((2 * CHIP, LD), f32)],
        (pay, ue, v, en, te, proj, yl, gml, gpl), [pltpu.VMEM(sq, f32)])
    recv = lax.ppermute(send, "c", swap)
    xt = xc.T.reshape(ZN, 2, DP, 2, CHIP).transpose(2, 1, 0, 3, 4).reshape(d, CHIP)
    width = HALF + STATE
    top = pl.BlockSpec((CHIP, LD), lambda i, c, g: (0, 0))
    low = pl.BlockSpec((CHIP, LD), lambda i, c, g: (1, 0))
    (grad,) = call(
        weight_kernel, place, [((d, width), f32)], (xt, gm, pk, recv), (),
        [whole(xt.shape), whole(gm.shape), whole(pk.shape), top])

    rows = d // DP // 2
    part = lax.all_to_all(grad.reshape(2 * DP, rows, width), ("dp", "c"), 0, 0, tiled=True)
    (part,) = call(fold_kernel, place, [((ZN, rows // ZN, 2 * width), f32)], (part,))
    part = lax.all_to_all(part, "z", 0, 0, tiled=True)
    (part,) = call(lambda *refs: spread_kernel(grad_scale, *refs), place, [((DP, rows // ZN, 2 * width), f32)], (part,))
    part = lax.all_to_all(part, "dp", 0, 0, tiled=True)
    x_grad, bc_grad, y = call(
        place_kernel, place,
        [((2 * DP, 2 * HALF), f32), ((2 * DP, 2 * STATE), f32), ((LD, 2 * HALF), bf16)], (part, yk, recv), (),
        [whole(part.shape), whole(yk.shape), low])
    return y[None], x_grad, bc_grad


def solution(mesh):
    mesh = Mesh(mesh.devices.reshape(DP, ZN, 2), ("dp", "z", "c"))
    frames = P("dp", ("z", "c"), None)
    rows = P(("z", "c"), None)
    return jax.shard_map(
        body,
        mesh=mesh,
        in_specs=(frames, P(), P(), frames, frames),
        out_specs=(frames, rows, rows),
        check_vma=False,
    )
```

```python
import jax
import jax.numpy as jnp
from jax import lax
from jax.experimental import pallas as pl
from jax.experimental.pallas import tpu as pltpu
from jax.sharding import Mesh, PartitionSpec as P

f32 = jnp.float32
bf16 = jnp.bfloat16

LD = 128
CHIP = 2 * LD
HEADS = 8
HEAD = 64
STATE = 128
HALF = HEADS * HEAD // 2
ZN = 16
DP = 16
GROUP = 4
GROUPS = ZN // GROUP


def mm(a, b):
    return jnp.dot(a, b, preferred_element_type=f32)


def mm_tn(a, b):
    return lax.dot_general(a, b, (((0,), (0,)), ((), ())), preferred_element_type=f32)


def mm_nt(a, b):
    return lax.dot_general(a, b, (((1,), (1,)), ((), ())), preferred_element_type=f32)


def causal(shape):
    return lax.broadcasted_iota(jnp.int32, shape, 0) >= lax.broadcasted_iota(jnp.int32, shape, 1)


def pack_kernel(c_ref, group_ref, x_ref, g_ref, codes_ref, out_ref):
    d = x_ref.shape[1]
    out_ref[:, :d] = x_ref[...].astype(f32)
    out_ref[:, d:d + HALF] = g_ref[...].astype(f32)
    out_ref[:, d + HALF:] = jnp.zeros((LD, LD), f32)
    out_ref[0:HEADS, d + HALF:] = codes_ref[...].astype(f32)


def own_kernel(c_ref, group_ref, x_ref, g_ref, codes_ref, wx_ref, wbc_ref,
               mix_ref, proj_ref, g_out_ref, codes_out_ref, x_out_ref, wx_out_ref, wbc_out_ref):
    x = x_ref[...]
    wx = wx_ref[...]
    wbc = wbc_ref[...]
    mix_ref[...] = mm(x, wx).astype(bf16)
    proj_ref[...] = mm(x, wbc).astype(bf16)
    g_out_ref[...] = g_ref[...]
    codes_out_ref[...] = codes_ref[...].astype(f32)
    x_out_ref[...] = x
    wx_out_ref[...] = wx
    wbc_out_ref[...] = wbc


def local_kernel(unit, c_ref, group_ref, mix_ref, pj_ref, g_ref, codes_ref, x_ref, wx_ref, wbc_ref, pack_ref,
                 pay_ref, ue_ref, v_ref, en_ref, te_ref, proj_ref, xc_ref, yl_ref, gm_ref, gp_ref,
                 gs_ref, cs_ref, ms_ref):
    c = c_ref[0]
    own = pl.multiple_of(c * LD, LD)
    oth = pl.multiple_of((1 - c) * LD, LD)
    d = x_ref.shape[1]
    xo = pack_ref[:, :d].astype(bf16)
    xc_ref[pl.ds(own, LD), :] = x_ref[...]
    xc_ref[pl.ds(oth, LD), :] = xo
    gs_ref[pl.ds(own, LD), :] = g_ref[...].astype(f32)
    gs_ref[pl.ds(oth, LD), :] = pack_ref[:, d:d + HALF]
    cs_ref[:, pl.ds(own, LD)] = codes_ref[...]
    cs_ref[:, pl.ds(oth, LD)] = pack_ref[0:HEADS, d + HALF:]
    ms_ref[pl.ds(own, LD), :] = mix_ref[...]
    ms_ref[pl.ds(oth, LD), :] = mm(xo, wx_ref[...]).astype(bf16)
    proj_ref[pl.ds(own, LD), :] = pj_ref[...]
    proj_ref[pl.ds(oth, LD), :] = mm(xo, wbc_ref[...]).astype(bf16)
    codes = cs_ref[...]
    hi = jnp.floor(codes * (1.0 / 32.0))
    lo = codes - 32.0 * hi
    row = lax.broadcasted_iota(jnp.int32, (HEADS, HALF), 0)
    col = lax.broadcasted_iota(jnp.int32, (HEADS, HALF), 1)
    spread = jnp.where(row == col // HEAD + c * (HEADS // 2), 1.0, 0.0).astype(bf16)
    hi = mm_tn(hi.astype(bf16), spread).astype(bf16)
    lo = mm_tn(lo.astype(bf16), spread).astype(bf16)
    mask = causal((CHIP, CHIP))
    tri = jnp.where(mask, 1.0, 0.0).astype(bf16)
    running = unit * (32.0 * mm(tri, hi) + mm(tri, lo))
    last = running[CHIP - 1:CHIP, :]
    en = jnp.exp(-running)
    ep = jnp.exp(running)
    te = jnp.exp(running - last)
    en_ref[...] = en
    te_ref[...] = te
    mixer = ms_ref[...].astype(f32)
    inject = proj_ref[:, :STATE]
    readout = proj_ref[:, STATE:]
    v = (en * gs_ref[...]).astype(bf16)
    ue = (te * mixer).astype(bf16)
    u = (ep * mixer).astype(bf16)
    ue_ref[...] = ue
    v_ref[...] = v
    state = mm_tn(ue, inject)
    adjoint = mm_tn(v, readout)
    for h in range(GROUP):
        at = (group_ref[0] + h) & (GROUP - 1)
        pay_ref[at, 0:HEAD, :] = state[h * HEAD:(h + 1) * HEAD, :]
        pay_ref[at, HEAD:2 * HEAD, :] = adjoint[h * HEAD:(h + 1) * HEAD, :]
        pay_ref[at, 2 * HEAD:, :] = jnp.broadcast_to(last[:, h * HEAD:h * HEAD + 1], (8, STATE))
    scores = jnp.where(mask, mm_nt(readout, inject), 0.0).astype(bf16)
    pairs = jnp.where(mask, mm_nt(v, u), 0.0).astype(bf16)
    yl_ref[...] = en * mm(scores, u)
    gm_ref[...] = ep * mm_tn(scores, v)
    gp_ref[:, :STATE] = mm_tn(pairs, readout)
    gp_ref[:, STATE:] = mm(pairs, inject)


def total_kernel(c_ref, group_ref, in_ref, out_ref):
    group = group_ref[0]
    logs = [in_ref[k, 2 * HEAD:, :] for k in range(GROUP)]
    decay = [jnp.exp(-a[0:1, :]) for a in logs]
    state = in_ref[0, 0:HEAD, :]
    for k in range(1, GROUP):
        state = decay[k] * state + in_ref[k, 0:HEAD, :]
    adjoint = in_ref[GROUP - 1, HEAD:2 * HEAD, :]
    for k in reversed(range(GROUP - 1)):
        adjoint = decay[k] * adjoint + in_ref[k, HEAD:2 * HEAD, :]
    total = logs[0] + logs[1] + logs[2] + logs[3]
    for k in range(GROUPS):
        out_ref[k, 0:HEAD, :] = jnp.where(k > group, state, adjoint)
        out_ref[k, HEAD:, :] = total


def prefix_kernel(c_ref, group_ref, in_ref, far_ref, out_ref):
    group = group_ref[0]
    far = [jnp.exp(-far_ref[k, HEAD:HEAD + 1, :]) for k in range(GROUPS)]
    decay = [jnp.exp(-in_ref[k, 2 * HEAD:2 * HEAD + 1, :]) for k in range(GROUP)]
    carry = jnp.zeros((HEAD, STATE), f32)
    for k in range(GROUPS - 1):
        carry = jnp.where(k < group, far[k] * carry + far_ref[k, 0:HEAD, :], carry)
    for k in range(GROUP):
        out_ref[k, 0:HEAD, :] = carry
        if k + 1 < GROUP:
            carry = decay[k] * carry + in_ref[k, 0:HEAD, :]
    carry = jnp.zeros((HEAD, STATE), f32)
    for k in reversed(range(1, GROUPS)):
        carry = jnp.where(k > group, far[k] * carry + far_ref[k, 0:HEAD, :], carry)
    for k in reversed(range(GROUP)):
        out_ref[k, HEAD:, :] = carry
        if k:
            carry = decay[k] * carry + in_ref[k, HEAD:2 * HEAD, :]


def outer_kernel(scale, c_ref, group_ref, in_ref, u_ref, v_ref, en_ref, te_ref, proj_ref,
                 yl_ref, gml_ref, gp_ref, gm_ref, pk_ref, yk_ref, send_ref, y_ref):
    c = c_ref[0]
    pieces = [in_ref[(group_ref[0] + h) & (GROUP - 1)] for h in range(GROUP)]
    carry = jnp.concatenate([a[:HEAD] for a in pieces], axis=0).astype(bf16)
    adjoint = jnp.concatenate([a[HEAD:] for a in pieces], axis=0).astype(bf16)
    inject = proj_ref[:, :STATE]
    readout = proj_ref[:, STATE:]
    gi = scale * (gp_ref[:, :STATE] + mm(u_ref[...], adjoint))
    gr = scale * (gp_ref[:, STATE:] + mm(v_ref[...], carry))
    pk_ref[...] = jnp.where(c == 0, gi, gr)
    send_ref[0:CHIP, :] = jnp.where(c == 0, gr, gi)
    grad = gml_ref[...] + te_ref[...] * mm_nt(inject, adjoint)
    gm_ref[...] = (scale * grad).astype(bf16)
    y_ref[...] = yl_ref[...] + en_ref[...] * mm_nt(readout, carry)
    yk_ref[...] = y_ref[pl.ds(pl.multiple_of(c * LD, LD), LD), :]
    there = y_ref[pl.ds(pl.multiple_of((1 - c) * LD, LD), LD), :]
    send_ref[CHIP:CHIP + LD, :] = there[:, :LD]
    send_ref[CHIP + LD:, :] = there[:, LD:]


def weight_kernel(c_ref, group_ref, xt_ref, gm_ref, pk_ref, recv_ref, out_ref):
    xt = xt_ref[...]
    out_ref[:, :HALF] = mm(xt, gm_ref[...])
    out_ref[:, HALF:] = mm(xt, (pk_ref[...] + recv_ref[...]).astype(bf16))


def fold_kernel(c_ref, group_ref, in_ref, out_ref):
    total = jnp.sum(in_ref[...], axis=0)
    step = out_ref.shape[1]
    for k in range(2 * ZN):
        out_ref[k] = total[k * step:(k + 1) * step, :]


def spread_kernel(scale, c_ref, group_ref, in_ref, out_ref):
    width = in_ref.shape[2]
    for half in range(2):
        total = in_ref[half]
        for k in range(1, ZN):
            total = total + in_ref[2 * k + half]
        total = scale * total
        for k in range(DP):
            out_ref[k, :, half * width:(half + 1) * width] = total


def place_kernel(c_ref, group_ref, in_ref, yk_ref, recv_ref, x_ref, bc_ref, y_ref):
    width = HALF + STATE
    for k in range(DP):
        piece = in_ref[k]
        for half in range(2):
            at = half * width
            x_ref[2 * k:2 * k + 2, half * HALF:(half + 1) * HALF] = piece[:, at:at + HALF]
            bc_ref[2 * k:2 * k + 2, half * STATE:(half + 1) * STATE] = piece[:, at + HALF:at + width]
    c = c_ref[0]
    own = pl.multiple_of(c * HALF, LD)
    oth = pl.multiple_of((1 - c) * HALF, LD)
    y_ref[:, pl.ds(own, HALF)] = yk_ref[...].astype(bf16)
    y_ref[:, pl.ds(oth, LD)] = recv_ref[0:LD, :].astype(bf16)
    y_ref[:, pl.ds(pl.multiple_of(oth + LD, LD), LD)] = recv_ref[LD:, :].astype(bf16)


def whole(shape):
    return pl.BlockSpec(shape, lambda i, c, g: (0,) * len(shape))


def call(kernel, place, outs, ins, scratch=(), specs=None):
    return pl.pallas_call(
        kernel,
        out_shape=[jax.ShapeDtypeStruct(s, d) for s, d in outs],
        grid_spec=pltpu.PrefetchScalarGridSpec(
            num_scalar_prefetch=2, grid=(1,), in_specs=specs or [whole(a.shape) for a in ins],
            out_specs=[whole(s) for s, _ in outs], scratch_shapes=list(scratch)),
        compiler_params=pltpu.CompilerParams(vmem_limit_bytes=16 * 1024 * 1024),
    )(*place, *ins)


def body(records, x_weight, bc_weight, decay_codes, out_grad):
    x = records[0]
    g = out_grad[0]
    codes = decay_codes[0].T
    d = x.shape[1]
    frames = LD * 2 * ZN
    unit = 1.0 / (32.0 * frames)
    out_scale = float((STATE * frames) ** -0.5)
    grad_scale = float((DP * frames) ** -0.5)
    place = lax.optimization_barrier((
        lax.axis_index("c").astype(jnp.int32).reshape(1),
        lax.div(lax.axis_index("z"), GROUP).astype(jnp.int32).reshape(1)))
    swap = [(0, 1), (1, 0)]
    near = [[GROUP * a + b for b in range(GROUP)] for a in range(GROUPS)]
    across = [[GROUP * a + (a + b) % GROUP for a in range(GROUPS)] for b in range(GROUP)]

    here = pl.BlockSpec((LD, HALF), lambda i, c, g: (0, c[0]))
    there = pl.BlockSpec((LD, HALF), lambda i, c, g: (0, 1 - c[0]))
    x, g, codes, wx, wbc = (
        pltpu.with_memory_space_constraint(a, pltpu.MemorySpace.HBM)
        for a in (x, g, codes, x_weight, bc_weight))
    (pack,) = call(
        pack_kernel, place, [((LD, d + HALF + LD), f32)], (x, g, codes), (),
        [whole(x.shape), there, whole(codes.shape)])
    pack = lax.ppermute(pack, "c", swap)
    half = (LD, HALF)
    owned = call(
        own_kernel, place,
        [(half, bf16), ((LD, 2 * STATE), bf16), (half, bf16), ((HEADS, LD), f32), ((LD, d), bf16),
         ((d, HALF), bf16), ((d, 2 * STATE), bf16)],
        (x, g, codes, wx, wbc), (),
        [whole(x.shape), here, whole(codes.shape), pl.BlockSpec((d, HALF), lambda i, c, g: (0, c[0])),
         whole(wbc.shape)])

    sq = (CHIP, HALF)
    pay, ue, v, en, te, proj, xc, yl, gml, gpl = call(
        lambda *refs: local_kernel(unit, *refs), place,
        [((GROUP, 2 * HEAD + 8, STATE), f32), (sq, bf16), (sq, bf16), (sq, f32), (sq, f32),
         ((CHIP, 2 * STATE), bf16), ((CHIP, d), bf16), (sq, f32), (sq, f32), ((CHIP, 2 * STATE), f32)],
        (*owned, pack), [pltpu.VMEM(sq, f32), pltpu.VMEM((HEADS, CHIP), f32), pltpu.VMEM(sq, bf16)])

    pay = lax.all_to_all(pay, "z", 0, 0, tiled=True, axis_index_groups=near)
    (far,) = call(total_kernel, place, [((GROUPS, HEAD + 8, STATE), f32)], (pay,))
    far = lax.all_to_all(far, "z", 0, 0, tiled=True, axis_index_groups=across)
    (pay,) = call(prefix_kernel, place, [((GROUP, 2 * HEAD, STATE), f32)], (pay, far))
    pay = lax.all_to_all(pay, "z", 0, 0, tiled=True, axis_index_groups=near)

    gm, pk, yk, send = call(
        lambda *refs: outer_kernel(out_scale, *refs), place,
        [(sq, bf16), ((CHIP, STATE), f32), ((LD, HALF), f32), ((2 * CHIP, LD), f32)],
        (pay, ue, v, en, te, proj, yl, gml, gpl), [pltpu.VMEM(sq, f32)])
    recv = lax.ppermute(send, "c", swap)
    xt = xc.T.reshape(ZN, 2, DP, 2, CHIP).transpose(2, 0, 1, 3, 4).reshape(d, CHIP)
    width = HALF + STATE
    top = pl.BlockSpec((CHIP, LD), lambda i, c, g: (0, 0))
    low = pl.BlockSpec((CHIP, LD), lambda i, c, g: (1, 0))
    (grad,) = call(
        weight_kernel, place, [((d, width), f32)], (xt, gm, pk, recv), (),
        [whole(xt.shape), whole(gm.shape), whole(pk.shape), top])

    rows = d // DP
    step = rows // ZN // 2
    part = lax.all_to_all(grad.reshape(DP, rows, width), "dp", 0, 0, tiled=True)
    (part,) = call(fold_kernel, place, [((2 * ZN, step, width), f32)], (part,))
    part = lax.all_to_all(part, ("z", "c"), 0, 0, tiled=True)
    (part,) = call(lambda *refs: spread_kernel(grad_scale, *refs), place, [((DP, step, 2 * width), f32)], (part,))
    part = lax.all_to_all(part, "dp", 0, 0, tiled=True)
    x_grad, bc_grad, y = call(
        place_kernel, place,
        [((2 * DP, 2 * HALF), f32), ((2 * DP, 2 * STATE), f32), ((LD, 2 * HALF), bf16)], (part, yk, recv), (),
        [whole(part.shape), whole(yk.shape), low])
    return y[None], x_grad, bc_grad


def solution(mesh):
    mesh = Mesh(mesh.devices.reshape(DP, ZN, 2), ("dp", "z", "c"))
    frames = P("dp", ("z", "c"), None)
    rows = P(("z", "c"), None)
    return jax.shard_map(
        body,
        mesh=mesh,
        in_specs=(frames, P(), P(), frames, frames),
        out_specs=(frames, rows, rows),
        check_vma=False,
    )
```

```python
import jax
import jax.numpy as jnp
from jax import lax
from jax.experimental import pallas as pl
from jax.experimental.pallas import tpu as pltpu
from jax.sharding import Mesh, PartitionSpec as P

f32 = jnp.float32
bf16 = jnp.bfloat16

LD = 128
CHIP = 2 * LD
HEADS = 8
HEAD = 64
STATE = 128
HALF = HEADS * HEAD // 2
ZN = 16
DP = 16
GROUP = 4
GROUPS = ZN // GROUP


def mm(a, b):
    return jnp.dot(a, b, preferred_element_type=f32)


def mm_tn(a, b):
    return lax.dot_general(a, b, (((0,), (0,)), ((), ())), preferred_element_type=f32)


def mm_nt(a, b):
    return lax.dot_general(a, b, (((1,), (1,)), ((), ())), preferred_element_type=f32)


def causal(shape):
    return lax.broadcasted_iota(jnp.int32, shape, 0) >= lax.broadcasted_iota(jnp.int32, shape, 1)


def pack_kernel(c_ref, group_ref, x_ref, g_ref, codes_ref, out_ref):
    d = x_ref.shape[1]
    out_ref[:, :d] = x_ref[...].astype(f32)
    out_ref[:, d:d + HALF] = g_ref[...].astype(f32)
    out_ref[:, d + HALF:] = jnp.zeros((LD, LD), f32)
    out_ref[0:HEADS, d + HALF:] = codes_ref[...].astype(f32)


def own_kernel(c_ref, group_ref, x_ref, g_ref, codes_ref, wx_ref, wbc_ref,
               mix_ref, proj_ref, g_out_ref, codes_out_ref, x_out_ref, wx_out_ref, wbc_out_ref):
    x = x_ref[...]
    wx = wx_ref[...]
    wbc = wbc_ref[...]
    mix_ref[...] = mm(x, wx).astype(bf16)
    proj_ref[...] = mm(x, wbc).astype(bf16)
    g_out_ref[...] = g_ref[...]
    codes_out_ref[...] = codes_ref[...].astype(f32)
    x_out_ref[...] = x
    wx_out_ref[...] = wx
    wbc_out_ref[...] = wbc


def local_kernel(unit, c_ref, group_ref, mix_ref, pj_ref, g_ref, codes_ref, x_ref, wx_ref, wbc_ref, pack_ref,
                 pay_ref, ue_ref, v_ref, en_ref, te_ref, proj_ref, xc_ref, yl_ref, gm_ref, gp_ref,
                 gs_ref, cs_ref, ms_ref):
    c = c_ref[0]
    own = pl.multiple_of(c * LD, LD)
    oth = pl.multiple_of((1 - c) * LD, LD)
    d = x_ref.shape[1]
    xo = pack_ref[:, :d].astype(bf16)
    xc_ref[pl.ds(own, LD), :] = x_ref[...]
    xc_ref[pl.ds(oth, LD), :] = xo
    gs_ref[pl.ds(own, LD), :] = g_ref[...].astype(f32)
    gs_ref[pl.ds(oth, LD), :] = pack_ref[:, d:d + HALF]
    cs_ref[:, pl.ds(own, LD)] = codes_ref[...]
    cs_ref[:, pl.ds(oth, LD)] = pack_ref[0:HEADS, d + HALF:]
    ms_ref[pl.ds(own, LD), :] = mix_ref[...]
    ms_ref[pl.ds(oth, LD), :] = mm(xo, wx_ref[...]).astype(bf16)
    proj_ref[pl.ds(own, LD), :] = pj_ref[...]
    proj_ref[pl.ds(oth, LD), :] = mm(xo, wbc_ref[...]).astype(bf16)
    codes = cs_ref[...]
    hi = jnp.floor(codes * (1.0 / 32.0))
    lo = codes - 32.0 * hi
    row = lax.broadcasted_iota(jnp.int32, (HEADS, HALF), 0)
    col = lax.broadcasted_iota(jnp.int32, (HEADS, HALF), 1)
    spread = jnp.where(row == col // HEAD + c * (HEADS // 2), 1.0, 0.0).astype(bf16)
    hi = mm_tn(hi.astype(bf16), spread).astype(bf16)
    lo = mm_tn(lo.astype(bf16), spread).astype(bf16)
    mask = causal((CHIP, CHIP))
    tri = jnp.where(mask, 1.0, 0.0).astype(bf16)
    running = unit * (32.0 * mm(tri, hi) + mm(tri, lo))
    last = running[CHIP - 1:CHIP, :]
    en = jnp.exp(-running)
    ep = jnp.exp(running)
    te = jnp.exp(running - last)
    en_ref[...] = en
    te_ref[...] = te
    mixer = ms_ref[...].astype(f32)
    inject = proj_ref[:, :STATE]
    readout = proj_ref[:, STATE:]
    v = (en * gs_ref[...]).astype(bf16)
    ue = (te * mixer).astype(bf16)
    u = (ep * mixer).astype(bf16)
    ue_ref[...] = ue
    v_ref[...] = v
    state = mm_tn(ue, inject)
    adjoint = mm_tn(v, readout)
    for h in range(GROUP):
        at = (group_ref[0] + h) & (GROUP - 1)
        pay_ref[at, 0:HEAD, :] = state[h * HEAD:(h + 1) * HEAD, :]
        pay_ref[at, HEAD:2 * HEAD, :] = adjoint[h * HEAD:(h + 1) * HEAD, :]
        pay_ref[at, 2 * HEAD:, :] = jnp.broadcast_to(last[:, h * HEAD:h * HEAD + 1], (8, STATE))
    scores = jnp.where(mask, mm_nt(readout, inject), 0.0).astype(bf16)
    pairs = jnp.where(mask, mm_nt(v, u), 0.0).astype(bf16)
    yl_ref[...] = en * mm(scores, u)
    gm_ref[...] = ep * mm_tn(scores, v)
    gp_ref[:, :STATE] = mm_tn(pairs, readout)
    gp_ref[:, STATE:] = mm(pairs, inject)


def total_kernel(c_ref, group_ref, in_ref, out_ref):
    group = group_ref[0]
    logs = [in_ref[k, 2 * HEAD:, :] for k in range(GROUP)]
    decay = [jnp.exp(-a[0:1, :]) for a in logs]
    state = in_ref[0, 0:HEAD, :]
    for k in range(1, GROUP):
        state = decay[k] * state + in_ref[k, 0:HEAD, :]
    adjoint = in_ref[GROUP - 1, HEAD:2 * HEAD, :]
    for k in reversed(range(GROUP - 1)):
        adjoint = decay[k] * adjoint + in_ref[k, HEAD:2 * HEAD, :]
    total = logs[0] + logs[1] + logs[2] + logs[3]
    for k in range(GROUPS):
        out_ref[k, 0:HEAD, :] = jnp.where(k > group, state, adjoint)
        out_ref[k, HEAD:, :] = total


def prefix_kernel(c_ref, group_ref, in_ref, far_ref, out_ref):
    group = group_ref[0]
    far = [jnp.exp(-far_ref[k, HEAD:HEAD + 1, :]) for k in range(GROUPS)]
    decay = [jnp.exp(-in_ref[k, 2 * HEAD:2 * HEAD + 1, :]) for k in range(GROUP)]
    carry = jnp.zeros((HEAD, STATE), f32)
    for k in range(GROUPS - 1):
        carry = jnp.where(k < group, far[k] * carry + far_ref[k, 0:HEAD, :], carry)
    for k in range(GROUP):
        out_ref[k, 0:HEAD, :] = carry
        if k + 1 < GROUP:
            carry = decay[k] * carry + in_ref[k, 0:HEAD, :]
    carry = jnp.zeros((HEAD, STATE), f32)
    for k in reversed(range(1, GROUPS)):
        carry = jnp.where(k > group, far[k] * carry + far_ref[k, 0:HEAD, :], carry)
    for k in reversed(range(GROUP)):
        out_ref[k, HEAD:, :] = carry
        if k:
            carry = decay[k] * carry + in_ref[k, HEAD:2 * HEAD, :]


def outer_kernel(scale, c_ref, group_ref, in_ref, u_ref, v_ref, en_ref, te_ref, proj_ref,
                 yl_ref, gml_ref, gp_ref, gm_ref, pk_ref, yk_ref, send_ref, y_ref):
    c = c_ref[0]
    pieces = [in_ref[(group_ref[0] + h) & (GROUP - 1)] for h in range(GROUP)]
    carry = jnp.concatenate([a[:HEAD] for a in pieces], axis=0).astype(bf16)
    adjoint = jnp.concatenate([a[HEAD:] for a in pieces], axis=0).astype(bf16)
    inject = proj_ref[:, :STATE]
    readout = proj_ref[:, STATE:]
    gi = scale * (gp_ref[:, :STATE] + mm(u_ref[...], adjoint))
    gr = scale * (gp_ref[:, STATE:] + mm(v_ref[...], carry))
    grad = scale * (gml_ref[...] + te_ref[...] * mm_nt(inject, adjoint))
    gm_ref[...] = grad.astype(bf16)
    pk_ref[:, :STATE] = gi
    pk_ref[:, STATE:] = gr
    send_ref[:, :HALF] = grad
    send_ref[:, HALF:HALF + STATE] = gi
    send_ref[:, HALF + STATE:2 * HALF] = gr
    y_ref[...] = yl_ref[...] + en_ref[...] * mm_nt(readout, carry)
    yk_ref[...] = y_ref[pl.ds(pl.multiple_of(c * LD, LD), LD), :]
    there = y_ref[pl.ds(pl.multiple_of((1 - c) * LD, LD), LD), :]
    send_ref[0:LD, 2 * HALF:] = there[:, :LD]
    send_ref[LD:, 2 * HALF:] = there[:, LD:]


def weight_kernel(c_ref, group_ref, xt_ref, gm_ref, pk_ref, recv_ref, out_ref):
    c = c_ref[0]
    rows = out_ref.shape[0]
    xt = xt_ref[pl.ds(pl.multiple_of(c * rows, rows), rows), :]
    out_ref[:, pl.ds(pl.multiple_of(c * HALF, HALF), HALF)] = mm(xt, gm_ref[...])
    out_ref[:, pl.ds(pl.multiple_of((1 - c) * HALF, HALF), HALF)] = mm(xt, recv_ref[:, :HALF].astype(bf16))
    out_ref[:, 2 * HALF:] = mm(xt, (pk_ref[...] + recv_ref[:, HALF:2 * HALF]).astype(bf16))


def fold_kernel(c_ref, group_ref, in_ref, out_ref):
    total = jnp.sum(in_ref[...], axis=0)
    step = out_ref.shape[1]
    for k in range(ZN):
        out_ref[k] = total[k * step:(k + 1) * step, :]


def spread_kernel(scale, c_ref, group_ref, in_ref, out_ref):
    total = scale * jnp.sum(in_ref[...], axis=0)
    for k in range(DP):
        out_ref[k] = total


def place_kernel(c_ref, group_ref, in_ref, yk_ref, recv_ref, x_ref, bc_ref, y_ref):
    for k in range(DP):
        piece = in_ref[k]
        x_ref[2 * k:2 * k + 2, :] = piece[:, :2 * HALF]
        bc_ref[2 * k:2 * k + 2, :] = piece[:, 2 * HALF:]
    c = c_ref[0]
    own = pl.multiple_of(c * HALF, LD)
    oth = pl.multiple_of((1 - c) * HALF, LD)
    y_ref[:, pl.ds(own, HALF)] = yk_ref[...].astype(bf16)
    y_ref[:, pl.ds(oth, LD)] = recv_ref[0:LD, :].astype(bf16)
    y_ref[:, pl.ds(pl.multiple_of(oth + LD, LD), LD)] = recv_ref[LD:, :].astype(bf16)


def whole(shape):
    return pl.BlockSpec(shape, lambda i, c, g: (0,) * len(shape))


def call(kernel, place, outs, ins, scratch=(), specs=None):
    return pl.pallas_call(
        kernel,
        out_shape=[jax.ShapeDtypeStruct(s, d) for s, d in outs],
        grid_spec=pltpu.PrefetchScalarGridSpec(
            num_scalar_prefetch=2, grid=(1,), in_specs=specs or [whole(a.shape) for a in ins],
            out_specs=[whole(s) for s, _ in outs], scratch_shapes=list(scratch)),
        compiler_params=pltpu.CompilerParams(vmem_limit_bytes=16 * 1024 * 1024),
    )(*place, *ins)


def body(records, x_weight, bc_weight, decay_codes, out_grad):
    x = records[0]
    g = out_grad[0]
    codes = decay_codes[0].T
    d = x.shape[1]
    frames = LD * 2 * ZN
    unit = 1.0 / (32.0 * frames)
    out_scale = float((STATE * frames) ** -0.5)
    grad_scale = float((DP * frames) ** -0.5)
    place = lax.optimization_barrier((
        lax.axis_index("c").astype(jnp.int32).reshape(1),
        lax.div(lax.axis_index("z"), GROUP).astype(jnp.int32).reshape(1)))
    swap = [(0, 1), (1, 0)]
    near = [[GROUP * a + b for b in range(GROUP)] for a in range(GROUPS)]
    across = [[GROUP * a + (a + b) % GROUP for a in range(GROUPS)] for b in range(GROUP)]

    here = pl.BlockSpec((LD, HALF), lambda i, c, g: (0, c[0]))
    there = pl.BlockSpec((LD, HALF), lambda i, c, g: (0, 1 - c[0]))
    x, g, codes, wx, wbc = (
        pltpu.with_memory_space_constraint(a, pltpu.MemorySpace.HBM)
        for a in (x, g, codes, x_weight, bc_weight))
    (pack,) = call(
        pack_kernel, place, [((LD, d + HALF + LD), f32)], (x, g, codes), (),
        [whole(x.shape), there, whole(codes.shape)])
    pack = lax.ppermute(pack, "c", swap)
    half = (LD, HALF)
    owned = call(
        own_kernel, place,
        [(half, bf16), ((LD, 2 * STATE), bf16), (half, bf16), ((HEADS, LD), f32), ((LD, d), bf16),
         ((d, HALF), bf16), ((d, 2 * STATE), bf16)],
        (x, g, codes, wx, wbc), (),
        [whole(x.shape), here, whole(codes.shape), pl.BlockSpec((d, HALF), lambda i, c, g: (0, c[0])),
         whole(wbc.shape)])

    sq = (CHIP, HALF)
    pay, ue, v, en, te, proj, xc, yl, gml, gpl = call(
        lambda *refs: local_kernel(unit, *refs), place,
        [((GROUP, 2 * HEAD + 8, STATE), f32), (sq, bf16), (sq, bf16), (sq, f32), (sq, f32),
         ((CHIP, 2 * STATE), bf16), ((CHIP, d), bf16), (sq, f32), (sq, f32), ((CHIP, 2 * STATE), f32)],
        (*owned, pack), [pltpu.VMEM(sq, f32), pltpu.VMEM((HEADS, CHIP), f32), pltpu.VMEM(sq, bf16)])

    pay = lax.all_to_all(pay, "z", 0, 0, tiled=True, axis_index_groups=near)
    (far,) = call(total_kernel, place, [((GROUPS, HEAD + 8, STATE), f32)], (pay,))
    far = lax.all_to_all(far, "z", 0, 0, tiled=True, axis_index_groups=across)
    (pay,) = call(prefix_kernel, place, [((GROUP, 2 * HEAD, STATE), f32)], (pay, far))
    pay = lax.all_to_all(pay, "z", 0, 0, tiled=True, axis_index_groups=near)

    gm, pk, yk, send = call(
        lambda *refs: outer_kernel(out_scale, *refs), place,
        [(sq, bf16), ((CHIP, 2 * STATE), f32), ((LD, HALF), f32), ((CHIP, 2 * HALF + LD), f32)],
        (pay, ue, v, en, te, proj, yl, gml, gpl), [pltpu.VMEM(sq, f32)])
    recv = lax.ppermute(send, "c", swap)
    xt = xc.T.reshape(ZN, 2, DP, 2, CHIP).transpose(1, 2, 0, 3, 4).reshape(d, CHIP)
    width = 2 * HALF + 2 * STATE
    (grad,) = call(weight_kernel, place, [((d // 2, width), f32)], (xt, gm, pk, recv))

    rows = d // 2 // DP
    part = lax.all_to_all(grad.reshape(DP, rows, width), "dp", 0, 0, tiled=True)
    (part,) = call(fold_kernel, place, [((ZN, rows // ZN, width), f32)], (part,))
    part = lax.all_to_all(part, "z", 0, 0, tiled=True)
    (part,) = call(lambda *refs: spread_kernel(grad_scale, *refs), place, [((DP, rows // ZN, width), f32)], (part,))
    part = lax.all_to_all(part, "dp", 0, 0, tiled=True)
    x_grad, bc_grad, y = call(
        place_kernel, place,
        [((2 * DP, 2 * HALF), f32), ((2 * DP, 2 * STATE), f32), ((LD, 2 * HALF), bf16)], (part, yk, recv), (),
        [whole(part.shape), whole(yk.shape), pl.BlockSpec((CHIP, LD), lambda i, c, g: (0, 2 * HALF // LD))])
    return y[None], x_grad, bc_grad


def solution(mesh):
    mesh = Mesh(mesh.devices.reshape(DP, ZN, 2), ("dp", "z", "c"))
    frames = P("dp", ("z", "c"), None)
    rows = P(("z", "c"), None)
    return jax.shard_map(
        body,
        mesh=mesh,
        in_specs=(frames, P(), P(), frames, frames),
        out_specs=(frames, rows, rows),
        check_vma=False,
    )
```

```python
import jax
import jax.numpy as jnp
from jax import lax
from jax.experimental import pallas as pl
from jax.experimental.pallas import tpu as pltpu
from jax.sharding import Mesh, PartitionSpec as P

f32 = jnp.float32
bf16 = jnp.bfloat16

LD = 128
CHIP = 2 * LD
HEADS = 8
HEAD = 64
STATE = 128
HALF = HEADS * HEAD // 2
ZN = 16
DP = 16
GROUP = 4
CUTS = 4
GROUPS = ZN // GROUP


def mm(a, b):
    return jnp.dot(a, b, preferred_element_type=f32)


def mm_tn(a, b):
    return lax.dot_general(a, b, (((0,), (0,)), ((), ())), preferred_element_type=f32)


def mm_nt(a, b):
    return lax.dot_general(a, b, (((1,), (1,)), ((), ())), preferred_element_type=f32)


def causal(shape):
    return lax.broadcasted_iota(jnp.int32, shape, 0) >= lax.broadcasted_iota(jnp.int32, shape, 1)


def pack_kernel(c_ref, group_ref, x_hbm, g_hbm, codes_hbm, out_ref, x_ref, g_ref, codes_ref, sems):
    d = x_ref.shape[1]
    other = pl.multiple_of((1 - c_ref[0]) * HALF, HALF)
    step = LD // CUTS
    copies = [
        pltpu.make_async_copy(x_hbm.at[k * step:(k + 1) * step], x_ref.at[k * step:(k + 1) * step], sems.at[k])
        for k in range(CUTS)]
    copies.append(pltpu.make_async_copy(g_hbm.at[:, pl.ds(other, HALF)], g_ref, sems.at[CUTS]))
    copies.append(pltpu.make_async_copy(codes_hbm, codes_ref, sems.at[CUTS + 1]))
    for copy in copies:
        copy.start()
    out_ref[HEADS:, d + HALF:] = jnp.zeros((LD - HEADS, LD), f32)
    for k in range(CUTS):
        copies[k].wait()
        out_ref[k * step:(k + 1) * step, :d] = x_ref[k * step:(k + 1) * step, :].astype(f32)
    copies[CUTS].wait()
    out_ref[:, d:d + HALF] = g_ref[...].astype(f32)
    copies[CUTS + 1].wait()
    out_ref[0:HEADS, d + HALF:] = codes_ref[...].astype(f32)


def own_kernel(c_ref, group_ref, x_ref, g_ref, codes_ref, wx_ref, wbc_ref,
               mix_ref, proj_ref, g_out_ref, codes_out_ref, x_out_ref, wx_out_ref, wbc_out_ref):
    x = x_ref[...]
    wx = wx_ref[...]
    wbc = wbc_ref[...]
    mix_ref[...] = mm(x, wx).astype(bf16)
    proj_ref[...] = mm(x, wbc).astype(bf16)
    g_out_ref[...] = g_ref[...]
    codes_out_ref[...] = codes_ref[...].astype(f32)
    x_out_ref[...] = x
    wx_out_ref[...] = wx
    wbc_out_ref[...] = wbc


def local_kernel(unit, c_ref, group_ref, mix_ref, pj_ref, g_ref, codes_ref, x_ref, wx_ref, wbc_ref, pack_ref,
                 pay_ref, ue_ref, v_ref, en_ref, te_ref, proj_ref, xc_ref, yl_ref, gm_ref, gp_ref,
                 gs_ref, cs_ref, ms_ref):
    c = c_ref[0]
    own = pl.multiple_of(c * LD, LD)
    oth = pl.multiple_of((1 - c) * LD, LD)
    d = x_ref.shape[1]
    xo = pack_ref[:, :d].astype(bf16)
    xc_ref[pl.ds(own, LD), :] = x_ref[...]
    xc_ref[pl.ds(oth, LD), :] = xo
    gs_ref[pl.ds(own, LD), :] = g_ref[...].astype(f32)
    gs_ref[pl.ds(oth, LD), :] = pack_ref[:, d:d + HALF]
    cs_ref[:, pl.ds(own, LD)] = codes_ref[...]
    cs_ref[:, pl.ds(oth, LD)] = pack_ref[0:HEADS, d + HALF:]
    ms_ref[pl.ds(own, LD), :] = mix_ref[...]
    ms_ref[pl.ds(oth, LD), :] = mm(xo, wx_ref[...]).astype(bf16)
    proj_ref[pl.ds(own, LD), :] = pj_ref[...]
    proj_ref[pl.ds(oth, LD), :] = mm(xo, wbc_ref[...]).astype(bf16)
    codes = cs_ref[...]
    hi = jnp.floor(codes * (1.0 / 32.0))
    lo = codes - 32.0 * hi
    row = lax.broadcasted_iota(jnp.int32, (HEADS, HALF), 0)
    col = lax.broadcasted_iota(jnp.int32, (HEADS, HALF), 1)
    spread = jnp.where(row == col // HEAD + c * (HEADS // 2), 1.0, 0.0).astype(bf16)
    hi = mm_tn(hi.astype(bf16), spread).astype(bf16)
    lo = mm_tn(lo.astype(bf16), spread).astype(bf16)
    mask = causal((CHIP, CHIP))
    tri = jnp.where(mask, 1.0, 0.0).astype(bf16)
    running = unit * (32.0 * mm(tri, hi) + mm(tri, lo))
    last = running[CHIP - 1:CHIP, :]
    en = jnp.exp(-running)
    ep = jnp.exp(running)
    te = ep * jnp.exp(-last)
    en_ref[...] = en
    te_ref[...] = te
    mixer = ms_ref[...].astype(f32)
    inject = proj_ref[:, :STATE]
    readout = proj_ref[:, STATE:]
    v = (en * gs_ref[...]).astype(bf16)
    ue = (te * mixer).astype(bf16)
    u = (ep * mixer).astype(bf16)
    ue_ref[...] = ue
    v_ref[...] = v
    state = mm_tn(ue, inject)
    adjoint = mm_tn(v, readout)
    for h in range(GROUP):
        at = (group_ref[0] + h) & (GROUP - 1)
        pay_ref[at, 0:HEAD, :] = state[h * HEAD:(h + 1) * HEAD, :]
        pay_ref[at, HEAD:2 * HEAD, :] = adjoint[h * HEAD:(h + 1) * HEAD, :]
        pay_ref[at, 2 * HEAD:, :] = jnp.broadcast_to(last[:, h * HEAD:h * HEAD + 1], (8, STATE))
    scores = jnp.where(mask, mm_nt(readout, inject), 0.0).astype(bf16)
    pairs = jnp.where(mask, mm_nt(v, u), 0.0).astype(bf16)
    yl_ref[...] = en * mm(scores, u)
    gm_ref[...] = ep * mm_tn(scores, v)
    gp_ref[:, :STATE] = mm_tn(pairs, readout)
    gp_ref[:, STATE:] = mm(pairs, inject)


def total_kernel(c_ref, group_ref, in_ref, out_ref):
    group = group_ref[0]
    logs = [in_ref[k, 2 * HEAD:, :] for k in range(GROUP)]
    decay = [jnp.exp(-a[0:1, :]) for a in logs]
    state = in_ref[0, 0:HEAD, :]
    for k in range(1, GROUP):
        state = decay[k] * state + in_ref[k, 0:HEAD, :]
    adjoint = in_ref[GROUP - 1, HEAD:2 * HEAD, :]
    for k in reversed(range(GROUP - 1)):
        adjoint = decay[k] * adjoint + in_ref[k, HEAD:2 * HEAD, :]
    total = logs[0] + logs[1] + logs[2] + logs[3]
    for k in range(GROUPS):
        out_ref[k, 0:HEAD, :] = jnp.where(k > group, state, adjoint)
        out_ref[k, HEAD:, :] = total


def prefix_kernel(c_ref, group_ref, in_ref, far_ref, out_ref):
    group = group_ref[0]
    far = [jnp.exp(-far_ref[k, HEAD:HEAD + 1, :]) for k in range(GROUPS)]
    decay = [jnp.exp(-in_ref[k, 2 * HEAD:2 * HEAD + 1, :]) for k in range(GROUP)]
    carry = jnp.zeros((HEAD, STATE), f32)
    for k in range(GROUPS - 1):
        carry = jnp.where(k < group, far[k] * carry + far_ref[k, 0:HEAD, :], carry)
    for k in range(GROUP):
        out_ref[k, 0:HEAD, :] = carry
        if k + 1 < GROUP:
            carry = decay[k] * carry + in_ref[k, 0:HEAD, :]
    carry = jnp.zeros((HEAD, STATE), f32)
    for k in reversed(range(1, GROUPS)):
        carry = jnp.where(k > group, far[k] * carry + far_ref[k, 0:HEAD, :], carry)
    for k in reversed(range(GROUP)):
        out_ref[k, HEAD:, :] = carry
        if k:
            carry = decay[k] * carry + in_ref[k, HEAD:2 * HEAD, :]


def outer_kernel(scale, c_ref, group_ref, in_ref, u_ref, v_ref, en_ref, te_ref, proj_ref,
                 yl_ref, gml_ref, gp_ref, gm_ref, pk_ref, yk_ref, send_ref, y_ref):
    c = c_ref[0]
    pieces = [in_ref[(group_ref[0] + h) & (GROUP - 1)] for h in range(GROUP)]
    carry = jnp.concatenate([a[:HEAD] for a in pieces], axis=0).astype(bf16)
    adjoint = jnp.concatenate([a[HEAD:] for a in pieces], axis=0).astype(bf16)
    inject = proj_ref[:, :STATE]
    readout = proj_ref[:, STATE:]
    gi = scale * (gp_ref[:, :STATE] + mm(u_ref[...], adjoint))
    gr = scale * (gp_ref[:, STATE:] + mm(v_ref[...], carry))
    grad = scale * (gml_ref[...] + te_ref[...] * mm_nt(inject, adjoint))
    gm_ref[...] = grad.astype(bf16)
    pk_ref[:, :STATE] = gi
    pk_ref[:, STATE:] = gr
    send_ref[:, :HALF] = grad
    send_ref[:, HALF:HALF + STATE] = gi
    send_ref[:, HALF + STATE:2 * HALF] = gr
    y_ref[...] = yl_ref[...] + en_ref[...] * mm_nt(readout, carry)
    yk_ref[...] = y_ref[pl.ds(pl.multiple_of(c * LD, LD), LD), :]
    there = y_ref[pl.ds(pl.multiple_of((1 - c) * LD, LD), LD), :]
    send_ref[0:LD, 2 * HALF:] = there[:, :LD]
    send_ref[LD:, 2 * HALF:] = there[:, LD:]


def near_kernel(c_ref, group_ref, xt_ref, gm_ref, out_ref):
    rows = out_ref.shape[0]
    xt = xt_ref[pl.ds(pl.multiple_of(c_ref[0] * rows, rows), rows), :]
    out_ref[...] = mm(xt, gm_ref[...])


def weight_kernel(c_ref, group_ref, xt_ref, near_ref, pk_ref, recv_ref, out_ref):
    c = c_ref[0]
    rows = out_ref.shape[0]
    xt = xt_ref[pl.ds(pl.multiple_of(c * rows, rows), rows), :]
    out_ref[:, pl.ds(pl.multiple_of(c * HALF, HALF), HALF)] = near_ref[...]
    out_ref[:, pl.ds(pl.multiple_of((1 - c) * HALF, HALF), HALF)] = mm(xt, recv_ref[:, :HALF].astype(bf16))
    out_ref[:, 2 * HALF:] = mm(xt, (pk_ref[...] + recv_ref[:, HALF:2 * HALF]).astype(bf16))


def fold_kernel(c_ref, group_ref, in_ref, out_ref):
    total = jnp.sum(in_ref[...], axis=0)
    step = out_ref.shape[1]
    for k in range(ZN):
        out_ref[k] = total[k * step:(k + 1) * step, :]


def spread_kernel(scale, c_ref, group_ref, in_ref, out_ref):
    total = scale * jnp.sum(in_ref[...], axis=0)
    for k in range(DP):
        out_ref[k] = total


def place_kernel(c_ref, group_ref, in_ref, yk_ref, recv_ref, x_ref, bc_ref, y_ref):
    for k in range(DP):
        piece = in_ref[k]
        x_ref[2 * k:2 * k + 2, :] = piece[:, :2 * HALF]
        bc_ref[2 * k:2 * k + 2, :] = piece[:, 2 * HALF:]
    c = c_ref[0]
    own = pl.multiple_of(c * HALF, LD)
    oth = pl.multiple_of((1 - c) * HALF, LD)
    y_ref[:, pl.ds(own, HALF)] = yk_ref[...].astype(bf16)
    y_ref[:, pl.ds(oth, LD)] = recv_ref[0:LD, :].astype(bf16)
    y_ref[:, pl.ds(pl.multiple_of(oth + LD, LD), LD)] = recv_ref[LD:, :].astype(bf16)


def whole(shape):
    return pl.BlockSpec(shape, lambda i, c, g: (0,) * len(shape))


def call(kernel, place, outs, ins, scratch=(), specs=None):
    return pl.pallas_call(
        kernel,
        out_shape=[jax.ShapeDtypeStruct(s, d) for s, d in outs],
        grid_spec=pltpu.PrefetchScalarGridSpec(
            num_scalar_prefetch=2, grid=(1,), in_specs=specs or [whole(a.shape) for a in ins],
            out_specs=[whole(s) for s, _ in outs], scratch_shapes=list(scratch)),
        compiler_params=pltpu.CompilerParams(vmem_limit_bytes=16 * 1024 * 1024),
    )(*place, *ins)


def body(records, x_weight, bc_weight, decay_codes, out_grad):
    x = records[0]
    g = out_grad[0]
    codes = decay_codes[0].T
    d = x.shape[1]
    frames = LD * 2 * ZN
    unit = 1.0 / (32.0 * frames)
    out_scale = float((STATE * frames) ** -0.5)
    grad_scale = float((DP * frames) ** -0.5)
    place = lax.optimization_barrier((
        lax.axis_index("c").astype(jnp.int32).reshape(1),
        lax.div(lax.axis_index("z"), GROUP).astype(jnp.int32).reshape(1)))
    swap = [(0, 1), (1, 0)]
    near = [[GROUP * a + b for b in range(GROUP)] for a in range(GROUPS)]
    across = [[GROUP * a + (a + b) % GROUP for a in range(GROUPS)] for b in range(GROUP)]

    here = pl.BlockSpec((LD, HALF), lambda i, c, g: (0, c[0]))
    x, g, codes, wx, wbc = (
        pltpu.with_memory_space_constraint(a, pltpu.MemorySpace.HBM)
        for a in (x, g, codes, x_weight, bc_weight))
    raw = pl.BlockSpec(memory_space=pl.ANY)
    (pack,) = call(
        pack_kernel, place, [((LD, d + HALF + LD), f32)], (x, g, codes),
        [pltpu.VMEM((LD, d), bf16), pltpu.VMEM((LD, HALF), bf16), pltpu.VMEM((HEADS, LD), jnp.int32),
         pltpu.SemaphoreType.DMA((CUTS + 2,))],
        [raw, raw, raw])
    pack = lax.ppermute(pack, "c", swap)
    half = (LD, HALF)
    owned = call(
        own_kernel, place,
        [(half, bf16), ((LD, 2 * STATE), bf16), (half, bf16), ((HEADS, LD), f32), ((LD, d), bf16),
         ((d, HALF), bf16), ((d, 2 * STATE), bf16)],
        (x, g, codes, wx, wbc), (),
        [whole(x.shape), here, whole(codes.shape), pl.BlockSpec((d, HALF), lambda i, c, g: (0, c[0])),
         whole(wbc.shape)])

    sq = (CHIP, HALF)
    pay, ue, v, en, te, proj, xc, yl, gml, gpl = call(
        lambda *refs: local_kernel(unit, *refs), place,
        [((GROUP, 2 * HEAD + 8, STATE), f32), (sq, bf16), (sq, bf16), (sq, f32), (sq, f32),
         ((CHIP, 2 * STATE), bf16), ((CHIP, d), bf16), (sq, f32), (sq, f32), ((CHIP, 2 * STATE), f32)],
        (*owned, pack), [pltpu.VMEM(sq, f32), pltpu.VMEM((HEADS, CHIP), f32), pltpu.VMEM(sq, bf16)])

    pay = lax.all_to_all(pay, "z", 0, 0, tiled=True, axis_index_groups=near)
    (far,) = call(total_kernel, place, [((GROUPS, HEAD + 8, STATE), f32)], (pay,))
    far = lax.all_to_all(far, "z", 0, 0, tiled=True, axis_index_groups=across)
    (pay,) = call(prefix_kernel, place, [((GROUP, 2 * HEAD, STATE), f32)], (pay, far))
    pay = lax.all_to_all(pay, "z", 0, 0, tiled=True, axis_index_groups=near)

    gm, pk, yk, send = call(
        lambda *refs: outer_kernel(out_scale, *refs), place,
        [(sq, bf16), ((CHIP, 2 * STATE), f32), ((LD, HALF), f32), ((CHIP, 2 * HALF + LD), f32)],
        (pay, ue, v, en, te, proj, yl, gml, gpl), [pltpu.VMEM(sq, f32)])
    recv = lax.ppermute(send, "c", swap)
    xt = xc.T.reshape(ZN, 2, DP, 2, CHIP).transpose(1, 2, 0, 3, 4).reshape(d, CHIP)
    width = 2 * HALF + 2 * STATE
    (near_part,) = call(near_kernel, place, [((d // 2, HALF), f32)], (xt, gm))
    (grad,) = call(weight_kernel, place, [((d // 2, width), f32)], (xt, near_part, pk, recv))

    rows = d // 2 // DP
    part = lax.all_to_all(grad.reshape(DP, rows, width), "dp", 0, 0, tiled=True)
    (part,) = call(fold_kernel, place, [((ZN, rows // ZN, width), f32)], (part,))
    part = lax.all_to_all(part, "z", 0, 0, tiled=True)
    (part,) = call(lambda *refs: spread_kernel(grad_scale, *refs), place, [((DP, rows // ZN, width), f32)], (part,))
    part = lax.all_to_all(part, "dp", 0, 0, tiled=True)
    x_grad, bc_grad, y = call(
        place_kernel, place,
        [((2 * DP, 2 * HALF), f32), ((2 * DP, 2 * STATE), f32), ((LD, 2 * HALF), bf16)], (part, yk, recv), (),
        [whole(part.shape), whole(yk.shape), pl.BlockSpec((CHIP, LD), lambda i, c, g: (0, 2 * HALF // LD))])
    return y[None], x_grad, bc_grad


def solution(mesh):
    mesh = Mesh(mesh.devices.reshape(DP, ZN, 2), ("dp", "z", "c"))
    frames = P("dp", ("z", "c"), None)
    rows = P(("z", "c"), None)
    return jax.shard_map(
        body,
        mesh=mesh,
        in_specs=(frames, P(), P(), frames, frames),
        out_specs=(frames, rows, rows),
        check_vma=False,
    )
```

```python
import jax
import jax.numpy as jnp
from jax import lax
from jax.experimental import pallas as pl
from jax.experimental.pallas import tpu as pltpu
from jax.sharding import Mesh, PartitionSpec as P

f32 = jnp.float32
bf16 = jnp.bfloat16

LD = 128
CHIP = 2 * LD
HEADS = 8
HEAD = 64
STATE = 128
HALF = HEADS * HEAD // 2
ZN = 16
DP = 16
SIDE = 4
GROUP = 4
CUTS = 4
GROUPS = ZN // GROUP


def mm(a, b):
    return jnp.dot(a, b, preferred_element_type=f32)


def mm_tn(a, b):
    return lax.dot_general(a, b, (((0,), (0,)), ((), ())), preferred_element_type=f32)


def mm_nt(a, b):
    return lax.dot_general(a, b, (((1,), (1,)), ((), ())), preferred_element_type=f32)


def causal(shape):
    return lax.broadcasted_iota(jnp.int32, shape, 0) >= lax.broadcasted_iota(jnp.int32, shape, 1)


def pack_kernel(c_ref, group_ref, x_hbm, g_hbm, codes_hbm, out_ref, x_ref, g_ref, codes_ref, sems):
    d = x_ref.shape[1]
    other = pl.multiple_of((1 - c_ref[0]) * HALF, HALF)
    step = LD // CUTS
    copies = [
        pltpu.make_async_copy(x_hbm.at[k * step:(k + 1) * step], x_ref.at[k * step:(k + 1) * step], sems.at[k])
        for k in range(CUTS)]
    copies.append(pltpu.make_async_copy(g_hbm.at[:, pl.ds(other, HALF)], g_ref, sems.at[CUTS]))
    copies.append(pltpu.make_async_copy(codes_hbm, codes_ref, sems.at[CUTS + 1]))
    for copy in copies:
        copy.start()
    out_ref[HEADS:, d + HALF:] = jnp.zeros((LD - HEADS, LD), f32)
    for k in range(CUTS):
        copies[k].wait()
        out_ref[k * step:(k + 1) * step, :d] = x_ref[k * step:(k + 1) * step, :].astype(f32)
    copies[CUTS].wait()
    out_ref[:, d:d + HALF] = g_ref[...].astype(f32)
    copies[CUTS + 1].wait()
    out_ref[0:HEADS, d + HALF:] = codes_ref[...].astype(f32)


def own_kernel(c_ref, group_ref, x_ref, g_ref, codes_ref, wx_ref, wbc_ref,
               mix_ref, proj_ref, g_out_ref, codes_out_ref, x_out_ref, wx_out_ref, wbc_out_ref):
    x = x_ref[...]
    wx = wx_ref[...]
    wbc = wbc_ref[...]
    mix_ref[...] = mm(x, wx).astype(bf16)
    proj_ref[...] = mm(x, wbc).astype(bf16)
    g_out_ref[...] = g_ref[...]
    codes_out_ref[...] = codes_ref[...].astype(f32)
    x_out_ref[...] = x
    wx_out_ref[...] = wx
    wbc_out_ref[...] = wbc


def local_kernel(unit, c_ref, group_ref, mix_ref, pj_ref, g_ref, codes_ref, x_ref, wx_ref, wbc_ref, pack_ref,
                 pay_ref, ue_ref, v_ref, en_ref, te_ref, proj_ref, xc_ref, yl_ref, gm_ref, gp_ref,
                 gs_ref, cs_ref, ms_ref):
    c = c_ref[0]
    own = pl.multiple_of(c * LD, LD)
    oth = pl.multiple_of((1 - c) * LD, LD)
    d = x_ref.shape[1]
    xo = pack_ref[:, :d].astype(bf16)
    xc_ref[pl.ds(own, LD), :] = x_ref[...]
    xc_ref[pl.ds(oth, LD), :] = xo
    gs_ref[pl.ds(own, LD), :] = g_ref[...].astype(f32)
    gs_ref[pl.ds(oth, LD), :] = pack_ref[:, d:d + HALF]
    cs_ref[:, pl.ds(own, LD)] = codes_ref[...]
    cs_ref[:, pl.ds(oth, LD)] = pack_ref[0:HEADS, d + HALF:]
    ms_ref[pl.ds(own, LD), :] = mix_ref[...]
    ms_ref[pl.ds(oth, LD), :] = mm(xo, wx_ref[...]).astype(bf16)
    proj_ref[pl.ds(own, LD), :] = pj_ref[...]
    proj_ref[pl.ds(oth, LD), :] = mm(xo, wbc_ref[...]).astype(bf16)
    codes = cs_ref[...]
    hi = jnp.floor(codes * (1.0 / 32.0))
    lo = codes - 32.0 * hi
    row = lax.broadcasted_iota(jnp.int32, (HEADS, HALF), 0)
    col = lax.broadcasted_iota(jnp.int32, (HEADS, HALF), 1)
    spread = jnp.where(row == col // HEAD + c * (HEADS // 2), 1.0, 0.0).astype(bf16)
    hi = mm_tn(hi.astype(bf16), spread).astype(bf16)
    lo = mm_tn(lo.astype(bf16), spread).astype(bf16)
    mask = causal((CHIP, CHIP))
    tri = jnp.where(mask, 1.0, 0.0).astype(bf16)
    running = unit * (32.0 * mm(tri, hi) + mm(tri, lo))
    last = running[CHIP - 1:CHIP, :]
    en = jnp.exp(-running)
    ep = jnp.exp(running)
    te = ep * jnp.exp(-last)
    en_ref[...] = en
    te_ref[...] = te
    mixer = ms_ref[...].astype(f32)
    inject = proj_ref[:, :STATE]
    readout = proj_ref[:, STATE:]
    v = (en * gs_ref[...]).astype(bf16)
    ue = (te * mixer).astype(bf16)
    u = (ep * mixer).astype(bf16)
    ue_ref[...] = ue
    v_ref[...] = v
    state = mm_tn(ue, inject)
    adjoint = mm_tn(v, readout)
    for h in range(GROUP):
        at = (group_ref[0] + h) & (GROUP - 1)
        pay_ref[at, 0:HEAD, :] = state[h * HEAD:(h + 1) * HEAD, :]
        pay_ref[at, HEAD:2 * HEAD, :] = adjoint[h * HEAD:(h + 1) * HEAD, :]
        pay_ref[at, 2 * HEAD:, :] = jnp.broadcast_to(last[:, h * HEAD:h * HEAD + 1], (8, STATE))
    scores = jnp.where(mask, mm_nt(readout, inject), 0.0).astype(bf16)
    pairs = jnp.where(mask, mm_nt(v, u), 0.0).astype(bf16)
    yl_ref[...] = en * mm(scores, u)
    gm_ref[...] = ep * mm_tn(scores, v)
    gp_ref[:, :STATE] = mm_tn(pairs, readout)
    gp_ref[:, STATE:] = mm(pairs, inject)


def total_kernel(c_ref, group_ref, in_ref, out_ref):
    group = group_ref[0]
    logs = [in_ref[k, 2 * HEAD:, :] for k in range(GROUP)]
    decay = [jnp.exp(-a[0:1, :]) for a in logs]
    state = in_ref[0, 0:HEAD, :]
    for k in range(1, GROUP):
        state = decay[k] * state + in_ref[k, 0:HEAD, :]
    adjoint = in_ref[GROUP - 1, HEAD:2 * HEAD, :]
    for k in reversed(range(GROUP - 1)):
        adjoint = decay[k] * adjoint + in_ref[k, HEAD:2 * HEAD, :]
    total = logs[0] + logs[1] + logs[2] + logs[3]
    for k in range(GROUPS):
        out_ref[k, 0:HEAD, :] = jnp.where(k > group, state, adjoint)
        out_ref[k, HEAD:, :] = total


def prefix_kernel(c_ref, group_ref, in_ref, far_ref, out_ref):
    group = group_ref[0]
    far = [jnp.exp(-far_ref[k, HEAD:HEAD + 1, :]) for k in range(GROUPS)]
    decay = [jnp.exp(-in_ref[k, 2 * HEAD:2 * HEAD + 1, :]) for k in range(GROUP)]
    carry = jnp.zeros((HEAD, STATE), f32)
    for k in range(GROUPS - 1):
        carry = jnp.where(k < group, far[k] * carry + far_ref[k, 0:HEAD, :], carry)
    for k in range(GROUP):
        out_ref[k, 0:HEAD, :] = carry
        if k + 1 < GROUP:
            carry = decay[k] * carry + in_ref[k, 0:HEAD, :]
    carry = jnp.zeros((HEAD, STATE), f32)
    for k in reversed(range(1, GROUPS)):
        carry = jnp.where(k > group, far[k] * carry + far_ref[k, 0:HEAD, :], carry)
    for k in reversed(range(GROUP)):
        out_ref[k, HEAD:, :] = carry
        if k:
            carry = decay[k] * carry + in_ref[k, HEAD:2 * HEAD, :]


def outer_kernel(scale, c_ref, group_ref, in_ref, u_ref, v_ref, en_ref, te_ref, proj_ref,
                 yl_ref, gml_ref, gp_ref, gm_ref, pk_ref, yk_ref, send_ref, y_ref):
    c = c_ref[0]
    pieces = [in_ref[(group_ref[0] + h) & (GROUP - 1)] for h in range(GROUP)]
    carry = jnp.concatenate([a[:HEAD] for a in pieces], axis=0).astype(bf16)
    adjoint = jnp.concatenate([a[HEAD:] for a in pieces], axis=0).astype(bf16)
    inject = proj_ref[:, :STATE]
    readout = proj_ref[:, STATE:]
    gi = scale * (gp_ref[:, :STATE] + mm(u_ref[...], adjoint))
    gr = scale * (gp_ref[:, STATE:] + mm(v_ref[...], carry))
    grad = scale * (gml_ref[...] + te_ref[...] * mm_nt(inject, adjoint))
    gm_ref[...] = grad.astype(bf16)
    pk_ref[:, :STATE] = gi
    pk_ref[:, STATE:] = gr
    send_ref[:, :HALF] = grad
    send_ref[:, HALF:HALF + STATE] = gi
    send_ref[:, HALF + STATE:2 * HALF] = gr
    y_ref[...] = yl_ref[...] + en_ref[...] * mm_nt(readout, carry)
    yk_ref[...] = y_ref[pl.ds(pl.multiple_of(c * LD, LD), LD), :]
    there = y_ref[pl.ds(pl.multiple_of((1 - c) * LD, LD), LD), :]
    send_ref[0:LD, 2 * HALF:] = there[:, :LD]
    send_ref[LD:, 2 * HALF:] = there[:, LD:]


def near_kernel(c_ref, group_ref, xa_ref, xb_ref, gm_ref, out_ref):
    xt = jnp.where(c_ref[0] == 0, xa_ref[...], xb_ref[...])
    out_ref[...] = mm(xt, gm_ref[...])


def weight_kernel(c_ref, group_ref, xa_ref, xb_ref, near_ref, pk_ref, recv_ref, out_ref):
    c = c_ref[0]
    xt = jnp.where(c == 0, xa_ref[...], xb_ref[...])
    out_ref[:, pl.ds(pl.multiple_of(c * HALF, HALF), HALF)] = near_ref[...]
    out_ref[:, pl.ds(pl.multiple_of((1 - c) * HALF, HALF), HALF)] = mm(xt, recv_ref[:, :HALF].astype(bf16))
    out_ref[:, 2 * HALF:] = mm(xt, (pk_ref[...] + recv_ref[:, HALF:2 * HALF]).astype(bf16))


def half_fold_kernel(c_ref, group_ref, in_ref, out_ref):
    total = jnp.sum(in_ref[...], axis=0)
    step = out_ref.shape[1]
    for k in range(SIDE):
        out_ref[k] = total[k * step:(k + 1) * step, :]


def fold_kernel(c_ref, group_ref, in_ref, out_ref):
    total = jnp.sum(in_ref[...], axis=0)
    step = out_ref.shape[1]
    for k in range(ZN):
        out_ref[k] = total[k * step:(k + 1) * step, :]


def spread_kernel(scale, c_ref, group_ref, in_ref, out_ref):
    total = scale * jnp.sum(in_ref[...], axis=0)
    for k in range(DP):
        out_ref[k] = total


def place_kernel(c_ref, group_ref, in_ref, yk_ref, recv_ref, x_ref, bc_ref, y_ref):
    for k in range(DP):
        piece = in_ref[k]
        x_ref[2 * k:2 * k + 2, :] = piece[:, :2 * HALF]
        bc_ref[2 * k:2 * k + 2, :] = piece[:, 2 * HALF:]
    c = c_ref[0]
    own = pl.multiple_of(c * HALF, LD)
    oth = pl.multiple_of((1 - c) * HALF, LD)
    y_ref[:, pl.ds(own, HALF)] = yk_ref[...].astype(bf16)
    y_ref[:, pl.ds(oth, LD)] = recv_ref[0:LD, :].astype(bf16)
    y_ref[:, pl.ds(pl.multiple_of(oth + LD, LD), LD)] = recv_ref[LD:, :].astype(bf16)


def whole(shape):
    return pl.BlockSpec(shape, lambda i, c, g: (0,) * len(shape))


def call(kernel, place, outs, ins, scratch=(), specs=None):
    return pl.pallas_call(
        kernel,
        out_shape=[jax.ShapeDtypeStruct(s, d) for s, d in outs],
        grid_spec=pltpu.PrefetchScalarGridSpec(
            num_scalar_prefetch=2, grid=(1,), in_specs=specs or [whole(a.shape) for a in ins],
            out_specs=[whole(s) for s, _ in outs], scratch_shapes=list(scratch)),
        compiler_params=pltpu.CompilerParams(vmem_limit_bytes=16 * 1024 * 1024),
    )(*place, *ins)


def lines(turn):
    def device(x, y, z, core):
        return ((x * SIDE + y) * ZN + z) * 2 + core

    groups = []
    for core in range(2):
        for z in range(ZN):
            for fixed in range(SIDE):
                along = range(SIDE)
                if core == turn:
                    groups.append([device(k, fixed, z, core) for k in along])
                else:
                    groups.append([device(fixed, k, z, core) for k in along])
    return groups


def body(records, x_weight, bc_weight, decay_codes, out_grad):
    x = records[0]
    g = out_grad[0]
    codes = decay_codes[0].T
    d = x.shape[1]
    frames = LD * 2 * ZN
    unit = 1.0 / (32.0 * frames)
    out_scale = float((STATE * frames) ** -0.5)
    grad_scale = float((DP * frames) ** -0.5)
    place = lax.optimization_barrier((
        lax.axis_index("c").astype(jnp.int32).reshape(1),
        lax.div(lax.axis_index("z"), GROUP).astype(jnp.int32).reshape(1)))
    swap = [(0, 1), (1, 0)]
    near = [[GROUP * a + b for b in range(GROUP)] for a in range(GROUPS)]
    across = [[GROUP * a + (a + b) % GROUP for a in range(GROUPS)] for b in range(GROUP)]

    here = pl.BlockSpec((LD, HALF), lambda i, c, g: (0, c[0]))
    x, g, codes, wx, wbc = (
        pltpu.with_memory_space_constraint(a, pltpu.MemorySpace.HBM)
        for a in (x, g, codes, x_weight, bc_weight))
    raw = pl.BlockSpec(memory_space=pl.ANY)
    (pack,) = call(
        pack_kernel, place, [((LD, d + HALF + LD), f32)], (x, g, codes),
        [pltpu.VMEM((LD, d), bf16), pltpu.VMEM((LD, HALF), bf16), pltpu.VMEM((HEADS, LD), jnp.int32),
         pltpu.SemaphoreType.DMA((CUTS + 2,))],
        [raw, raw, raw])
    pack = lax.ppermute(pack, "c", swap)
    half = (LD, HALF)
    owned = call(
        own_kernel, place,
        [(half, bf16), ((LD, 2 * STATE), bf16), (half, bf16), ((HEADS, LD), f32), ((LD, d), bf16),
         ((d, HALF), bf16), ((d, 2 * STATE), bf16)],
        (x, g, codes, wx, wbc), (),
        [whole(x.shape), here, whole(codes.shape), pl.BlockSpec((d, HALF), lambda i, c, g: (0, c[0])),
         whole(wbc.shape)])

    sq = (CHIP, HALF)
    pay, ue, v, en, te, proj, xc, yl, gml, gpl = call(
        lambda *refs: local_kernel(unit, *refs), place,
        [((GROUP, 2 * HEAD + 8, STATE), f32), (sq, bf16), (sq, bf16), (sq, f32), (sq, f32),
         ((CHIP, 2 * STATE), bf16), ((CHIP, d), bf16), (sq, f32), (sq, f32), ((CHIP, 2 * STATE), f32)],
        (*owned, pack), [pltpu.VMEM(sq, f32), pltpu.VMEM((HEADS, CHIP), f32), pltpu.VMEM(sq, bf16)])

    pay = lax.all_to_all(pay, "z", 0, 0, tiled=True, axis_index_groups=near)
    (far,) = call(total_kernel, place, [((GROUPS, HEAD + 8, STATE), f32)], (pay,))
    far = lax.all_to_all(far, "z", 0, 0, tiled=True, axis_index_groups=across)
    (pay,) = call(prefix_kernel, place, [((GROUP, 2 * HEAD, STATE), f32)], (pay, far))
    pay = lax.all_to_all(pay, "z", 0, 0, tiled=True, axis_index_groups=near)

    gm, pk, yk, send = call(
        lambda *refs: outer_kernel(out_scale, *refs), place,
        [(sq, bf16), ((CHIP, 2 * STATE), f32), ((LD, HALF), f32), ((CHIP, 2 * HALF + LD), f32)],
        (pay, ue, v, en, te, proj, yl, gml, gpl), [pltpu.VMEM(sq, f32)])
    recv = lax.ppermute(send, "c", swap)
    xt = xc.T.reshape(ZN, 2, SIDE, SIDE, 2, CHIP)
    xa = xt[:, 0].transpose(1, 2, 0, 3, 4).reshape(d // 2, CHIP)
    xb = xt[:, 1].transpose(2, 1, 0, 3, 4).reshape(d // 2, CHIP)
    width = 2 * HALF + 2 * STATE
    (near_part,) = call(near_kernel, place, [((d // 2, HALF), f32)], (xa, xb, gm))
    (grad,) = call(weight_kernel, place, [((d // 2, width), f32)], (xa, xb, near_part, pk, recv))

    rows = d // 2 // DP
    every = ("dp", "z", "c")
    first, second = lines(0), lines(1)
    part = lax.all_to_all(grad.reshape(SIDE, SIDE * rows, width), every, 0, 0, tiled=True, axis_index_groups=first)
    (part,) = call(half_fold_kernel, place, [((SIDE, rows, width), f32)], (part,))
    part = lax.all_to_all(part, every, 0, 0, tiled=True, axis_index_groups=second)
    (part,) = call(fold_kernel, place, [((ZN, rows // ZN, width), f32)], (part,))
    part = lax.all_to_all(part, "z", 0, 0, tiled=True)
    (part,) = call(lambda *refs: spread_kernel(grad_scale, *refs), place, [((DP, rows // ZN, width), f32)], (part,))
    part = lax.all_to_all(part, "dp", 0, 0, tiled=True)
    x_grad, bc_grad, y = call(
        place_kernel, place,
        [((2 * DP, 2 * HALF), f32), ((2 * DP, 2 * STATE), f32), ((LD, 2 * HALF), bf16)], (part, yk, recv), (),
        [whole(part.shape), whole(yk.shape), pl.BlockSpec((CHIP, LD), lambda i, c, g: (0, 2 * HALF // LD))])
    return y[None], x_grad, bc_grad


def solution(mesh):
    mesh = Mesh(mesh.devices.reshape(DP, ZN, 2), ("dp", "z", "c"))
    frames = P("dp", ("z", "c"), None)
    rows = P(("z", "c"), None)
    return jax.shard_map(
        body,
        mesh=mesh,
        in_specs=(frames, P(), P(), frames, frames),
        out_specs=(frames, rows, rows),
        check_vma=False,
    )
```

```python
import jax
import jax.numpy as jnp
from jax import lax
from jax.experimental import pallas as pl
from jax.experimental.pallas import tpu as pltpu
from jax.sharding import Mesh, PartitionSpec as P

f32 = jnp.float32
bf16 = jnp.bfloat16

LD = 128
CHIP = 2 * LD
HEADS = 8
HEAD = 64
STATE = 128
HALF = HEADS * HEAD // 2
ZN = 16
DP = 16
SIDE = 4
GROUP = 4
CUTS = 4
NEAR = (0, 3, 1, 2)
NEAR_AT = (0, 2, 3, 1)
FAR = (0, 2, 1, 3)
FAR_AT = (0, 2, 1, 3)
GROUPS = ZN // GROUP


def mm(a, b):
    return jnp.dot(a, b, preferred_element_type=f32)


def mm_tn(a, b):
    return lax.dot_general(a, b, (((0,), (0,)), ((), ())), preferred_element_type=f32)


def mm_nt(a, b):
    return lax.dot_general(a, b, (((1,), (1,)), ((), ())), preferred_element_type=f32)


def head_at(group_ref, h):
    chip = (group_ref[0] + h) & (GROUP - 1)
    return jnp.where(chip == 0, 0, jnp.where(chip == GROUP - 1, 1, chip + 1))


def causal(shape):
    return lax.broadcasted_iota(jnp.int32, shape, 0) >= lax.broadcasted_iota(jnp.int32, shape, 1)


def pack_kernel(c_ref, group_ref, x_hbm, g_hbm, codes_hbm, out_ref, x_ref, g_ref, codes_ref, sems):
    d = x_ref.shape[1]
    other = pl.multiple_of((1 - c_ref[0]) * HALF, HALF)
    step = LD // CUTS
    copies = [
        pltpu.make_async_copy(x_hbm.at[k * step:(k + 1) * step], x_ref.at[k * step:(k + 1) * step], sems.at[k])
        for k in range(CUTS)]
    copies.append(pltpu.make_async_copy(g_hbm.at[:, pl.ds(other, HALF)], g_ref, sems.at[CUTS]))
    copies.append(pltpu.make_async_copy(codes_hbm, codes_ref, sems.at[CUTS + 1]))
    for copy in copies:
        copy.start()
    out_ref[HEADS:, d + HALF:] = jnp.zeros((LD - HEADS, LD), f32)
    for k in range(CUTS):
        copies[k].wait()
        out_ref[k * step:(k + 1) * step, :d] = x_ref[k * step:(k + 1) * step, :].astype(f32)
    copies[CUTS].wait()
    out_ref[:, d:d + HALF] = g_ref[...].astype(f32)
    copies[CUTS + 1].wait()
    out_ref[0:HEADS, d + HALF:] = codes_ref[...].astype(f32)


def own_kernel(c_ref, group_ref, x_ref, g_ref, codes_ref, wx_ref, wbc_ref,
               mix_ref, proj_ref, g_out_ref, codes_out_ref, x_out_ref, wx_out_ref, wbc_out_ref):
    x = x_ref[...]
    wx = wx_ref[...]
    wbc = wbc_ref[...]
    mix_ref[...] = mm(x, wx).astype(bf16)
    proj_ref[...] = mm(x, wbc).astype(bf16)
    g_out_ref[...] = g_ref[...]
    codes_out_ref[...] = codes_ref[...].astype(f32)
    x_out_ref[...] = x
    wx_out_ref[...] = wx
    wbc_out_ref[...] = wbc


def local_kernel(unit, c_ref, group_ref, mix_ref, pj_ref, g_ref, codes_ref, x_ref, wx_ref, wbc_ref, pack_ref,
                 pay_ref, ue_ref, v_ref, en_ref, te_ref, proj_ref, xc_ref, yl_ref, gm_ref, gp_ref,
                 gs_ref, cs_ref, ms_ref):
    c = c_ref[0]
    own = pl.multiple_of(c * LD, LD)
    oth = pl.multiple_of((1 - c) * LD, LD)
    d = x_ref.shape[1]
    xo = pack_ref[:, :d].astype(bf16)
    xc_ref[pl.ds(own, LD), :] = x_ref[...]
    xc_ref[pl.ds(oth, LD), :] = xo
    gs_ref[pl.ds(own, LD), :] = g_ref[...].astype(f32)
    gs_ref[pl.ds(oth, LD), :] = pack_ref[:, d:d + HALF]
    cs_ref[:, pl.ds(own, LD)] = codes_ref[...]
    cs_ref[:, pl.ds(oth, LD)] = pack_ref[0:HEADS, d + HALF:]
    ms_ref[pl.ds(own, LD), :] = mix_ref[...]
    ms_ref[pl.ds(oth, LD), :] = mm(xo, wx_ref[...]).astype(bf16)
    proj_ref[pl.ds(own, LD), :] = pj_ref[...]
    proj_ref[pl.ds(oth, LD), :] = mm(xo, wbc_ref[...]).astype(bf16)
    codes = cs_ref[...]
    hi = jnp.floor(codes * (1.0 / 32.0))
    lo = codes - 32.0 * hi
    row = lax.broadcasted_iota(jnp.int32, (HEADS, HALF), 0)
    col = lax.broadcasted_iota(jnp.int32, (HEADS, HALF), 1)
    spread = jnp.where(row == col // HEAD + c * (HEADS // 2), 1.0, 0.0).astype(bf16)
    hi = mm_tn(hi.astype(bf16), spread).astype(bf16)
    lo = mm_tn(lo.astype(bf16), spread).astype(bf16)
    mask = causal((CHIP, CHIP))
    tri = jnp.where(mask, 1.0, 0.0).astype(bf16)
    running = unit * (32.0 * mm(tri, hi) + mm(tri, lo))
    last = running[CHIP - 1:CHIP, :]
    en = jnp.exp(-running)
    ep = jnp.exp(running)
    te = ep * jnp.exp(-last)
    en_ref[...] = en
    te_ref[...] = te
    mixer = ms_ref[...].astype(f32)
    inject = proj_ref[:, :STATE]
    readout = proj_ref[:, STATE:]
    v = (en * gs_ref[...]).astype(bf16)
    ue = (te * mixer).astype(bf16)
    u = (ep * mixer).astype(bf16)
    ue_ref[...] = ue
    v_ref[...] = v
    state = mm_tn(ue, inject)
    adjoint = mm_tn(v, readout)
    for h in range(GROUP):
        at = head_at(group_ref, h)
        pay_ref[at, 0:HEAD, :] = state[h * HEAD:(h + 1) * HEAD, :]
        pay_ref[at, HEAD:2 * HEAD, :] = adjoint[h * HEAD:(h + 1) * HEAD, :]
        pay_ref[at, 2 * HEAD:, :] = jnp.broadcast_to(last[:, h * HEAD:h * HEAD + 1], (8, STATE))
    scores = jnp.where(mask, mm_nt(readout, inject), 0.0).astype(bf16)
    pairs = jnp.where(mask, mm_nt(v, u), 0.0).astype(bf16)
    yl_ref[...] = en * mm(scores, u)
    gm_ref[...] = ep * mm_tn(scores, v)
    gp_ref[:, :STATE] = mm_tn(pairs, readout)
    gp_ref[:, STATE:] = mm(pairs, inject)


def total_kernel(c_ref, group_ref, in_ref, out_ref):
    group = group_ref[0]
    logs = [in_ref[NEAR_AT[k], 2 * HEAD:, :] for k in range(GROUP)]
    decay = [jnp.exp(-a[0:1, :]) for a in logs]
    state = in_ref[NEAR_AT[0], 0:HEAD, :]
    for k in range(1, GROUP):
        state = decay[k] * state + in_ref[NEAR_AT[k], 0:HEAD, :]
    adjoint = in_ref[NEAR_AT[GROUP - 1], HEAD:2 * HEAD, :]
    for k in reversed(range(GROUP - 1)):
        adjoint = decay[k] * adjoint + in_ref[NEAR_AT[k], HEAD:2 * HEAD, :]
    total = logs[0] + logs[1] + logs[2] + logs[3]
    for k in range(GROUPS):
        out_ref[FAR_AT[k], 0:HEAD, :] = jnp.where(k > group, state, adjoint)
        out_ref[FAR_AT[k], HEAD:, :] = total


def prefix_kernel(c_ref, group_ref, in_ref, far_ref, out_ref):
    group = group_ref[0]
    far = [jnp.exp(-far_ref[FAR_AT[k], HEAD:HEAD + 1, :]) for k in range(GROUPS)]
    decay = [jnp.exp(-in_ref[NEAR_AT[k], 2 * HEAD:2 * HEAD + 1, :]) for k in range(GROUP)]
    carry = jnp.zeros((HEAD, STATE), f32)
    for k in range(GROUPS - 1):
        carry = jnp.where(k < group, far[k] * carry + far_ref[FAR_AT[k], 0:HEAD, :], carry)
    for k in range(GROUP):
        out_ref[NEAR_AT[k], 0:HEAD, :] = carry
        if k + 1 < GROUP:
            carry = decay[k] * carry + in_ref[NEAR_AT[k], 0:HEAD, :]
    carry = jnp.zeros((HEAD, STATE), f32)
    for k in reversed(range(1, GROUPS)):
        carry = jnp.where(k > group, far[k] * carry + far_ref[FAR_AT[k], 0:HEAD, :], carry)
    for k in reversed(range(GROUP)):
        out_ref[NEAR_AT[k], HEAD:, :] = carry
        if k:
            carry = decay[k] * carry + in_ref[NEAR_AT[k], HEAD:2 * HEAD, :]


def outer_kernel(scale, c_ref, group_ref, in_ref, u_ref, v_ref, en_ref, te_ref, proj_ref,
                 yl_ref, gml_ref, gp_ref, gm_ref, pk_ref, yk_ref, send_ref, y_ref):
    c = c_ref[0]
    pieces = [in_ref[head_at(group_ref, h)] for h in range(GROUP)]
    carry = jnp.concatenate([a[:HEAD] for a in pieces], axis=0).astype(bf16)
    adjoint = jnp.concatenate([a[HEAD:] for a in pieces], axis=0).astype(bf16)
    inject = proj_ref[:, :STATE]
    readout = proj_ref[:, STATE:]
    gi = scale * (gp_ref[:, :STATE] + mm(u_ref[...], adjoint))
    gr = scale * (gp_ref[:, STATE:] + mm(v_ref[...], carry))
    grad = scale * (gml_ref[...] + te_ref[...] * mm_nt(inject, adjoint))
    gm_ref[...] = grad.astype(bf16)
    pk_ref[:, :STATE] = gi
    pk_ref[:, STATE:] = gr
    send_ref[:, :HALF] = grad
    send_ref[:, HALF:HALF + STATE] = gi
    send_ref[:, HALF + STATE:2 * HALF] = gr
    y_ref[...] = yl_ref[...] + en_ref[...] * mm_nt(readout, carry)
    yk_ref[...] = y_ref[pl.ds(pl.multiple_of(c * LD, LD), LD), :]
    there = y_ref[pl.ds(pl.multiple_of((1 - c) * LD, LD), LD), :]
    send_ref[0:LD, 2 * HALF:] = there[:, :LD]
    send_ref[LD:, 2 * HALF:] = there[:, LD:]


def near_kernel(c_ref, group_ref, xa_ref, xb_ref, gm_ref, out_ref):
    xt = jnp.where(c_ref[0] == 0, xa_ref[...], xb_ref[...])
    out_ref[...] = mm(xt, gm_ref[...])


def weight_kernel(c_ref, group_ref, xa_ref, xb_ref, near_ref, pk_ref, recv_ref, out_ref):
    c = c_ref[0]
    xt = jnp.where(c == 0, xa_ref[...], xb_ref[...])
    out_ref[:, pl.ds(pl.multiple_of(c * HALF, HALF), HALF)] = near_ref[...]
    out_ref[:, pl.ds(pl.multiple_of((1 - c) * HALF, HALF), HALF)] = mm(xt, recv_ref[:, :HALF].astype(bf16))
    out_ref[:, 2 * HALF:] = mm(xt, (pk_ref[...] + recv_ref[:, HALF:2 * HALF]).astype(bf16))


def half_fold_kernel(c_ref, group_ref, in_ref, out_ref):
    total = jnp.sum(in_ref[...], axis=0)
    step = out_ref.shape[1]
    for k in range(SIDE):
        out_ref[k] = total[k * step:(k + 1) * step, :]


def fold_kernel(c_ref, group_ref, in_ref, out_ref):
    total = jnp.sum(in_ref[...], axis=0)
    step = out_ref.shape[1]
    for k in range(ZN):
        out_ref[k] = total[k * step:(k + 1) * step, :]


def spread_kernel(scale, c_ref, group_ref, in_ref, out_ref):
    total = scale * jnp.sum(in_ref[...], axis=0)
    for k in range(DP):
        out_ref[k] = total


def place_kernel(c_ref, group_ref, in_ref, yk_ref, recv_ref, x_ref, bc_ref, y_ref):
    for k in range(DP):
        piece = in_ref[k]
        x_ref[2 * k:2 * k + 2, :] = piece[:, :2 * HALF]
        bc_ref[2 * k:2 * k + 2, :] = piece[:, 2 * HALF:]
    c = c_ref[0]
    own = pl.multiple_of(c * HALF, LD)
    oth = pl.multiple_of((1 - c) * HALF, LD)
    y_ref[:, pl.ds(own, HALF)] = yk_ref[...].astype(bf16)
    y_ref[:, pl.ds(oth, LD)] = recv_ref[0:LD, :].astype(bf16)
    y_ref[:, pl.ds(pl.multiple_of(oth + LD, LD), LD)] = recv_ref[LD:, :].astype(bf16)


def whole(shape):
    return pl.BlockSpec(shape, lambda i, c, g: (0,) * len(shape))


def call(kernel, place, outs, ins, scratch=(), specs=None):
    return pl.pallas_call(
        kernel,
        out_shape=[jax.ShapeDtypeStruct(s, d) for s, d in outs],
        grid_spec=pltpu.PrefetchScalarGridSpec(
            num_scalar_prefetch=2, grid=(1,), in_specs=specs or [whole(a.shape) for a in ins],
            out_specs=[whole(s) for s, _ in outs], scratch_shapes=list(scratch)),
        compiler_params=pltpu.CompilerParams(vmem_limit_bytes=16 * 1024 * 1024),
    )(*place, *ins)


def lines(turn):
    def device(x, y, z, core):
        return ((x * SIDE + y) * ZN + z) * 2 + core

    groups = []
    for core in range(2):
        for z in range(ZN):
            for fixed in range(SIDE):
                along = range(SIDE)
                if core == turn:
                    groups.append([device(k, fixed, z, core) for k in along])
                else:
                    groups.append([device(fixed, k, z, core) for k in along])
    return groups


def body(records, x_weight, bc_weight, decay_codes, out_grad):
    x = records[0]
    g = out_grad[0]
    codes = decay_codes[0].T
    d = x.shape[1]
    frames = LD * 2 * ZN
    unit = 1.0 / (32.0 * frames)
    out_scale = float((STATE * frames) ** -0.5)
    grad_scale = float((DP * frames) ** -0.5)
    place = lax.optimization_barrier((
        lax.axis_index("c").astype(jnp.int32).reshape(1),
        lax.div(lax.axis_index("z"), GROUP).astype(jnp.int32).reshape(1)))
    swap = [(0, 1), (1, 0)]
    near = [[GROUP * a + b for b in NEAR] for a in range(GROUPS)]
    across = [[GROUP * a + (a + b) % GROUP for a in FAR] for b in range(GROUP)]

    here = pl.BlockSpec((LD, HALF), lambda i, c, g: (0, c[0]))
    x, g, codes, wx, wbc = (
        pltpu.with_memory_space_constraint(a, pltpu.MemorySpace.HBM)
        for a in (x, g, codes, x_weight, bc_weight))
    raw = pl.BlockSpec(memory_space=pl.ANY)
    (pack,) = call(
        pack_kernel, place, [((LD, d + HALF + LD), f32)], (x, g, codes),
        [pltpu.VMEM((LD, d), bf16), pltpu.VMEM((LD, HALF), bf16), pltpu.VMEM((HEADS, LD), jnp.int32),
         pltpu.SemaphoreType.DMA((CUTS + 2,))],
        [raw, raw, raw])
    pack = lax.ppermute(pack, "c", swap)
    half = (LD, HALF)
    owned = call(
        own_kernel, place,
        [(half, bf16), ((LD, 2 * STATE), bf16), (half, bf16), ((HEADS, LD), f32), ((LD, d), bf16),
         ((d, HALF), bf16), ((d, 2 * STATE), bf16)],
        (x, g, codes, wx, wbc), (),
        [whole(x.shape), here, whole(codes.shape), pl.BlockSpec((d, HALF), lambda i, c, g: (0, c[0])),
         whole(wbc.shape)])

    sq = (CHIP, HALF)
    pay, ue, v, en, te, proj, xc, yl, gml, gpl = call(
        lambda *refs: local_kernel(unit, *refs), place,
        [((GROUP, 2 * HEAD + 8, STATE), f32), (sq, bf16), (sq, bf16), (sq, f32), (sq, f32),
         ((CHIP, 2 * STATE), bf16), ((CHIP, d), bf16), (sq, f32), (sq, f32), ((CHIP, 2 * STATE), f32)],
        (*owned, pack), [pltpu.VMEM(sq, f32), pltpu.VMEM((HEADS, CHIP), f32), pltpu.VMEM(sq, bf16)])

    pay = lax.all_to_all(pay, "z", 0, 0, tiled=True, axis_index_groups=near)
    (far,) = call(total_kernel, place, [((GROUPS, HEAD + 8, STATE), f32)], (pay,))
    far = lax.all_to_all(far, "z", 0, 0, tiled=True, axis_index_groups=across)
    (pay,) = call(prefix_kernel, place, [((GROUP, 2 * HEAD, STATE), f32)], (pay, far))
    pay = lax.all_to_all(pay, "z", 0, 0, tiled=True, axis_index_groups=near)

    gm, pk, yk, send = call(
        lambda *refs: outer_kernel(out_scale, *refs), place,
        [(sq, bf16), ((CHIP, 2 * STATE), f32), ((LD, HALF), f32), ((CHIP, 2 * HALF + LD), f32)],
        (pay, ue, v, en, te, proj, yl, gml, gpl), [pltpu.VMEM(sq, f32)])
    recv = lax.ppermute(send, "c", swap)
    xt = xc.T.reshape(ZN, 2, SIDE, SIDE, 2, CHIP)
    xa = xt[:, 0].transpose(1, 2, 0, 3, 4).reshape(d // 2, CHIP)
    xb = xt[:, 1].transpose(2, 1, 0, 3, 4).reshape(d // 2, CHIP)
    width = 2 * HALF + 2 * STATE
    (near_part,) = call(near_kernel, place, [((d // 2, HALF), f32)], (xa, xb, gm))
    (grad,) = call(weight_kernel, place, [((d // 2, width), f32)], (xa, xb, near_part, pk, recv))

    rows = d // 2 // DP
    every = ("dp", "z", "c")
    first, second = lines(0), lines(1)
    part = lax.all_to_all(grad.reshape(SIDE, SIDE * rows, width), every, 0, 0, tiled=True, axis_index_groups=first)
    (part,) = call(half_fold_kernel, place, [((SIDE, rows, width), f32)], (part,))
    part = lax.all_to_all(part, every, 0, 0, tiled=True, axis_index_groups=second)
    (part,) = call(fold_kernel, place, [((ZN, rows // ZN, width), f32)], (part,))
    part = lax.all_to_all(part, "z", 0, 0, tiled=True)
    (part,) = call(lambda *refs: spread_kernel(grad_scale, *refs), place, [((DP, rows // ZN, width), f32)], (part,))
    part = lax.all_to_all(part, "dp", 0, 0, tiled=True)
    x_grad, bc_grad, y = call(
        place_kernel, place,
        [((2 * DP, 2 * HALF), f32), ((2 * DP, 2 * STATE), f32), ((LD, 2 * HALF), bf16)], (part, yk, recv), (),
        [whole(part.shape), whole(yk.shape), pl.BlockSpec((CHIP, LD), lambda i, c, g: (0, 2 * HALF // LD))])
    return y[None], x_grad, bc_grad


def solution(mesh):
    mesh = Mesh(mesh.devices.reshape(DP, ZN, 2), ("dp", "z", "c"))
    frames = P("dp", ("z", "c"), None)
    rows = P(("z", "c"), None)
    return jax.shard_map(
        body,
        mesh=mesh,
        in_specs=(frames, P(), P(), frames, frames),
        out_specs=(frames, rows, rows),
        check_vma=False,
    )
```

```python
import jax
import jax.numpy as jnp
from jax import lax
from jax.experimental import pallas as pl
from jax.experimental.pallas import tpu as pltpu
from jax.sharding import Mesh, PartitionSpec as P

f32 = jnp.float32
bf16 = jnp.bfloat16

LD = 128
CHIP = 2 * LD
HEADS = 8
HEAD = 64
STATE = 128
HALF = HEADS * HEAD // 2
ZN = 16
DP = 16
SIDE = 4
GROUP = 4
CUTS = 4
NEAR = (0, 1, 2, 3)
NEAR_AT = (0, 1, 2, 3)
FAR = (0, 2, 1, 3)
FAR_AT = (0, 2, 1, 3)
GROUPS = ZN // GROUP


def mm(a, b):
    return jnp.dot(a, b, preferred_element_type=f32)


def mm_tn(a, b):
    return lax.dot_general(a, b, (((0,), (0,)), ((), ())), preferred_element_type=f32)


def mm_nt(a, b):
    return lax.dot_general(a, b, (((1,), (1,)), ((), ())), preferred_element_type=f32)


def head_at(group_ref, h):
    return (group_ref[0] + h) & (GROUP - 1)


def causal(shape):
    return lax.broadcasted_iota(jnp.int32, shape, 0) >= lax.broadcasted_iota(jnp.int32, shape, 1)


def pack_kernel(c_ref, group_ref, x_hbm, g_hbm, codes_hbm, out_ref, x_ref, g_ref, codes_ref, sems):
    d = x_ref.shape[1]
    other = pl.multiple_of((1 - c_ref[0]) * HALF, HALF)
    step = LD // CUTS
    copies = [
        pltpu.make_async_copy(x_hbm.at[k * step:(k + 1) * step], x_ref.at[k * step:(k + 1) * step], sems.at[k])
        for k in range(CUTS)]
    copies.append(pltpu.make_async_copy(g_hbm.at[:, pl.ds(other, HALF)], g_ref, sems.at[CUTS]))
    copies.append(pltpu.make_async_copy(codes_hbm, codes_ref, sems.at[CUTS + 1]))
    for copy in copies:
        copy.start()
    out_ref[HEADS:, d + HALF:] = jnp.zeros((LD - HEADS, LD), f32)
    for k in range(CUTS):
        copies[k].wait()
        out_ref[k * step:(k + 1) * step, :d] = x_ref[k * step:(k + 1) * step, :].astype(f32)
    copies[CUTS].wait()
    out_ref[:, d:d + HALF] = g_ref[...].astype(f32)
    copies[CUTS + 1].wait()
    out_ref[0:HEADS, d + HALF:] = codes_ref[...].astype(f32)


def own_kernel(c_ref, group_ref, x_ref, g_ref, codes_ref, wx_ref, wbc_ref,
               mix_ref, proj_ref, g_out_ref, codes_out_ref, x_out_ref, wx_out_ref, wbc_out_ref):
    x = x_ref[...]
    wx = wx_ref[...]
    wbc = wbc_ref[...]
    mix_ref[...] = mm(x, wx).astype(bf16)
    proj_ref[...] = mm(x, wbc).astype(bf16)
    g_out_ref[...] = g_ref[...]
    codes_out_ref[...] = codes_ref[...].astype(f32)
    x_out_ref[...] = x
    wx_out_ref[...] = wx
    wbc_out_ref[...] = wbc


def local_kernel(unit, c_ref, group_ref, mix_ref, pj_ref, g_ref, codes_ref, x_ref, wx_ref, wbc_ref, pack_ref,
                 pay_ref, ue_ref, v_ref, en_ref, te_ref, proj_ref, xc_ref, yl_ref, gm_ref, gp_ref,
                 gs_ref, cs_ref, ms_ref):
    c = c_ref[0]
    own = pl.multiple_of(c * LD, LD)
    oth = pl.multiple_of((1 - c) * LD, LD)
    d = x_ref.shape[1]
    xo = pack_ref[:, :d].astype(bf16)
    xc_ref[pl.ds(own, LD), :] = x_ref[...]
    xc_ref[pl.ds(oth, LD), :] = xo
    gs_ref[pl.ds(own, LD), :] = g_ref[...].astype(f32)
    gs_ref[pl.ds(oth, LD), :] = pack_ref[:, d:d + HALF]
    cs_ref[:, pl.ds(own, LD)] = codes_ref[...]
    cs_ref[:, pl.ds(oth, LD)] = pack_ref[0:HEADS, d + HALF:]
    ms_ref[pl.ds(own, LD), :] = mix_ref[...]
    ms_ref[pl.ds(oth, LD), :] = mm(xo, wx_ref[...]).astype(bf16)
    proj_ref[pl.ds(own, LD), :] = pj_ref[...]
    proj_ref[pl.ds(oth, LD), :] = mm(xo, wbc_ref[...]).astype(bf16)
    codes = cs_ref[...]
    hi = jnp.floor(codes * (1.0 / 32.0))
    lo = codes - 32.0 * hi
    row = lax.broadcasted_iota(jnp.int32, (HEADS, HALF), 0)
    col = lax.broadcasted_iota(jnp.int32, (HEADS, HALF), 1)
    spread = jnp.where(row == col // HEAD + c * (HEADS // 2), 1.0, 0.0).astype(bf16)
    hi = mm_tn(hi.astype(bf16), spread).astype(bf16)
    lo = mm_tn(lo.astype(bf16), spread).astype(bf16)
    mask = causal((CHIP, CHIP))
    tri = jnp.where(mask, 1.0, 0.0).astype(bf16)
    running = unit * (32.0 * mm(tri, hi) + mm(tri, lo))
    last = running[CHIP - 1:CHIP, :]
    en = jnp.exp(-running)
    ep = jnp.exp(running)
    te = ep * jnp.exp(-last)
    en_ref[...] = en
    te_ref[...] = te
    mixer = ms_ref[...].astype(f32)
    inject = proj_ref[:, :STATE]
    readout = proj_ref[:, STATE:]
    v = (en * gs_ref[...]).astype(bf16)
    ue = (te * mixer).astype(bf16)
    u = (ep * mixer).astype(bf16)
    ue_ref[...] = ue
    v_ref[...] = v
    state = mm_tn(ue, inject)
    adjoint = mm_tn(v, readout)
    for h in range(GROUP):
        at = head_at(group_ref, h)
        pay_ref[at, 0:HEAD, :] = state[h * HEAD:(h + 1) * HEAD, :]
        pay_ref[at, HEAD:2 * HEAD, :] = adjoint[h * HEAD:(h + 1) * HEAD, :]
        pay_ref[at, 2 * HEAD:, :] = jnp.broadcast_to(last[:, h * HEAD:h * HEAD + 1], (8, STATE))
    scores = jnp.where(mask, mm_nt(readout, inject), 0.0).astype(bf16)
    pairs = jnp.where(mask, mm_nt(v, u), 0.0).astype(bf16)
    yl_ref[...] = en * mm(scores, u)
    gm_ref[...] = ep * mm_tn(scores, v)
    gp_ref[:, :STATE] = mm_tn(pairs, readout)
    gp_ref[:, STATE:] = mm(pairs, inject)


def total_kernel(c_ref, group_ref, in_ref, out_ref):
    group = group_ref[0]
    logs = [in_ref[NEAR_AT[k], 2 * HEAD:, :] for k in range(GROUP)]
    decay = [jnp.exp(-a[0:1, :]) for a in logs]
    state = in_ref[NEAR_AT[0], 0:HEAD, :]
    for k in range(1, GROUP):
        state = decay[k] * state + in_ref[NEAR_AT[k], 0:HEAD, :]
    adjoint = in_ref[NEAR_AT[GROUP - 1], HEAD:2 * HEAD, :]
    for k in reversed(range(GROUP - 1)):
        adjoint = decay[k] * adjoint + in_ref[NEAR_AT[k], HEAD:2 * HEAD, :]
    total = logs[0] + logs[1] + logs[2] + logs[3]
    for k in range(GROUPS):
        out_ref[FAR_AT[k], 0:HEAD, :] = jnp.where(k > group, state, adjoint)
        out_ref[FAR_AT[k], HEAD:, :] = total


def prefix_kernel(c_ref, group_ref, in_ref, far_ref, out_ref):
    group = group_ref[0]
    far = [jnp.exp(-far_ref[FAR_AT[k], HEAD:HEAD + 1, :]) for k in range(GROUPS)]
    decay = [jnp.exp(-in_ref[NEAR_AT[k], 2 * HEAD:2 * HEAD + 1, :]) for k in range(GROUP)]
    carry = jnp.zeros((HEAD, STATE), f32)
    for k in range(GROUPS - 1):
        carry = jnp.where(k < group, far[k] * carry + far_ref[FAR_AT[k], 0:HEAD, :], carry)
    for k in range(GROUP):
        out_ref[NEAR_AT[k], 0:HEAD, :] = carry
        if k + 1 < GROUP:
            carry = decay[k] * carry + in_ref[NEAR_AT[k], 0:HEAD, :]
    carry = jnp.zeros((HEAD, STATE), f32)
    for k in reversed(range(1, GROUPS)):
        carry = jnp.where(k > group, far[k] * carry + far_ref[FAR_AT[k], 0:HEAD, :], carry)
    for k in reversed(range(GROUP)):
        out_ref[NEAR_AT[k], HEAD:, :] = carry
        if k:
            carry = decay[k] * carry + in_ref[NEAR_AT[k], HEAD:2 * HEAD, :]


def outer_kernel(scale, c_ref, group_ref, in_ref, u_ref, v_ref, en_ref, te_ref, proj_ref,
                 yl_ref, gml_ref, gp_ref, gm_ref, pk_ref, yk_ref, send_ref, y_ref):
    c = c_ref[0]
    pieces = [in_ref[head_at(group_ref, h)] for h in range(GROUP)]
    carry = jnp.concatenate([a[:HEAD] for a in pieces], axis=0).astype(bf16)
    adjoint = jnp.concatenate([a[HEAD:] for a in pieces], axis=0).astype(bf16)
    inject = proj_ref[:, :STATE]
    readout = proj_ref[:, STATE:]
    gi = scale * (gp_ref[:, :STATE] + mm(u_ref[...], adjoint))
    gr = scale * (gp_ref[:, STATE:] + mm(v_ref[...], carry))
    grad = scale * (gml_ref[...] + te_ref[...] * mm_nt(inject, adjoint))
    gm_ref[...] = grad.astype(bf16)
    pk_ref[:, :STATE] = gi
    pk_ref[:, STATE:] = gr
    send_ref[:, :HALF] = grad
    send_ref[:, HALF:HALF + STATE] = gi
    send_ref[:, HALF + STATE:2 * HALF] = gr
    y_ref[...] = yl_ref[...] + en_ref[...] * mm_nt(readout, carry)
    yk_ref[...] = y_ref[pl.ds(pl.multiple_of(c * LD, LD), LD), :]
    there = y_ref[pl.ds(pl.multiple_of((1 - c) * LD, LD), LD), :]
    send_ref[0:LD, 2 * HALF:] = there[:, :LD]
    send_ref[LD:, 2 * HALF:] = there[:, LD:]


def near_kernel(c_ref, group_ref, xa_ref, xb_ref, gm_ref, out_ref):
    xt = jnp.where(c_ref[0] == 0, xa_ref[...], xb_ref[...])
    out_ref[...] = mm(xt, gm_ref[...])


def weight_kernel(c_ref, group_ref, xa_ref, xb_ref, near_ref, pk_ref, recv_ref, out_ref):
    c = c_ref[0]
    xt = jnp.where(c == 0, xa_ref[...], xb_ref[...])
    out_ref[:, pl.ds(pl.multiple_of(c * HALF, HALF), HALF)] = near_ref[...]
    out_ref[:, pl.ds(pl.multiple_of((1 - c) * HALF, HALF), HALF)] = mm(xt, recv_ref[:, :HALF].astype(bf16))
    out_ref[:, 2 * HALF:] = mm(xt, (pk_ref[...] + recv_ref[:, HALF:2 * HALF]).astype(bf16))


def half_fold_kernel(c_ref, group_ref, in_ref, out_ref):
    total = jnp.sum(in_ref[...], axis=0)
    step = out_ref.shape[1]
    for k in range(SIDE):
        out_ref[k] = total[k * step:(k + 1) * step, :]


def fold_kernel(c_ref, group_ref, in_ref, out_ref):
    total = jnp.sum(in_ref[...], axis=0)
    step = out_ref.shape[1]
    for k in range(ZN):
        out_ref[k] = total[k * step:(k + 1) * step, :]


def spread_kernel(scale, c_ref, group_ref, in_ref, out_ref):
    total = scale * jnp.sum(in_ref[...], axis=0)
    for k in range(DP):
        out_ref[k] = total


def place_kernel(c_ref, group_ref, in_ref, yk_ref, recv_ref, x_ref, bc_ref, y_ref):
    for k in range(DP):
        piece = in_ref[k]
        x_ref[2 * k:2 * k + 2, :] = piece[:, :2 * HALF]
        bc_ref[2 * k:2 * k + 2, :] = piece[:, 2 * HALF:]
    c = c_ref[0]
    own = pl.multiple_of(c * HALF, LD)
    oth = pl.multiple_of((1 - c) * HALF, LD)
    y_ref[:, pl.ds(own, HALF)] = yk_ref[...].astype(bf16)
    y_ref[:, pl.ds(oth, LD)] = recv_ref[0:LD, :].astype(bf16)
    y_ref[:, pl.ds(pl.multiple_of(oth + LD, LD), LD)] = recv_ref[LD:, :].astype(bf16)


def whole(shape):
    return pl.BlockSpec(shape, lambda i, c, g: (0,) * len(shape))


def call(kernel, place, outs, ins, scratch=(), specs=None):
    return pl.pallas_call(
        kernel,
        out_shape=[jax.ShapeDtypeStruct(s, d) for s, d in outs],
        grid_spec=pltpu.PrefetchScalarGridSpec(
            num_scalar_prefetch=2, grid=(1,), in_specs=specs or [whole(a.shape) for a in ins],
            out_specs=[whole(s) for s, _ in outs], scratch_shapes=list(scratch)),
        compiler_params=pltpu.CompilerParams(vmem_limit_bytes=16 * 1024 * 1024),
    )(*place, *ins)


def lines(turn):
    def device(x, y, z, core):
        return ((x * SIDE + y) * ZN + z) * 2 + core

    groups = []
    for core in range(2):
        for z in range(ZN):
            for fixed in range(SIDE):
                along = range(SIDE)
                if core == turn:
                    groups.append([device(k, fixed, z, core) for k in along])
                else:
                    groups.append([device(fixed, k, z, core) for k in along])
    return groups


def body(records, x_weight, bc_weight, decay_codes, out_grad):
    x = records[0]
    g = out_grad[0]
    codes = decay_codes[0].T
    d = x.shape[1]
    frames = LD * 2 * ZN
    unit = 1.0 / (32.0 * frames)
    out_scale = float((STATE * frames) ** -0.5)
    grad_scale = float((DP * frames) ** -0.5)
    place = lax.optimization_barrier((
        lax.axis_index("c").astype(jnp.int32).reshape(1),
        lax.div(lax.axis_index("z"), GROUP).astype(jnp.int32).reshape(1)))
    swap = [(0, 1), (1, 0)]
    near = [[GROUP * a + b for b in NEAR] for a in range(GROUPS)]
    across = [[GROUP * a + (a + b) % GROUP for a in FAR] for b in range(GROUP)]

    here = pl.BlockSpec((LD, HALF), lambda i, c, g: (0, c[0]))
    x, g, codes, wx, wbc = (
        pltpu.with_memory_space_constraint(a, pltpu.MemorySpace.HBM)
        for a in (x, g, codes, x_weight, bc_weight))
    raw = pl.BlockSpec(memory_space=pl.ANY)
    (pack,) = call(
        pack_kernel, place, [((LD, d + HALF + LD), f32)], (x, g, codes),
        [pltpu.VMEM((LD, d), bf16), pltpu.VMEM((LD, HALF), bf16), pltpu.VMEM((HEADS, LD), jnp.int32),
         pltpu.SemaphoreType.DMA((CUTS + 2,))],
        [raw, raw, raw])
    pack = lax.ppermute(pack, "c", swap)
    half = (LD, HALF)
    owned = call(
        own_kernel, place,
        [(half, bf16), ((LD, 2 * STATE), bf16), (half, bf16), ((HEADS, LD), f32), ((LD, d), bf16),
         ((d, HALF), bf16), ((d, 2 * STATE), bf16)],
        (x, g, codes, wx, wbc), (),
        [whole(x.shape), here, whole(codes.shape), pl.BlockSpec((d, HALF), lambda i, c, g: (0, c[0])),
         whole(wbc.shape)])

    sq = (CHIP, HALF)
    pay, ue, v, en, te, proj, xc, yl, gml, gpl = call(
        lambda *refs: local_kernel(unit, *refs), place,
        [((GROUP, 2 * HEAD + 8, STATE), f32), (sq, bf16), (sq, bf16), (sq, f32), (sq, f32),
         ((CHIP, 2 * STATE), bf16), ((CHIP, d), bf16), (sq, f32), (sq, f32), ((CHIP, 2 * STATE), f32)],
        (*owned, pack), [pltpu.VMEM(sq, f32), pltpu.VMEM((HEADS, CHIP), f32), pltpu.VMEM(sq, bf16)])

    pay = lax.all_to_all(pay, "z", 0, 0, tiled=True, axis_index_groups=near)
    (far,) = call(total_kernel, place, [((GROUPS, HEAD + 8, STATE), f32)], (pay,))
    far = lax.all_to_all(far, "z", 0, 0, tiled=True, axis_index_groups=across)
    (pay,) = call(prefix_kernel, place, [((GROUP, 2 * HEAD, STATE), f32)], (pay, far))
    pay = lax.all_to_all(pay, "z", 0, 0, tiled=True, axis_index_groups=near)

    gm, pk, yk, send = call(
        lambda *refs: outer_kernel(out_scale, *refs), place,
        [(sq, bf16), ((CHIP, 2 * STATE), f32), ((LD, HALF), f32), ((CHIP, 2 * HALF + LD), f32)],
        (pay, ue, v, en, te, proj, yl, gml, gpl), [pltpu.VMEM(sq, f32)])
    recv = lax.ppermute(send, "c", swap)
    xt = xc.T.reshape(ZN, 2, SIDE, SIDE, 2, CHIP)
    xa = xt[:, 0].transpose(1, 2, 0, 3, 4).reshape(d // 2, CHIP)
    xb = xt[:, 1].transpose(2, 1, 0, 3, 4).reshape(d // 2, CHIP)
    width = 2 * HALF + 2 * STATE
    (near_part,) = call(near_kernel, place, [((d // 2, HALF), f32)], (xa, xb, gm))
    (grad,) = call(weight_kernel, place, [((d // 2, width), f32)], (xa, xb, near_part, pk, recv))

    rows = d // 2 // DP
    every = ("dp", "z", "c")
    first, second = lines(0), lines(1)
    part = lax.all_to_all(grad.reshape(SIDE, SIDE * rows, width), every, 0, 0, tiled=True, axis_index_groups=first)
    (part,) = call(half_fold_kernel, place, [((SIDE, rows, width), f32)], (part,))
    part = lax.all_to_all(part, every, 0, 0, tiled=True, axis_index_groups=second)
    (part,) = call(fold_kernel, place, [((ZN, rows // ZN, width), f32)], (part,))
    part = lax.all_to_all(part, "z", 0, 0, tiled=True)
    (part,) = call(lambda *refs: spread_kernel(grad_scale, *refs), place, [((DP, rows // ZN, width), f32)], (part,))
    part = lax.all_to_all(part, "dp", 0, 0, tiled=True)
    x_grad, bc_grad, y = call(
        place_kernel, place,
        [((2 * DP, 2 * HALF), f32), ((2 * DP, 2 * STATE), f32), ((LD, 2 * HALF), bf16)], (part, yk, recv), (),
        [whole(part.shape), whole(yk.shape), pl.BlockSpec((CHIP, LD), lambda i, c, g: (0, 2 * HALF // LD))])
    return y[None], x_grad, bc_grad


def solution(mesh):
    mesh = Mesh(mesh.devices.reshape(DP, ZN, 2), ("dp", "z", "c"))
    frames = P("dp", ("z", "c"), None)
    rows = P(("z", "c"), None)
    return jax.shard_map(
        body,
        mesh=mesh,
        in_specs=(frames, P(), P(), frames, frames),
        out_specs=(frames, rows, rows),
        check_vma=False,
    )
```

```python
import jax
import jax.numpy as jnp
from jax import lax
from jax.experimental import pallas as pl
from jax.experimental.pallas import tpu as pltpu
from jax.sharding import Mesh, PartitionSpec as P

f32 = jnp.float32
bf16 = jnp.bfloat16

LD = 128
CHIP = 2 * LD
HEADS = 8
HEAD = 64
STATE = 128
HALF = HEADS * HEAD // 2
ZN = 16
DP = 16
SIDE = 4
GROUP = 4
CUTS = 4
NEAR = (0, 2, 1, 3)
NEAR_AT = (0, 2, 1, 3)
FAR = (0, 2, 1, 3)
FAR_AT = (0, 2, 1, 3)
GROUPS = ZN // GROUP


def mm(a, b):
    return jnp.dot(a, b, preferred_element_type=f32)


def mm_tn(a, b):
    return lax.dot_general(a, b, (((0,), (0,)), ((), ())), preferred_element_type=f32)


def mm_nt(a, b):
    return lax.dot_general(a, b, (((1,), (1,)), ((), ())), preferred_element_type=f32)


def head_at(group_ref, h):
    chip = (group_ref[0] + h) & (GROUP - 1)
    return jnp.where((chip == 1) | (chip == 2), GROUP - 1 - chip, chip)


def causal(shape):
    return lax.broadcasted_iota(jnp.int32, shape, 0) >= lax.broadcasted_iota(jnp.int32, shape, 1)


def pack_kernel(c_ref, group_ref, x_hbm, g_hbm, codes_hbm, out_ref, x_ref, g_ref, codes_ref, sems):
    d = x_ref.shape[1]
    other = pl.multiple_of((1 - c_ref[0]) * HALF, HALF)
    step = LD // CUTS
    copies = [
        pltpu.make_async_copy(x_hbm.at[k * step:(k + 1) * step], x_ref.at[k * step:(k + 1) * step], sems.at[k])
        for k in range(CUTS)]
    copies.append(pltpu.make_async_copy(g_hbm.at[:, pl.ds(other, HALF)], g_ref, sems.at[CUTS]))
    copies.append(pltpu.make_async_copy(codes_hbm, codes_ref, sems.at[CUTS + 1]))
    for copy in copies:
        copy.start()
    out_ref[HEADS:, d + HALF:] = jnp.zeros((LD - HEADS, LD), f32)
    for k in range(CUTS):
        copies[k].wait()
        out_ref[k * step:(k + 1) * step, :d] = x_ref[k * step:(k + 1) * step, :].astype(f32)
    copies[CUTS].wait()
    out_ref[:, d:d + HALF] = g_ref[...].astype(f32)
    copies[CUTS + 1].wait()
    out_ref[0:HEADS, d + HALF:] = codes_ref[...].astype(f32)


def own_kernel(c_ref, group_ref, x_ref, g_ref, codes_ref, wx_ref, wbc_ref,
               mix_ref, proj_ref, g_out_ref, codes_out_ref, x_out_ref, wx_out_ref, wbc_out_ref):
    x = x_ref[...]
    wx = wx_ref[...]
    wbc = wbc_ref[...]
    mix_ref[...] = mm(x, wx).astype(bf16)
    proj_ref[...] = mm(x, wbc).astype(bf16)
    g_out_ref[...] = g_ref[...]
    codes_out_ref[...] = codes_ref[...].astype(f32)
    x_out_ref[...] = x
    wx_out_ref[...] = wx
    wbc_out_ref[...] = wbc


def local_kernel(unit, c_ref, group_ref, mix_ref, pj_ref, g_ref, codes_ref, x_ref, wx_ref, wbc_ref, pack_ref,
                 pay_ref, ue_ref, v_ref, en_ref, te_ref, proj_ref, xc_ref, yl_ref, gm_ref, gp_ref,
                 gs_ref, cs_ref, ms_ref):
    c = c_ref[0]
    own = pl.multiple_of(c * LD, LD)
    oth = pl.multiple_of((1 - c) * LD, LD)
    d = x_ref.shape[1]
    xo = pack_ref[:, :d].astype(bf16)
    xc_ref[pl.ds(own, LD), :] = x_ref[...]
    xc_ref[pl.ds(oth, LD), :] = xo
    gs_ref[pl.ds(own, LD), :] = g_ref[...].astype(f32)
    gs_ref[pl.ds(oth, LD), :] = pack_ref[:, d:d + HALF]
    cs_ref[:, pl.ds(own, LD)] = codes_ref[...]
    cs_ref[:, pl.ds(oth, LD)] = pack_ref[0:HEADS, d + HALF:]
    ms_ref[pl.ds(own, LD), :] = mix_ref[...]
    ms_ref[pl.ds(oth, LD), :] = mm(xo, wx_ref[...]).astype(bf16)
    proj_ref[pl.ds(own, LD), :] = pj_ref[...]
    proj_ref[pl.ds(oth, LD), :] = mm(xo, wbc_ref[...]).astype(bf16)
    codes = cs_ref[...]
    hi = jnp.floor(codes * (1.0 / 32.0))
    lo = codes - 32.0 * hi
    row = lax.broadcasted_iota(jnp.int32, (HEADS, HALF), 0)
    col = lax.broadcasted_iota(jnp.int32, (HEADS, HALF), 1)
    spread = jnp.where(row == col // HEAD + c * (HEADS // 2), 1.0, 0.0).astype(bf16)
    hi = mm_tn(hi.astype(bf16), spread).astype(bf16)
    lo = mm_tn(lo.astype(bf16), spread).astype(bf16)
    mask = causal((CHIP, CHIP))
    tri = jnp.where(mask, 1.0, 0.0).astype(bf16)
    running = unit * (32.0 * mm(tri, hi) + mm(tri, lo))
    last = running[CHIP - 1:CHIP, :]
    en = jnp.exp(-running)
    ep = jnp.exp(running)
    te = ep * jnp.exp(-last)
    en_ref[...] = en
    te_ref[...] = te
    mixer = ms_ref[...].astype(f32)
    inject = proj_ref[:, :STATE]
    readout = proj_ref[:, STATE:]
    v = (en * gs_ref[...]).astype(bf16)
    ue = (te * mixer).astype(bf16)
    u = (ep * mixer).astype(bf16)
    ue_ref[...] = ue
    v_ref[...] = v
    state = mm_tn(ue, inject)
    adjoint = mm_tn(v, readout)
    for h in range(GROUP):
        at = head_at(group_ref, h)
        pay_ref[at, 0:HEAD, :] = state[h * HEAD:(h + 1) * HEAD, :]
        pay_ref[at, HEAD:2 * HEAD, :] = adjoint[h * HEAD:(h + 1) * HEAD, :]
        pay_ref[at, 2 * HEAD:, :] = jnp.broadcast_to(last[:, h * HEAD:h * HEAD + 1], (8, STATE))
    scores = jnp.where(mask, mm_nt(readout, inject), 0.0).astype(bf16)
    pairs = jnp.where(mask, mm_nt(v, u), 0.0).astype(bf16)
    yl_ref[...] = en * mm(scores, u)
    gm_ref[...] = ep * mm_tn(scores, v)
    gp_ref[:, :STATE] = mm_tn(pairs, readout)
    gp_ref[:, STATE:] = mm(pairs, inject)


def total_kernel(c_ref, group_ref, in_ref, out_ref):
    group = group_ref[0]
    logs = [in_ref[NEAR_AT[k], 2 * HEAD:, :] for k in range(GROUP)]
    decay = [jnp.exp(-a[0:1, :]) for a in logs]
    state = in_ref[NEAR_AT[0], 0:HEAD, :]
    for k in range(1, GROUP):
        state = decay[k] * state + in_ref[NEAR_AT[k], 0:HEAD, :]
    adjoint = in_ref[NEAR_AT[GROUP - 1], HEAD:2 * HEAD, :]
    for k in reversed(range(GROUP - 1)):
        adjoint = decay[k] * adjoint + in_ref[NEAR_AT[k], HEAD:2 * HEAD, :]
    total = logs[0] + logs[1] + logs[2] + logs[3]
    for k in range(GROUPS):
        out_ref[FAR_AT[k], 0:HEAD, :] = jnp.where(k > group, state, adjoint)
        out_ref[FAR_AT[k], HEAD:, :] = total


def prefix_kernel(c_ref, group_ref, in_ref, far_ref, out_ref):
    group = group_ref[0]
    far = [jnp.exp(-far_ref[FAR_AT[k], HEAD:HEAD + 1, :]) for k in range(GROUPS)]
    decay = [jnp.exp(-in_ref[NEAR_AT[k], 2 * HEAD:2 * HEAD + 1, :]) for k in range(GROUP)]
    carry = jnp.zeros((HEAD, STATE), f32)
    for k in range(GROUPS - 1):
        carry = jnp.where(k < group, far[k] * carry + far_ref[FAR_AT[k], 0:HEAD, :], carry)
    for k in range(GROUP):
        out_ref[NEAR_AT[k], 0:HEAD, :] = carry
        if k + 1 < GROUP:
            carry = decay[k] * carry + in_ref[NEAR_AT[k], 0:HEAD, :]
    carry = jnp.zeros((HEAD, STATE), f32)
    for k in reversed(range(1, GROUPS)):
        carry = jnp.where(k > group, far[k] * carry + far_ref[FAR_AT[k], 0:HEAD, :], carry)
    for k in reversed(range(GROUP)):
        out_ref[NEAR_AT[k], HEAD:, :] = carry
        if k:
            carry = decay[k] * carry + in_ref[NEAR_AT[k], HEAD:2 * HEAD, :]


def outer_kernel(scale, c_ref, group_ref, in_ref, u_ref, v_ref, en_ref, te_ref, proj_ref,
                 yl_ref, gml_ref, gp_ref, gm_ref, pk_ref, yk_ref, send_ref, y_ref):
    c = c_ref[0]
    pieces = [in_ref[head_at(group_ref, h)] for h in range(GROUP)]
    carry = jnp.concatenate([a[:HEAD] for a in pieces], axis=0).astype(bf16)
    adjoint = jnp.concatenate([a[HEAD:] for a in pieces], axis=0).astype(bf16)
    inject = proj_ref[:, :STATE]
    readout = proj_ref[:, STATE:]
    gi = scale * (gp_ref[:, :STATE] + mm(u_ref[...], adjoint))
    gr = scale * (gp_ref[:, STATE:] + mm(v_ref[...], carry))
    grad = scale * (gml_ref[...] + te_ref[...] * mm_nt(inject, adjoint))
    gm_ref[...] = grad.astype(bf16)
    pk_ref[:, :STATE] = gi
    pk_ref[:, STATE:] = gr
    send_ref[:, :HALF] = grad
    send_ref[:, HALF:HALF + STATE] = gi
    send_ref[:, HALF + STATE:2 * HALF] = gr
    y_ref[...] = yl_ref[...] + en_ref[...] * mm_nt(readout, carry)
    yk_ref[...] = y_ref[pl.ds(pl.multiple_of(c * LD, LD), LD), :]
    there = y_ref[pl.ds(pl.multiple_of((1 - c) * LD, LD), LD), :]
    send_ref[0:LD, 2 * HALF:] = there[:, :LD]
    send_ref[LD:, 2 * HALF:] = there[:, LD:]


def near_kernel(c_ref, group_ref, xa_ref, xb_ref, gm_ref, out_ref):
    xt = jnp.where(c_ref[0] == 0, xa_ref[...], xb_ref[...])
    out_ref[...] = mm(xt, gm_ref[...])


def weight_kernel(c_ref, group_ref, xa_ref, xb_ref, near_ref, pk_ref, recv_ref, out_ref):
    c = c_ref[0]
    xt = jnp.where(c == 0, xa_ref[...], xb_ref[...])
    out_ref[:, pl.ds(pl.multiple_of(c * HALF, HALF), HALF)] = near_ref[...]
    out_ref[:, pl.ds(pl.multiple_of((1 - c) * HALF, HALF), HALF)] = mm(xt, recv_ref[:, :HALF].astype(bf16))
    out_ref[:, 2 * HALF:] = mm(xt, (pk_ref[...] + recv_ref[:, HALF:2 * HALF]).astype(bf16))


def half_fold_kernel(c_ref, group_ref, in_ref, out_ref):
    total = jnp.sum(in_ref[...], axis=0)
    step = out_ref.shape[1]
    for k in range(SIDE):
        out_ref[k] = total[k * step:(k + 1) * step, :]


def fold_kernel(c_ref, group_ref, in_ref, out_ref):
    total = jnp.sum(in_ref[...], axis=0)
    step = out_ref.shape[1]
    for k in range(ZN):
        out_ref[k] = total[k * step:(k + 1) * step, :]


def spread_kernel(scale, c_ref, group_ref, in_ref, out_ref):
    total = scale * jnp.sum(in_ref[...], axis=0)
    for k in range(DP):
        out_ref[k] = total


def place_kernel(c_ref, group_ref, in_ref, yk_ref, recv_ref, x_ref, bc_ref, y_ref):
    for k in range(DP):
        piece = in_ref[k]
        x_ref[2 * k:2 * k + 2, :] = piece[:, :2 * HALF]
        bc_ref[2 * k:2 * k + 2, :] = piece[:, 2 * HALF:]
    c = c_ref[0]
    own = pl.multiple_of(c * HALF, LD)
    oth = pl.multiple_of((1 - c) * HALF, LD)
    y_ref[:, pl.ds(own, HALF)] = yk_ref[...].astype(bf16)
    y_ref[:, pl.ds(oth, LD)] = recv_ref[0:LD, :].astype(bf16)
    y_ref[:, pl.ds(pl.multiple_of(oth + LD, LD), LD)] = recv_ref[LD:, :].astype(bf16)


def whole(shape):
    return pl.BlockSpec(shape, lambda i, c, g: (0,) * len(shape))


def call(kernel, place, outs, ins, scratch=(), specs=None):
    return pl.pallas_call(
        kernel,
        out_shape=[jax.ShapeDtypeStruct(s, d) for s, d in outs],
        grid_spec=pltpu.PrefetchScalarGridSpec(
            num_scalar_prefetch=2, grid=(1,), in_specs=specs or [whole(a.shape) for a in ins],
            out_specs=[whole(s) for s, _ in outs], scratch_shapes=list(scratch)),
        compiler_params=pltpu.CompilerParams(vmem_limit_bytes=16 * 1024 * 1024),
    )(*place, *ins)


def lines(turn):
    def device(x, y, z, core):
        return ((x * SIDE + y) * ZN + z) * 2 + core

    groups = []
    for core in range(2):
        for z in range(ZN):
            for fixed in range(SIDE):
                along = range(SIDE)
                if core == turn:
                    groups.append([device(k, fixed, z, core) for k in along])
                else:
                    groups.append([device(fixed, k, z, core) for k in along])
    return groups


def body(records, x_weight, bc_weight, decay_codes, out_grad):
    x = records[0]
    g = out_grad[0]
    codes = decay_codes[0].T
    d = x.shape[1]
    frames = LD * 2 * ZN
    unit = 1.0 / (32.0 * frames)
    out_scale = float((STATE * frames) ** -0.5)
    grad_scale = float((DP * frames) ** -0.5)
    place = lax.optimization_barrier((
        lax.axis_index("c").astype(jnp.int32).reshape(1),
        lax.div(lax.axis_index("z"), GROUP).astype(jnp.int32).reshape(1)))
    swap = [(0, 1), (1, 0)]
    near = [[GROUP * a + b for b in NEAR] for a in range(GROUPS)]
    across = [[GROUP * a + (a + b) % GROUP for a in FAR] for b in range(GROUP)]

    here = pl.BlockSpec((LD, HALF), lambda i, c, g: (0, c[0]))
    x, g, codes, wx, wbc = (
        pltpu.with_memory_space_constraint(a, pltpu.MemorySpace.HBM)
        for a in (x, g, codes, x_weight, bc_weight))
    raw = pl.BlockSpec(memory_space=pl.ANY)
    (pack,) = call(
        pack_kernel, place, [((LD, d + HALF + LD), f32)], (x, g, codes),
        [pltpu.VMEM((LD, d), bf16), pltpu.VMEM((LD, HALF), bf16), pltpu.VMEM((HEADS, LD), jnp.int32),
         pltpu.SemaphoreType.DMA((CUTS + 2,))],
        [raw, raw, raw])
    pack = lax.ppermute(pack, "c", swap)
    half = (LD, HALF)
    owned = call(
        own_kernel, place,
        [(half, bf16), ((LD, 2 * STATE), bf16), (half, bf16), ((HEADS, LD), f32), ((LD, d), bf16),
         ((d, HALF), bf16), ((d, 2 * STATE), bf16)],
        (x, g, codes, wx, wbc), (),
        [whole(x.shape), here, whole(codes.shape), pl.BlockSpec((d, HALF), lambda i, c, g: (0, c[0])),
         whole(wbc.shape)])

    sq = (CHIP, HALF)
    pay, ue, v, en, te, proj, xc, yl, gml, gpl = call(
        lambda *refs: local_kernel(unit, *refs), place,
        [((GROUP, 2 * HEAD + 8, STATE), f32), (sq, bf16), (sq, bf16), (sq, f32), (sq, f32),
         ((CHIP, 2 * STATE), bf16), ((CHIP, d), bf16), (sq, f32), (sq, f32), ((CHIP, 2 * STATE), f32)],
        (*owned, pack), [pltpu.VMEM(sq, f32), pltpu.VMEM((HEADS, CHIP), f32), pltpu.VMEM(sq, bf16)])

    pay = lax.all_to_all(pay, "z", 0, 0, tiled=True, axis_index_groups=near)
    (far,) = call(total_kernel, place, [((GROUPS, HEAD + 8, STATE), f32)], (pay,))
    far = lax.all_to_all(far, "z", 0, 0, tiled=True, axis_index_groups=across)
    (pay,) = call(prefix_kernel, place, [((GROUP, 2 * HEAD, STATE), f32)], (pay, far))
    pay = lax.all_to_all(pay, "z", 0, 0, tiled=True, axis_index_groups=near)

    gm, pk, yk, send = call(
        lambda *refs: outer_kernel(out_scale, *refs), place,
        [(sq, bf16), ((CHIP, 2 * STATE), f32), ((LD, HALF), f32), ((CHIP, 2 * HALF + LD), f32)],
        (pay, ue, v, en, te, proj, yl, gml, gpl), [pltpu.VMEM(sq, f32)])
    recv = lax.ppermute(send, "c", swap)
    xt = xc.T.reshape(ZN, 2, SIDE, SIDE, 2, CHIP)
    xa = xt[:, 0].transpose(1, 2, 0, 3, 4).reshape(d // 2, CHIP)
    xb = xt[:, 1].transpose(2, 1, 0, 3, 4).reshape(d // 2, CHIP)
    width = 2 * HALF + 2 * STATE
    (near_part,) = call(near_kernel, place, [((d // 2, HALF), f32)], (xa, xb, gm))
    (grad,) = call(weight_kernel, place, [((d // 2, width), f32)], (xa, xb, near_part, pk, recv))

    rows = d // 2 // DP
    every = ("dp", "z", "c")
    first, second = lines(0), lines(1)
    part = lax.all_to_all(grad.reshape(SIDE, SIDE * rows, width), every, 0, 0, tiled=True, axis_index_groups=first)
    (part,) = call(half_fold_kernel, place, [((SIDE, rows, width), f32)], (part,))
    part = lax.all_to_all(part, every, 0, 0, tiled=True, axis_index_groups=second)
    (part,) = call(fold_kernel, place, [((ZN, rows // ZN, width), f32)], (part,))
    part = lax.all_to_all(part, "z", 0, 0, tiled=True)
    (part,) = call(lambda *refs: spread_kernel(grad_scale, *refs), place, [((DP, rows // ZN, width), f32)], (part,))
    part = lax.all_to_all(part, "dp", 0, 0, tiled=True)
    x_grad, bc_grad, y = call(
        place_kernel, place,
        [((2 * DP, 2 * HALF), f32), ((2 * DP, 2 * STATE), f32), ((LD, 2 * HALF), bf16)], (part, yk, recv), (),
        [whole(part.shape), whole(yk.shape), pl.BlockSpec((CHIP, LD), lambda i, c, g: (0, 2 * HALF // LD))])
    return y[None], x_grad, bc_grad


def solution(mesh):
    mesh = Mesh(mesh.devices.reshape(DP, ZN, 2), ("dp", "z", "c"))
    frames = P("dp", ("z", "c"), None)
    rows = P(("z", "c"), None)
    return jax.shard_map(
        body,
        mesh=mesh,
        in_specs=(frames, P(), P(), frames, frames),
        out_specs=(frames, rows, rows),
        check_vma=False,
    )
```

```python
import jax
import jax.numpy as jnp
from jax import lax
from jax.experimental import pallas as pl
from jax.experimental.pallas import tpu as pltpu
from jax.sharding import Mesh, PartitionSpec as P

f32 = jnp.float32
bf16 = jnp.bfloat16

LD = 128
CHIP = 2 * LD
HEADS = 8
HEAD = 64
STATE = 128
HALF = HEADS * HEAD // 2
ZN = 16
DP = 16
SIDE = 4
GROUP = 4
CUTS = 4
NEAR = (0, 2, 1, 3)
NEAR_AT = (0, 2, 1, 3)
FAR = (0, 1, 2, 3)
FAR_AT = (0, 1, 2, 3)
GROUPS = ZN // GROUP


def mm(a, b):
    return jnp.dot(a, b, preferred_element_type=f32)


def mm_tn(a, b):
    return lax.dot_general(a, b, (((0,), (0,)), ((), ())), preferred_element_type=f32)


def mm_nt(a, b):
    return lax.dot_general(a, b, (((1,), (1,)), ((), ())), preferred_element_type=f32)


def head_at(group_ref, h):
    chip = (group_ref[0] + h) & (GROUP - 1)
    return jnp.where((chip == 1) | (chip == 2), GROUP - 1 - chip, chip)


def causal(shape):
    return lax.broadcasted_iota(jnp.int32, shape, 0) >= lax.broadcasted_iota(jnp.int32, shape, 1)


def pack_kernel(c_ref, group_ref, x_hbm, g_hbm, codes_hbm, out_ref, x_ref, g_ref, codes_ref, sems):
    d = x_ref.shape[1]
    other = pl.multiple_of((1 - c_ref[0]) * HALF, HALF)
    step = LD // CUTS
    copies = [
        pltpu.make_async_copy(x_hbm.at[k * step:(k + 1) * step], x_ref.at[k * step:(k + 1) * step], sems.at[k])
        for k in range(CUTS)]
    copies.append(pltpu.make_async_copy(g_hbm.at[:, pl.ds(other, HALF)], g_ref, sems.at[CUTS]))
    copies.append(pltpu.make_async_copy(codes_hbm, codes_ref, sems.at[CUTS + 1]))
    for copy in copies:
        copy.start()
    out_ref[HEADS:, d + HALF:] = jnp.zeros((LD - HEADS, LD), f32)
    for k in range(CUTS):
        copies[k].wait()
        out_ref[k * step:(k + 1) * step, :d] = x_ref[k * step:(k + 1) * step, :].astype(f32)
    copies[CUTS].wait()
    out_ref[:, d:d + HALF] = g_ref[...].astype(f32)
    copies[CUTS + 1].wait()
    out_ref[0:HEADS, d + HALF:] = codes_ref[...].astype(f32)


def own_kernel(c_ref, group_ref, x_ref, g_ref, codes_ref, wx_ref, wbc_ref,
               mix_ref, proj_ref, g_out_ref, codes_out_ref, x_out_ref, wx_out_ref, wbc_out_ref):
    x = x_ref[...]
    wx = wx_ref[...]
    wbc = wbc_ref[...]
    mix_ref[...] = mm(x, wx).astype(bf16)
    proj_ref[...] = mm(x, wbc).astype(bf16)
    g_out_ref[...] = g_ref[...]
    codes_out_ref[...] = codes_ref[...].astype(f32)
    x_out_ref[...] = x
    wx_out_ref[...] = wx
    wbc_out_ref[...] = wbc


def local_kernel(unit, c_ref, group_ref, mix_ref, pj_ref, g_ref, codes_ref, x_ref, wx_ref, wbc_ref, pack_ref,
                 pay_ref, ue_ref, v_ref, en_ref, te_ref, proj_ref, xc_ref, yl_ref, gm_ref, gp_ref,
                 gs_ref, cs_ref, ms_ref):
    c = c_ref[0]
    own = pl.multiple_of(c * LD, LD)
    oth = pl.multiple_of((1 - c) * LD, LD)
    d = x_ref.shape[1]
    xo = pack_ref[:, :d].astype(bf16)
    xc_ref[pl.ds(own, LD), :] = x_ref[...]
    xc_ref[pl.ds(oth, LD), :] = xo
    gs_ref[pl.ds(own, LD), :] = g_ref[...].astype(f32)
    gs_ref[pl.ds(oth, LD), :] = pack_ref[:, d:d + HALF]
    cs_ref[:, pl.ds(own, LD)] = codes_ref[...]
    cs_ref[:, pl.ds(oth, LD)] = pack_ref[0:HEADS, d + HALF:]
    ms_ref[pl.ds(own, LD), :] = mix_ref[...]
    ms_ref[pl.ds(oth, LD), :] = mm(xo, wx_ref[...]).astype(bf16)
    proj_ref[pl.ds(own, LD), :] = pj_ref[...]
    proj_ref[pl.ds(oth, LD), :] = mm(xo, wbc_ref[...]).astype(bf16)
    codes = cs_ref[...]
    hi = jnp.floor(codes * (1.0 / 32.0))
    lo = codes - 32.0 * hi
    row = lax.broadcasted_iota(jnp.int32, (HEADS, HALF), 0)
    col = lax.broadcasted_iota(jnp.int32, (HEADS, HALF), 1)
    spread = jnp.where(row == col // HEAD + c * (HEADS // 2), 1.0, 0.0).astype(bf16)
    hi = mm_tn(hi.astype(bf16), spread).astype(bf16)
    lo = mm_tn(lo.astype(bf16), spread).astype(bf16)
    mask = causal((CHIP, CHIP))
    tri = jnp.where(mask, 1.0, 0.0).astype(bf16)
    running = unit * (32.0 * mm(tri, hi) + mm(tri, lo))
    last = running[CHIP - 1:CHIP, :]
    en = jnp.exp(-running)
    ep = jnp.exp(running)
    te = ep * jnp.exp(-last)
    en_ref[...] = en
    te_ref[...] = te
    mixer = ms_ref[...].astype(f32)
    inject = proj_ref[:, :STATE]
    readout = proj_ref[:, STATE:]
    v = (en * gs_ref[...]).astype(bf16)
    ue = (te * mixer).astype(bf16)
    u = (ep * mixer).astype(bf16)
    ue_ref[...] = ue
    v_ref[...] = v
    state = mm_tn(ue, inject)
    adjoint = mm_tn(v, readout)
    for h in range(GROUP):
        at = head_at(group_ref, h)
        pay_ref[at, 0:HEAD, :] = state[h * HEAD:(h + 1) * HEAD, :]
        pay_ref[at, HEAD:2 * HEAD, :] = adjoint[h * HEAD:(h + 1) * HEAD, :]
        pay_ref[at, 2 * HEAD:, :] = jnp.broadcast_to(last[:, h * HEAD:h * HEAD + 1], (8, STATE))
    scores = jnp.where(mask, mm_nt(readout, inject), 0.0).astype(bf16)
    pairs = jnp.where(mask, mm_nt(v, u), 0.0).astype(bf16)
    yl_ref[...] = en * mm(scores, u)
    gm_ref[...] = ep * mm_tn(scores, v)
    gp_ref[:, :STATE] = mm_tn(pairs, readout)
    gp_ref[:, STATE:] = mm(pairs, inject)


def total_kernel(c_ref, group_ref, in_ref, out_ref):
    group = group_ref[0]
    logs = [in_ref[NEAR_AT[k], 2 * HEAD:, :] for k in range(GROUP)]
    decay = [jnp.exp(-a[0:1, :]) for a in logs]
    state = in_ref[NEAR_AT[0], 0:HEAD, :]
    for k in range(1, GROUP):
        state = decay[k] * state + in_ref[NEAR_AT[k], 0:HEAD, :]
    adjoint = in_ref[NEAR_AT[GROUP - 1], HEAD:2 * HEAD, :]
    for k in reversed(range(GROUP - 1)):
        adjoint = decay[k] * adjoint + in_ref[NEAR_AT[k], HEAD:2 * HEAD, :]
    total = logs[0] + logs[1] + logs[2] + logs[3]
    for k in range(GROUPS):
        out_ref[FAR_AT[k], 0:HEAD, :] = jnp.where(k > group, state, adjoint)
        out_ref[FAR_AT[k], HEAD:, :] = total


def prefix_kernel(c_ref, group_ref, in_ref, far_ref, out_ref):
    group = group_ref[0]
    far = [jnp.exp(-far_ref[FAR_AT[k], HEAD:HEAD + 1, :]) for k in range(GROUPS)]
    decay = [jnp.exp(-in_ref[NEAR_AT[k], 2 * HEAD:2 * HEAD + 1, :]) for k in range(GROUP)]
    carry = jnp.zeros((HEAD, STATE), f32)
    for k in range(GROUPS - 1):
        carry = jnp.where(k < group, far[k] * carry + far_ref[FAR_AT[k], 0:HEAD, :], carry)
    for k in range(GROUP):
        out_ref[NEAR_AT[k], 0:HEAD, :] = carry
        if k + 1 < GROUP:
            carry = decay[k] * carry + in_ref[NEAR_AT[k], 0:HEAD, :]
    carry = jnp.zeros((HEAD, STATE), f32)
    for k in reversed(range(1, GROUPS)):
        carry = jnp.where(k > group, far[k] * carry + far_ref[FAR_AT[k], 0:HEAD, :], carry)
    for k in reversed(range(GROUP)):
        out_ref[NEAR_AT[k], HEAD:, :] = carry
        if k:
            carry = decay[k] * carry + in_ref[NEAR_AT[k], HEAD:2 * HEAD, :]


def outer_kernel(scale, c_ref, group_ref, in_ref, u_ref, v_ref, en_ref, te_ref, proj_ref,
                 yl_ref, gml_ref, gp_ref, gm_ref, pk_ref, yk_ref, send_ref, y_ref):
    c = c_ref[0]
    pieces = [in_ref[head_at(group_ref, h)] for h in range(GROUP)]
    carry = jnp.concatenate([a[:HEAD] for a in pieces], axis=0).astype(bf16)
    adjoint = jnp.concatenate([a[HEAD:] for a in pieces], axis=0).astype(bf16)
    inject = proj_ref[:, :STATE]
    readout = proj_ref[:, STATE:]
    gi = scale * (gp_ref[:, :STATE] + mm(u_ref[...], adjoint))
    gr = scale * (gp_ref[:, STATE:] + mm(v_ref[...], carry))
    grad = scale * (gml_ref[...] + te_ref[...] * mm_nt(inject, adjoint))
    gm_ref[...] = grad.astype(bf16)
    pk_ref[:, :STATE] = gi
    pk_ref[:, STATE:] = gr
    send_ref[:, :HALF] = grad
    send_ref[:, HALF:HALF + STATE] = gi
    send_ref[:, HALF + STATE:2 * HALF] = gr
    y_ref[...] = yl_ref[...] + en_ref[...] * mm_nt(readout, carry)
    yk_ref[...] = y_ref[pl.ds(pl.multiple_of(c * LD, LD), LD), :]
    there = y_ref[pl.ds(pl.multiple_of((1 - c) * LD, LD), LD), :]
    send_ref[0:LD, 2 * HALF:] = there[:, :LD]
    send_ref[LD:, 2 * HALF:] = there[:, LD:]


def near_kernel(c_ref, group_ref, xa_ref, xb_ref, gm_ref, out_ref):
    xt = jnp.where(c_ref[0] == 0, xa_ref[...], xb_ref[...])
    out_ref[...] = mm(xt, gm_ref[...])


def weight_kernel(c_ref, group_ref, xa_ref, xb_ref, near_ref, pk_ref, recv_ref, out_ref):
    c = c_ref[0]
    xt = jnp.where(c == 0, xa_ref[...], xb_ref[...])
    out_ref[:, pl.ds(pl.multiple_of(c * HALF, HALF), HALF)] = near_ref[...]
    out_ref[:, pl.ds(pl.multiple_of((1 - c) * HALF, HALF), HALF)] = mm(xt, recv_ref[:, :HALF].astype(bf16))
    out_ref[:, 2 * HALF:] = mm(xt, (pk_ref[...] + recv_ref[:, HALF:2 * HALF]).astype(bf16))


def half_fold_kernel(c_ref, group_ref, in_ref, out_ref):
    total = jnp.sum(in_ref[...], axis=0)
    step = out_ref.shape[1]
    for k in range(SIDE):
        out_ref[k] = total[k * step:(k + 1) * step, :]


def fold_kernel(c_ref, group_ref, in_ref, out_ref):
    total = jnp.sum(in_ref[...], axis=0)
    step = out_ref.shape[1]
    for k in range(ZN):
        out_ref[k] = total[k * step:(k + 1) * step, :]


def spread_kernel(scale, c_ref, group_ref, in_ref, out_ref):
    total = scale * jnp.sum(in_ref[...], axis=0)
    for k in range(DP):
        out_ref[k] = total


def place_kernel(c_ref, group_ref, in_ref, yk_ref, recv_ref, x_ref, bc_ref, y_ref):
    for k in range(DP):
        piece = in_ref[k]
        x_ref[2 * k:2 * k + 2, :] = piece[:, :2 * HALF]
        bc_ref[2 * k:2 * k + 2, :] = piece[:, 2 * HALF:]
    c = c_ref[0]
    own = pl.multiple_of(c * HALF, LD)
    oth = pl.multiple_of((1 - c) * HALF, LD)
    y_ref[:, pl.ds(own, HALF)] = yk_ref[...].astype(bf16)
    y_ref[:, pl.ds(oth, LD)] = recv_ref[0:LD, :].astype(bf16)
    y_ref[:, pl.ds(pl.multiple_of(oth + LD, LD), LD)] = recv_ref[LD:, :].astype(bf16)


def whole(shape):
    return pl.BlockSpec(shape, lambda i, c, g: (0,) * len(shape))


def call(kernel, place, outs, ins, scratch=(), specs=None):
    return pl.pallas_call(
        kernel,
        out_shape=[jax.ShapeDtypeStruct(s, d) for s, d in outs],
        grid_spec=pltpu.PrefetchScalarGridSpec(
            num_scalar_prefetch=2, grid=(1,), in_specs=specs or [whole(a.shape) for a in ins],
            out_specs=[whole(s) for s, _ in outs], scratch_shapes=list(scratch)),
        compiler_params=pltpu.CompilerParams(vmem_limit_bytes=16 * 1024 * 1024),
    )(*place, *ins)


def lines(turn):
    def device(x, y, z, core):
        return ((x * SIDE + y) * ZN + z) * 2 + core

    groups = []
    for core in range(2):
        for z in range(ZN):
            for fixed in range(SIDE):
                along = range(SIDE)
                if core == turn:
                    groups.append([device(k, fixed, z, core) for k in along])
                else:
                    groups.append([device(fixed, k, z, core) for k in along])
    return groups


def body(records, x_weight, bc_weight, decay_codes, out_grad):
    x = records[0]
    g = out_grad[0]
    codes = decay_codes[0].T
    d = x.shape[1]
    frames = LD * 2 * ZN
    unit = 1.0 / (32.0 * frames)
    out_scale = float((STATE * frames) ** -0.5)
    grad_scale = float((DP * frames) ** -0.5)
    place = lax.optimization_barrier((
        lax.axis_index("c").astype(jnp.int32).reshape(1),
        lax.div(lax.axis_index("z"), GROUP).astype(jnp.int32).reshape(1)))
    swap = [(0, 1), (1, 0)]
    near = [[GROUP * a + b for b in NEAR] for a in range(GROUPS)]
    across = [[GROUP * a + (a + b) % GROUP for a in FAR] for b in range(GROUP)]

    here = pl.BlockSpec((LD, HALF), lambda i, c, g: (0, c[0]))
    x, g, codes, wx, wbc = (
        pltpu.with_memory_space_constraint(a, pltpu.MemorySpace.HBM)
        for a in (x, g, codes, x_weight, bc_weight))
    raw = pl.BlockSpec(memory_space=pl.ANY)
    (pack,) = call(
        pack_kernel, place, [((LD, d + HALF + LD), f32)], (x, g, codes),
        [pltpu.VMEM((LD, d), bf16), pltpu.VMEM((LD, HALF), bf16), pltpu.VMEM((HEADS, LD), jnp.int32),
         pltpu.SemaphoreType.DMA((CUTS + 2,))],
        [raw, raw, raw])
    pack = lax.ppermute(pack, "c", swap)
    half = (LD, HALF)
    owned = call(
        own_kernel, place,
        [(half, bf16), ((LD, 2 * STATE), bf16), (half, bf16), ((HEADS, LD), f32), ((LD, d), bf16),
         ((d, HALF), bf16), ((d, 2 * STATE), bf16)],
        (x, g, codes, wx, wbc), (),
        [whole(x.shape), here, whole(codes.shape), pl.BlockSpec((d, HALF), lambda i, c, g: (0, c[0])),
         whole(wbc.shape)])

    sq = (CHIP, HALF)
    pay, ue, v, en, te, proj, xc, yl, gml, gpl = call(
        lambda *refs: local_kernel(unit, *refs), place,
        [((GROUP, 2 * HEAD + 8, STATE), f32), (sq, bf16), (sq, bf16), (sq, f32), (sq, f32),
         ((CHIP, 2 * STATE), bf16), ((CHIP, d), bf16), (sq, f32), (sq, f32), ((CHIP, 2 * STATE), f32)],
        (*owned, pack), [pltpu.VMEM(sq, f32), pltpu.VMEM((HEADS, CHIP), f32), pltpu.VMEM(sq, bf16)])

    pay = lax.all_to_all(pay, "z", 0, 0, tiled=True, axis_index_groups=near)
    (far,) = call(total_kernel, place, [((GROUPS, HEAD + 8, STATE), f32)], (pay,))
    far = lax.all_to_all(far, "z", 0, 0, tiled=True, axis_index_groups=across)
    (pay,) = call(prefix_kernel, place, [((GROUP, 2 * HEAD, STATE), f32)], (pay, far))
    pay = lax.all_to_all(pay, "z", 0, 0, tiled=True, axis_index_groups=near)

    gm, pk, yk, send = call(
        lambda *refs: outer_kernel(out_scale, *refs), place,
        [(sq, bf16), ((CHIP, 2 * STATE), f32), ((LD, HALF), f32), ((CHIP, 2 * HALF + LD), f32)],
        (pay, ue, v, en, te, proj, yl, gml, gpl), [pltpu.VMEM(sq, f32)])
    recv = lax.ppermute(send, "c", swap)
    xt = xc.T.reshape(ZN, 2, SIDE, SIDE, 2, CHIP)
    xa = xt[:, 0].transpose(1, 2, 0, 3, 4).reshape(d // 2, CHIP)
    xb = xt[:, 1].transpose(2, 1, 0, 3, 4).reshape(d // 2, CHIP)
    width = 2 * HALF + 2 * STATE
    (near_part,) = call(near_kernel, place, [((d // 2, HALF), f32)], (xa, xb, gm))
    (grad,) = call(weight_kernel, place, [((d // 2, width), f32)], (xa, xb, near_part, pk, recv))

    rows = d // 2 // DP
    every = ("dp", "z", "c")
    first, second = lines(0), lines(1)
    part = lax.all_to_all(grad.reshape(SIDE, SIDE * rows, width), every, 0, 0, tiled=True, axis_index_groups=first)
    (part,) = call(half_fold_kernel, place, [((SIDE, rows, width), f32)], (part,))
    part = lax.all_to_all(part, every, 0, 0, tiled=True, axis_index_groups=second)
    (part,) = call(fold_kernel, place, [((ZN, rows // ZN, width), f32)], (part,))
    part = lax.all_to_all(part, "z", 0, 0, tiled=True)
    (part,) = call(lambda *refs: spread_kernel(grad_scale, *refs), place, [((DP, rows // ZN, width), f32)], (part,))
    part = lax.all_to_all(part, "dp", 0, 0, tiled=True)
    x_grad, bc_grad, y = call(
        place_kernel, place,
        [((2 * DP, 2 * HALF), f32), ((2 * DP, 2 * STATE), f32), ((LD, 2 * HALF), bf16)], (part, yk, recv), (),
        [whole(part.shape), whole(yk.shape), pl.BlockSpec((CHIP, LD), lambda i, c, g: (0, 2 * HALF // LD))])
    return y[None], x_grad, bc_grad


def solution(mesh):
    mesh = Mesh(mesh.devices.reshape(DP, ZN, 2), ("dp", "z", "c"))
    frames = P("dp", ("z", "c"), None)
    rows = P(("z", "c"), None)
    return jax.shard_map(
        body,
        mesh=mesh,
        in_specs=(frames, P(), P(), frames, frames),
        out_specs=(frames, rows, rows),
        check_vma=False,
    )
```
